128 devices in a mesh: seq: 16 (over z_lo, x, core), db: 8 (over y, z_hi).
Axes of the slice: x: 4, y: 4, z: 4 (z_hi: 2, z_lo: 2; z = z_hi * 2 + z_lo), core: 2. Of those that a mesh axis runs over, the one named last changes fastest.
Arguments:
- hidden_in: bfloat16 [4096, 4096], P('seq'), may hold values from -4 to 4
- query_rows: bfloat16 [4096, 4096], P('seq', 'db'), may hold values from -32 to 32
- key_rows: bfloat16 [4096, 4096], P('seq', 'db'), may hold values from -32 to 32
- value_rows: bfloat16 [4096, 4096], P('seq', 'db'), may hold values from -6 to 6
- w_self_out: bfloat16 [4096, 4096], P('db'), may hold values from -0.1796875 to 0.1796875
- norm_gain: bfloat16 [4096], replicated, may hold values from 0.099609375 to 1.8984375
- w_cross_q: bfloat16 [4096, 4096], P(None, 'db'), may hold values from -2 to 2
- w_cross_k: bfloat16 [1024, 4096], P(None, 'db'), may hold values from -1 to 1
- w_cross_v: bfloat16 [1024, 4096], P(None, 'db'), may hold values from -0.1875 to 0.1875
- w_cross_out: bfloat16 [4096, 4096], P('db'), may hold values from -0.09375 to 0.09375
- enc_table: bfloat16 [64, 128, 1024], P('db'), may hold values from -6 to 6
- nb_shard: int32 [64, 2], P('seq'), may hold values from 0 to 7, all different within a row; in each aligned block of 4 rows (0 to 3, 4 to 7, ...) at most 2 rows name the same one
- nb_row: int32 [64, 2], P('seq'), may hold values from 0 to 7
Outputs:
- block_out: float32 [4096, 4096], P(('seq', 'db'))
The draws below stay inside these ranges and needn't reach their ends.
Inputs may be any that keep to these rules, and one draw needn't show every extreme that they name: `nb_shard`: the spans held by one index of seq name each shard at most 2 times, and in the spans of some indices one shard exactly 2 times; the 2 neighbours of a span lie in different shards.
All inputs are finite; a program needn't handle non-finite values.
Results may differ from the reference program's by a relative error of at most 0.038.
Values may be sent and summed in bfloat16 or wider, within the bound.
A program may use at most 128 MiB of HBM per device.

```python
import math
import jax
import jax.numpy as jnp
import numpy as np
from jax import lax

D = 4096
H = 32
HD = 128
D_ENC = 1024
SPAN = 64
NEIGH = 2
NLEN = 128
ROWS_SHARD = 8
TOKENS = 4096
SPANS_DEV = 4
SPANS = 64
CAP = 2
DB_ROWS = 64
N_DB = 8


def drawn_pair(key):
    query_base = jnp.clip(jax.random.normal(jax.random.fold_in(key, 11), (TOKENS, H * HD), jnp.float32), -4.0, 4.0)
    key_base = jnp.clip(jax.random.normal(jax.random.fold_in(key, 12), (TOKENS, H * HD), jnp.float32), -4.0, 4.0)
    return (query_base, key_base)


def draw_query_rows(key, part):
    return drawn_pair(key)[0].astype(jnp.bfloat16)


def draw_key_rows(key, part):
    return drawn_pair(key)[1].astype(jnp.bfloat16)


def draw_hidden_in(key, part):
    base = 0.35 * jnp.clip(jax.random.normal(jax.random.fold_in(key, 24), (TOKENS, D), jnp.float32), -8.0, 8.0)
    return base.astype(jnp.bfloat16)


def draw_enc_table(key, part):
    base = jnp.clip(jax.random.normal(jax.random.fold_in(key, 26), (DB_ROWS, NLEN, D_ENC), jnp.float32), -6.0, 6.0)
    return base.astype(jnp.bfloat16)


def draw_w_cross_q(key, part):
    base = 2.0 * jnp.clip(jax.random.normal(jax.random.fold_in(key, 30), (D, H * HD), jnp.float32), -6.0, 6.0) / D ** 0.5
    return base.astype(jnp.bfloat16)


def draw_w_cross_k(key, part):
    base = jnp.clip(jax.random.normal(jax.random.fold_in(key, 29), (D_ENC, H * HD), jnp.float32), -6.0, 6.0) / D_ENC ** 0.5
    return base.astype(jnp.bfloat16)


def touch_ends(values, own_key, low, largest):
    longest = values.shape.index(max(values.shape))
    spots = []
    for shift in (0, 1):
        where = [jax.random.randint(jax.random.fold_in(own_key, axis), (), 0, length) for axis, length in enumerate(values.shape)]
        where[longest] = (where[longest] + shift) % values.shape[longest]
        spots.append(tuple(where))
    return values.at[spots[0]].set(low).at[spots[1]].set(largest)


def block_scale(stream_key, shape, split, low, high):
    factor_of, own = 1.0, jax.random.fold_in(stream_key, 6)
    for dim, blocks in split:
        draws = jnp.exp(jax.random.uniform(jax.random.fold_in(own, dim), (blocks,), jnp.float32, low / len(split), high / len(split)))
        factor_of = factor_of * jnp.repeat(draws, shape[dim] // blocks).reshape([-1 if axis == dim else 1 for axis in range(len(shape))])
    return factor_of


def routed_block(rng, own, number, rows, count, top, bound, skew):
    order = jax.random.permutation(rng, count)
    packed, ordinary = shares(count, rows * top, bound, skew, True), shares(count, rows * top, bound, skew, False)
    places = jnp.arange(count)

    def named(lengths, rotation):
        used = int((lengths > 0).sum())
        fixed = max(1, used // 4)
        shifted = fixed + (places - fixed + rotation * (used - fixed)) % max(1, count - fixed)
        return jnp.zeros((count,), jnp.int32).at[order[jnp.where(places < fixed, places, shifted)]].set(jnp.asarray(lengths, jnp.int32))

    lengths = jnp.where(number % 4 == 0, named(packed, number // 4), named(ordinary, number - number // 4 - 1))
    mixed = jax.random.permutation(jax.random.fold_in(own, 3), count)
    giver, sink = mixed[0:count // 2 * 2:2], mixed[1:count // 2 * 2:2]
    room = jnp.minimum(lengths[giver] - 1, bound - lengths[sink]) // 2
    room = jnp.where((giver == order[0]) | (sink == order[0]) | (lengths[sink] == 0), 0, jnp.maximum(room, 0))
    shifted = jax.random.randint(jax.random.fold_in(own, 4), (count // 2,), 0, 1 << 20) % (room + 1)
    lengths = lengths.at[giver].add(-shifted).at[sink].add(shifted)
    members = jnp.searchsorted(jnp.cumsum(lengths), jnp.arange(rows * top), side="right").astype(jnp.int32)
    table = members.reshape(top, rows).T
    table = table[jax.random.permutation(jax.random.fold_in(own, 1), rows)]
    rotation = jax.random.randint(jax.random.fold_in(own, 2), (rows, 1), 0, top)
    return jnp.take_along_axis(table, (jnp.arange(top)[None, :] + rotation) % top, axis=1)


def shares(number_of, total, limit, skew, full):
    loads = [(1 << 20) // math.isqrt(standing ** skew) + 1 for standing in range(1, number_of + 1)]
    largest = limit if full else min(limit, max(-(-total // number_of), total * loads[0] // sum(loads)))
    least = 1 if total - largest >= number_of - 1 else 0
    given, rest = [largest] + [least] * (number_of - 1), total - largest - least * (number_of - 1)
    while rest > 0:
        movable = [i for i in range(1, number_of) if given[i] < largest] or [i for i in range(1, number_of) if given[i] < limit]
        mass, left = sum([loads[i] for i in movable]), rest
        for i in movable:
            extra = min(limit - given[i], max(1, left * loads[i] // mass), rest)
            given[i] = given[i] + extra
            rest = rest - extra
    return np.array(given)


def scatter_about(stream_key, shape, scale, bound, pieces=(), held_as=jnp.bfloat16):
    result = scale * jax.random.normal(stream_key, shape, jnp.float32)
    if pieces:
        result = result * block_scale(stream_key, shape, pieces, -0.22, 0.18)
    return jnp.clip(result, -bound, bound).astype(held_as)


def setup_inputs(seed: int = 0) -> dict:
    seeds = jax.random.split(jax.random.key(seed), 14)
    hidden_in = draw_hidden_in(jax.random.fold_in(seeds[13], 71), 0)
    query_rows = draw_query_rows(jax.random.fold_in(seeds[13], 71), 0)
    key_rows = draw_key_rows(jax.random.fold_in(seeds[13], 71), 0)
    value_rows = scatter_about(seeds[3], (TOKENS, H * HD), 1.0, 6.0, ((0, 16), (1, 8)))
    w_self_out = scatter_about(seeds[4], (H * HD, D), 0.03, 0.1796875, ((0, 8),))
    norm_gain = jnp.clip(1.0 + 0.18 * jax.random.normal(seeds[5], (D,), jnp.float32), 0.099609375, 1.8984375).astype(jnp.bfloat16)
    w_cross_q = draw_w_cross_q(jax.random.fold_in(seeds[13], 71), 0)
    w_cross_k = draw_w_cross_k(jax.random.fold_in(seeds[13], 71), 0)
    w_cross_v = scatter_about(seeds[8], (D_ENC, H * HD), D_ENC ** -0.5, 0.1875, ((1, 8),))
    w_cross_out = scatter_about(seeds[9], (H * HD, D), (H * HD) ** -0.5, 0.09375, ((0, 8),))
    enc_table = draw_enc_table(jax.random.fold_in(seeds[13], 71), 0)
    nb_shard_keys = jax.random.split(jax.random.fold_in(seeds[11], 1), SPANS // SPANS_DEV)
    nb_shard_turns = jax.random.permutation(jax.random.fold_in(seeds[11], 3), SPANS // SPANS_DEV)
    nb_shard = jax.vmap(lambda own, number: routed_block(jax.random.fold_in(seeds[11], 2), own, number, SPANS_DEV, N_DB, NEIGH, CAP, 2))(nb_shard_keys, nb_shard_turns).reshape((SPANS, NEIGH))
    nb_row = touch_ends(jax.random.randint(seeds[12], (SPANS, NEIGH), 0, ROWS_SHARD), jax.random.fold_in(seeds[12], 1), 0, ROWS_SHARD - 1).astype(jnp.int32)
    return dict(hidden_in=hidden_in, query_rows=query_rows, key_rows=key_rows, value_rows=value_rows, w_self_out=w_self_out, norm_gain=norm_gain, w_cross_q=w_cross_q, w_cross_k=w_cross_k, w_cross_v=w_cross_v, w_cross_out=w_cross_out, enc_table=enc_table, nb_shard=nb_shard, nb_row=nb_row)


NEG_BIG = -1e+30

def reference(hidden_in, query_rows, key_rows, value_rows, w_self_out, norm_gain, w_cross_q, w_cross_k, w_cross_v, w_cross_out, enc_table, nb_shard, nb_row):
    score_scale = 1.0 / math.sqrt(HD)
    query_heads = query_rows.reshape(TOKENS, H, HD).transpose(1, 0, 2)
    key_heads = key_rows.reshape(TOKENS, H, HD).transpose(1, 0, 2)
    value_heads = value_rows.reshape(TOKENS, H, HD).transpose(1, 0, 2)
    positions = jnp.arange(TOKENS, dtype=jnp.int32)
    causal = positions[None, :] <= positions[:, None]

    def head_attend(operands):
        query_one, key_one, value_one = operands
        scores = jnp.dot(query_one, key_one.T, preferred_element_type=jnp.float32) * score_scale
        scores = jnp.where(causal, scores, NEG_BIG)
        top_score = lax.optimization_barrier(jnp.max(scores, axis=-1, keepdims=True))
        weights = jnp.exp(scores - top_score)
        totals = lax.optimization_barrier(jnp.sum(weights, axis=-1, keepdims=True))
        mixed = jnp.dot(weights.astype(jnp.bfloat16), value_one, preferred_element_type=jnp.float32) / totals
        return mixed.astype(jnp.bfloat16)
    head_outputs = lax.map(head_attend, (query_heads, key_heads, value_heads))
    attended = head_outputs.transpose(1, 0, 2).reshape(TOKENS, H * HD)
    attn_total = jnp.dot(attended, w_self_out, preferred_element_type=jnp.float32)
    residual = hidden_in.astype(jnp.float32) + attn_total
    mean_square = lax.optimization_barrier(jnp.mean(residual * residual, axis=-1, keepdims=True))
    normed = (residual * lax.rsqrt(mean_square + 1e-05) * norm_gain.astype(jnp.float32)).astype(jnp.bfloat16)
    cross_query = jnp.dot(normed, w_cross_q, preferred_element_type=jnp.float32).astype(jnp.bfloat16)
    table_rows = (nb_shard * ROWS_SHARD + nb_row).reshape(SPANS * NEIGH).astype(jnp.int32)
    encodings = jnp.take(enc_table, table_rows, axis=0).reshape(SPANS * NEIGH * NLEN, D_ENC)
    cross_keys = jnp.dot(encodings, w_cross_k, preferred_element_type=jnp.float32).astype(jnp.bfloat16)
    cross_values = jnp.dot(encodings, w_cross_v, preferred_element_type=jnp.float32).astype(jnp.bfloat16)
    zero_group = jnp.zeros((1, NEIGH * NLEN, H, HD), jnp.bfloat16)
    group_keys = jnp.concatenate((zero_group, cross_keys.reshape(SPANS, NEIGH * NLEN, H, HD)), axis=0)
    group_values = jnp.concatenate((zero_group, cross_values.reshape(SPANS, NEIGH * NLEN, H, HD)), axis=0)
    padded = jnp.pad(cross_query, ((1, SPAN - 1), (0, 0))).reshape(SPANS + 1, SPAN, H, HD)

    def group_attend(operands):
        query_group, key_group, value_group = operands
        scores = jnp.einsum('qhd,khd->hqk', query_group.astype(jnp.float32), key_group.astype(jnp.float32)) * score_scale
        top_score = lax.optimization_barrier(jnp.max(scores, axis=-1, keepdims=True))
        weights = jnp.exp(scores - top_score)
        totals = lax.optimization_barrier(jnp.sum(weights, axis=-1, keepdims=True))
        rounded = lax.optimization_barrier(weights.astype(jnp.bfloat16)).astype(jnp.float32)
        mixed = jnp.einsum('hqk,khd->hqd', rounded, value_group.astype(jnp.float32)) / totals
        return mixed.transpose(1, 0, 2).reshape(SPAN, H * HD).astype(jnp.bfloat16)
    grouped = lax.map(group_attend, (padded, group_keys, group_values))
    cross_mixed = grouped.reshape((SPANS + 1) * SPAN, H * HD)[1:TOKENS + 1]
    cross_total = jnp.dot(cross_mixed, w_cross_out, preferred_element_type=jnp.float32)
    return residual + cross_total
```

```python
import functools
import math

import jax
import jax.numpy as jnp
from jax import lax
from jax.experimental import pallas as pl
from jax.experimental.pallas import tpu as pltpu
from jax.sharding import PartitionSpec as P

HD = 128
SPAN = 64
NLEN = 128
TOK = 256
WIDTH = 512
D = 4096
SHARE = 32
NEG_BIG = -1e30
MESH = pl.DeviceIdType.MESH
EXP2_SCALE = math.log2(math.e) / math.sqrt(HD)
BF16 = jnp.bfloat16
F32 = jnp.float32


def remote(src, dst, send, recv, seq, db):
    return pltpu.make_async_remote_copy(
        src_ref=src, dst_ref=dst, send_sem=send, recv_sem=recv, device_id=(seq, db), device_id_type=MESH
    )


def dot_f32(a, b):
    return jnp.dot(a, b, preferred_element_type=F32)


def dot_nt(a, b):
    return lax.dot_general(a, b, (((1,), (1,)), ((), ())), preferred_element_type=F32)


def block_kernel(
    q_ref,
    k_ref,
    v_ref,
    gain_ref,
    shard_ref,
    row_ref,
    hidden_hbm,
    wso_hbm,
    wcq_hbm,
    wck_hbm,
    wcv_hbm,
    wco_hbm,
    enc_hbm,
    out_ref,
    wso,
    wcq,
    wck,
    wcv,
    wco,
    enc,
    hid,
    kvs,
    qst,
    kv,
    qb,
    ob,
    ret,
    sc_buf,
    lsum,
    acc,
    att,
    enc_out,
    arr,
    part,
    rs1,
    rs2,
    res,
    nf,
    cqa,
    qx,
    kx,
    vx,
    wsem,
    xs,
    xr,
    zs,
    zr,
    cs,
    cr,
    qs,
    qr,
    os_,
    or_,
    es,
    er,
    r1s,
    r1r,
    ags,
    agr,
    r2s,
    r2r,
    ps,
    pr,
):
    s = lax.axis_index("seq")
    d = lax.axis_index("db")
    c = s % 2
    x = (s // 2) % 4
    zl = s // 8

    def at(zz, xx, cc):
        return (zz * 4 + xx) * 2 + cc

    own_rows = pl.ds(pl.multiple_of(d * SHARE, SHARE), SHARE)

    bar = pltpu.get_barrier_semaphore()
    for step in range(1, 16):
        pl.semaphore_signal(bar, inc=1, device_id=((s + step) % 16, d), device_id_type=MESH)
    for step in range(1, 8):
        pl.semaphore_signal(bar, inc=1, device_id=(s, (d + step) % 8), device_id_type=MESH)

    loads = [
        pltpu.make_async_copy(enc_hbm, enc, wsem.at[0]),
        pltpu.make_async_copy(wso_hbm, wso, wsem.at[1]),
        pltpu.make_async_copy(hidden_hbm.at[own_rows], hid, wsem.at[2]),
        pltpu.make_async_copy(wck_hbm, wck, wsem.at[3]),
        pltpu.make_async_copy(wcv_hbm, wcv, wsem.at[4]),
        pltpu.make_async_copy(wcq_hbm, wcq, wsem.at[5]),
        pltpu.make_async_copy(wco_hbm, wco, wsem.at[6]),
    ]
    for load in loads:
        load.start()
    for h in range(4):
        cols = slice(h * HD, (h + 1) * HD)
        kvs[h, 0] = k_ref[:, cols]
        kvs[h, 1] = v_ref[:, cols]
        qst[h] = q_ref[:, cols]
    pl.semaphore_wait(bar, 22)

    sends = []

    def start(copy):
        copy.start()
        sends.append(copy)

    for dx in (1, 3, 2):
        other = (x + dx) % 4
        start(remote(kvs.at[other], kv.at[s], xs.at[dx], xr.at[dx], at(zl, other, c), d))
    kv[s] = kvs[x]
    low = s % 8
    high = low // 4
    j_to = (1 - high) * low + high * (7 - low)
    slot_to = (s // 8) * 2 + high
    for h in range(4):
        goal = at(j_to // 2, h, j_to % 2)

        @pl.when(goal != s)
        def _():
            remote(qst.at[h], qb.at[slot_to], qs.at[h], qr.at[slot_to], goal, d).start()

        @pl.when(goal == s)
        def _():
            pltpu.make_async_copy(qst.at[h], qb.at[slot_to], qr.at[slot_to]).start()

    loads[0].wait()
    first = jnp.int32(0)
    second = jnp.int32(0)
    found = jnp.int32(0)
    for e in range(8):
        match = shard_ref[e // 2, e % 2] == d
        row = row_ref[e // 2, e % 2]
        first = jnp.where(match & (found == 0), row, first)
        second = jnp.where(match & (found == 1), row, second)
        found = found + match.astype(jnp.int32)
    enc_out[0] = enc[first]
    enc_out[1] = enc[second]

    def forward(src, k):
        start(remote(kv.at[src], kv.at[src], zs.at[k], zr.at[k], at(1 - zl, x, c), d))
        start(remote(kv.at[src], kv.at[src], cs.at[k], cr.at[k], at(zl, x, 1 - c), d))

    forward(s, 0)
    for dx in (1, 3, 2):
        src = at(zl, (x - dx + 4) % 4, c)
        remote(kv.at[src], kv.at[src], xs.at[dx], xr.at[dx], src, d).wait_recv()
        forward(src, dx)
    for dd in (1, 7, 2, 6, 3, 5, 4):
        start(
            remote(enc_out, arr.at[pl.ds(2 * d, 2)], es.at[dd], er.at[dd], s, (d + dd) % 8)
        )
    arr[2 * d] = enc_out[0]
    arr[2 * d + 1] = enc_out[1]
    for dx in (0, 1, 3, 2):
        src = at(1 - zl, (x - dx + 4) % 4, c)
        remote(kv.at[src], kv.at[src], zs.at[dx], zr.at[dx], src, d).wait_recv()
        start(remote(kv.at[src], kv.at[src], cs.at[4 + dx], cr.at[4 + dx], at(zl, x, 1 - c), d))
    for zz in range(2):
        for dx in range(4):
            src = at((zl + zz) % 2, (x - dx + 4) % 4, 1 - c)
            k = 4 * zz + dx
            remote(kv.at[src], kv.at[src], cs.at[k], cr.at[k], src, d).wait_recv()

    j = zl * 2 + c

    def block_of(i):
        return (i // 2) * 8 + (i % 2) * (7 - j) + (1 - i % 2) * j

    def slot(i, carry):
        b = block_of(i)
        remote(qst.at[0], qb.at[i], qs.at[0], qr.at[i], s, d).wait_recv()
        query = qb[i]
        last = (b + 2) // 2 - 1

        def lanes_max(scores):
            return jnp.maximum(
                jnp.maximum(scores[:, 0:128], scores[:, 128:256]),
                jnp.maximum(scores[:, 256:384], scores[:, 384:512]),
            )

        def first_pass(kb, top):
            keys = kv[pl.ds(2 * kb, 2), 0].reshape(512, HD)
            scores = dot_nt(query, keys)
            sc_buf[kb] = scores
            return jnp.maximum(top, lanes_max(scores))

        top = lax.fori_loop(0, last, first_pass, jnp.full((TOK, 128), NEG_BIG, F32))
        keys = kv[pl.ds(2 * last, 2), 0].reshape(512, HD)
        scores = dot_nt(query, keys)
        key_pos = last * 512 + lax.broadcasted_iota(jnp.int32, (TOK, 512), 1)
        query_pos = b * TOK + lax.broadcasted_iota(jnp.int32, (TOK, 512), 0)
        scores = jnp.where(key_pos <= query_pos, scores, NEG_BIG)
        sc_buf[last] = scores
        top = jnp.max(jnp.maximum(top, lanes_max(scores)), axis=-1, keepdims=True)
        lsum[...] = jnp.zeros_like(lsum)
        acc[...] = jnp.zeros_like(acc)

        def second_pass(kb, carry):
            weights = jnp.exp2((sc_buf[kb] - top) * EXP2_SCALE)
            values = kv[pl.ds(2 * kb, 2), 1].reshape(512, HD)
            lsum[...] += (weights[:, 0:128] + weights[:, 128:256]) + (
                weights[:, 256:384] + weights[:, 384:512]
            )
            acc[...] += dot_f32(weights.astype(BF16), values)
            return carry

        lax.fori_loop(0, last + 1, second_pass, 0)
        total = jnp.sum(lsum[...], axis=-1, keepdims=True)
        ob[i] = (acc[...] / total).astype(BF16)

        @pl.when(b != s)
        def _():
            remote(ob.at[i], ret.at[x], os_.at[i], or_.at[x], b, d).start()

        @pl.when(b == s)
        def _():
            pltpu.make_async_copy(ob.at[i], ret.at[x], or_.at[x]).start()

        return carry

    lax.fori_loop(0, 4, slot, 0)
    for h in range(4):
        remote(ob.at[0], ret.at[h], os_.at[0], or_.at[h], s, d).wait_recv()
        att[:, h * HD : (h + 1) * HD] = ret[h]

    def project(lhs, weight):
        def tile(n, carry):
            cols = pl.ds(pl.multiple_of(n * 512, 512), 512)
            part[:, cols] = dot_f32(lhs, weight[:, cols]).astype(BF16)
            return carry

        lax.fori_loop(0, 8, tile, 0)

    loads[1].wait()
    project(att[...], wso)
    spread = []
    for dd in (4, 3, 5, 2, 6, 1, 7):
        other = (d + dd) % 8
        rows = pl.ds(pl.multiple_of(other * SHARE, SHARE), SHARE)
        copy = remote(part.at[rows], rs1.at[dd], r1s.at[dd], r1r.at[dd], s, other)
        copy.start()
        spread.append(copy)

    for dd in range(1, 8):
        src = (d - dd + 8) % 8
        remote(enc_out, arr.at[pl.ds(2 * src, 2)], es.at[dd], er.at[dd], s, src).wait_recv()
    loads[3].wait()
    loads[4].wait()
    for e in range(8):
        shard = shard_ref[e // 2, e % 2]
        rank = jnp.int32(0)
        for earlier in range(e):
            rank = rank + (shard_ref[earlier // 2, earlier % 2] == shard).astype(jnp.int32)
        entry = arr[shard * 2 + rank]
        rows = slice((e % 2) * NLEN, (e % 2 + 1) * NLEN)
        kx[e // 2 + 1, rows, :] = dot_f32(entry, wck[...]).astype(BF16)
        vx[e // 2 + 1, rows, :] = dot_f32(entry, wcv[...]).astype(BF16)

    @pl.when(s < 15)
    def _():
        remote(kx.at[4], kx.at[0], ps.at[0], pr.at[0], s + 1, d).start()
        remote(vx.at[4], vx.at[0], ps.at[1], pr.at[1], s + 1, d).start()

    @pl.when(s == 0)
    def _():
        kx[0] = jnp.zeros((2 * NLEN, WIDTH), BF16)
        vx[0] = jnp.zeros((2 * NLEN, WIDTH), BF16)

    loads[2].wait()
    for dd in range(1, 8):
        remote(part.at[own_rows], rs1.at[dd], r1s.at[dd], r1r.at[dd], s, d).wait_recv()

    def add_up(n, square):
        cols = pl.ds(pl.multiple_of(n * 512, 512), 512)
        total = part[own_rows, cols].astype(F32)
        for dd in range(1, 8):
            total = total + rs1[dd, :, cols].astype(F32)
        total = total + hid[:, cols].astype(F32)
        res[:, cols] = total
        return square + total * total

    square = lax.fori_loop(0, 8, add_up, jnp.zeros((SHARE, 512), F32))
    scale = lax.rsqrt(jnp.sum(square, axis=-1, keepdims=True) / D + 1e-05)

    def normalise(n, carry):
        cols = pl.ds(pl.multiple_of(n * 512, 512), 512)
        nf[own_rows, cols] = (res[:, cols] * scale * gain_ref[:, cols].astype(F32)).astype(BF16)
        return carry

    lax.fori_loop(0, 8, normalise, 0)
    for dd in (4, 3, 5, 2, 6, 1, 7):
        start(
            remote(nf.at[own_rows], nf.at[own_rows], ags.at[dd], agr.at[dd], s, (d + dd) % 8)
        )
    for copy in spread:
        copy.wait_send()
    loads[5].wait()
    for dd in range(1, 8):
        src = (d - dd + 8) % 8
        rows = pl.ds(pl.multiple_of(src * SHARE, SHARE), SHARE)
        remote(nf.at[rows], nf.at[rows], ags.at[dd], agr.at[dd], s, src).wait_recv()

    cqa[...] = jnp.zeros_like(cqa)

    def contract(n, carry):
        cols = pl.ds(pl.multiple_of(n * 512, 512), 512)
        cqa[...] += dot_f32(nf[:, cols], wcq[cols, :])
        return carry

    lax.fori_loop(0, 8, contract, 0)
    qx[...] = pltpu.roll(cqa[...].astype(BF16).astype(F32), 1, 0).astype(BF16)

    @pl.when(s > 0)
    def _():
        remote(kx.at[4], kx.at[0], ps.at[0], pr.at[0], s, d).wait_recv()
        remote(vx.at[4], vx.at[0], ps.at[1], pr.at[1], s, d).wait_recv()

    def attend(query, keys, values):
        scores = dot_nt(query, keys)
        top = jnp.max(scores, axis=-1, keepdims=True)
        weights = jnp.exp2((scores - top) * EXP2_SCALE)
        total = jnp.sum(weights, axis=-1, keepdims=True)
        return dot_f32(weights.astype(BF16), values) / total

    def group(g, carry):
        rows = pl.ds(pl.multiple_of(g * SPAN, SPAN), SPAN)
        for h in range(4):
            cols = slice(h * HD, (h + 1) * HD)
            cqa[rows, cols] = attend(qx[rows, cols], kx[g, :, cols], vx[g, :, cols])
        return carry

    lax.fori_loop(0, 4, group, 0)
    for h in range(4):
        cols = slice(h * HD, (h + 1) * HD)
        tail = attend(qx[0:16, cols], kx[4, :, cols], vx[4, :, cols])
        first_row = lax.broadcasted_iota(jnp.int32, (16, HD), 0) == 0
        cqa[0:16, cols] = jnp.where(first_row, tail, cqa[0:16, cols])
    att[...] = pltpu.roll(cqa[...], TOK - 1, 0).astype(BF16)

    loads[6].wait()
    project(att[...], wco)
    for dd in (4, 3, 5, 2, 6, 1, 7):
        other = (d + dd) % 8
        rows = pl.ds(pl.multiple_of(other * SHARE, SHARE), SHARE)
        start(remote(part.at[rows], rs2.at[dd], r2s.at[dd], r2r.at[dd], s, other))
    for dd in range(1, 8):
        remote(part.at[own_rows], rs2.at[dd], r2s.at[dd], r2r.at[dd], s, d).wait_recv()

    def finish(n, carry):
        cols = pl.ds(pl.multiple_of(n * 512, 512), 512)
        total = part[own_rows, cols].astype(F32)
        for dd in range(1, 8):
            total = total + rs2[dd, :, cols].astype(F32)
        out_ref[:, cols] = res[:, cols] + total
        return carry

    lax.fori_loop(0, 8, finish, 0)

    for copy in sends:
        copy.wait_send()
    for h in range(4):
        goal = at(j_to // 2, h, j_to % 2)

        @pl.when(goal != s)
        def _():
            remote(qst.at[h], qb.at[0], qs.at[h], qr.at[0], goal, d).wait_send()

    for i in range(4):

        @pl.when(block_of(i) != s)
        def _():
            remote(ob.at[i], ret.at[0], os_.at[i], or_.at[0], s, d).wait_send()

    @pl.when(s < 15)
    def _():
        remote(kx.at[4], kx.at[0], ps.at[0], pr.at[0], s, d).wait_send()
        remote(vx.at[4], vx.at[0], ps.at[1], pr.at[1], s, d).wait_send()


def per_device(
    hidden_in,
    query_rows,
    key_rows,
    value_rows,
    w_self_out,
    norm_gain,
    w_cross_q,
    w_cross_k,
    w_cross_v,
    w_cross_out,
    enc_table,
    nb_shard,
    nb_row,
):
    vmem = pl.BlockSpec(memory_space=pltpu.VMEM)
    smem = pl.BlockSpec(memory_space=pltpu.SMEM)
    hbm = pl.BlockSpec(memory_space=pl.ANY)
    scratch = [
        pltpu.VMEM((WIDTH, D), BF16),
        pltpu.VMEM((D, WIDTH), BF16),
        pltpu.VMEM((1024, WIDTH), BF16),
        pltpu.VMEM((1024, WIDTH), BF16),
        pltpu.VMEM((WIDTH, D), BF16),
        pltpu.VMEM((8, NLEN, 1024), BF16),
        pltpu.VMEM((SHARE, D), BF16),
        pltpu.VMEM((4, 2, TOK, HD), BF16),
        pltpu.VMEM((4, TOK, HD), BF16),
        pltpu.VMEM((16, 2, TOK, HD), BF16),
        pltpu.VMEM((4, TOK, HD), BF16),
        pltpu.VMEM((4, TOK, HD), BF16),
        pltpu.VMEM((4, TOK, HD), BF16),
        pltpu.VMEM((8, TOK, 512), F32),
        pltpu.VMEM((TOK, HD), F32),
        pltpu.VMEM((TOK, HD), F32),
        pltpu.VMEM((TOK, WIDTH), BF16),
        pltpu.VMEM((2, NLEN, 1024), BF16),
        pltpu.VMEM((16, NLEN, 1024), BF16),
        pltpu.VMEM((TOK, D), BF16),
        pltpu.VMEM((8, SHARE, D), BF16),
        pltpu.VMEM((8, SHARE, D), BF16),
        pltpu.VMEM((SHARE, D), F32),
        pltpu.VMEM((TOK, D), BF16),
        pltpu.VMEM((TOK, WIDTH), F32),
        pltpu.VMEM((TOK, WIDTH), BF16),
        pltpu.VMEM((5, 2 * NLEN, WIDTH), BF16),
        pltpu.VMEM((5, 2 * NLEN, WIDTH), BF16),
    ]
    counts = (7, 4, 4, 4, 4, 8, 8, 4, 4, 4, 4, 8, 8, 8, 8, 8, 8, 8, 8, 2, 2)
    scratch += [pltpu.SemaphoreType.DMA((count,)) for count in counts]
    return pl.pallas_call(
        block_kernel,
        out_shape=jax.ShapeDtypeStruct((SHARE, D), F32),
        in_specs=[vmem] * 4 + [smem] * 2 + [hbm] * 7,
        out_specs=vmem,
        scratch_shapes=scratch,
        compiler_params=pltpu.CompilerParams(
            collective_id=0, has_side_effects=True, vmem_limit_bytes=56 << 20
        ),
        name="retro_block",
    )(
        query_rows,
        key_rows,
        value_rows,
        norm_gain.reshape(1, D),
        nb_shard,
        nb_row,
        hidden_in,
        w_self_out,
        w_cross_q,
        w_cross_k,
        w_cross_v,
        w_cross_out,
        enc_table,
    )


def solution(mesh):
    placed = (
        P("seq", None),
        P("seq", "db"),
        P("seq", "db"),
        P("seq", "db"),
        P("db", None),
        P(),
        P(None, "db"),
        P(None, "db"),
        P(None, "db"),
        P("db", None),
        P("db", None, None),
        P("seq", None),
        P("seq", None),
    )
    return jax.shard_map(
        per_device, mesh=mesh, in_specs=placed, out_specs=P(("seq", "db"), None), check_vma=False
    )
```

```python
import math

import jax
import jax.numpy as jnp
from jax import lax
from jax.experimental import pallas as pl
from jax.experimental.pallas import tpu as pltpu
from jax.sharding import PartitionSpec as P

HD = 128
SPAN = 64
NLEN = 128
TOK = 256
WIDTH = 512
D = 4096
SHARE = 32
HALF = 2048
NEG_BIG = -1e30
MESH = pl.DeviceIdType.MESH
EXP2_SCALE = math.log2(math.e) / math.sqrt(HD)
BF16 = jnp.bfloat16
F32 = jnp.float32


def remote(src, dst, send, recv, seq, db):
    return pltpu.make_async_remote_copy(
        src_ref=src, dst_ref=dst, send_sem=send, recv_sem=recv, device_id=(seq, db), device_id_type=MESH
    )


def dot_f32(a, b):
    return jnp.dot(a, b, preferred_element_type=F32)


def dot_nt(a, b):
    return lax.dot_general(a, b, (((1,), (1,)), ((), ())), preferred_element_type=F32)


def block_kernel(
    q_ref,
    k_ref,
    v_ref,
    gain_ref,
    shard_ref,
    row_ref,
    hidden_hbm,
    wso_hbm,
    wcq_hbm,
    wck_hbm,
    wcv_hbm,
    wco_hbm,
    enc_hbm,
    out_ref,
    wso,
    wcq,
    wck,
    wcv,
    wco,
    enc,
    hid,
    kvs,
    qst,
    kv,
    qb,
    ob,
    ret,
    sc_buf,
    lsum,
    acc,
    att,
    arr,
    part_a,
    part_b,
    za1,
    ya1,
    yb1,
    zb1,
    za2,
    ya2,
    yb2,
    zb2,
    sum_a,
    sum_b,
    res,
    nf_a,
    nf_b,
    cqa,
    qx,
    kx,
    vx,
    wsem,
    xs,
    xr,
    zs,
    zr,
    cs,
    cr,
    qs,
    qr,
    os_,
    or_,
    es,
    er,
    r1s,
    r1r,
    ags,
    agr,
    r2s,
    r2r,
    ps,
    pr,
):
    s = lax.axis_index("seq")
    d = lax.axis_index("db")
    c = s % 2
    x = (s // 2) % 4
    zl = s // 8
    y = d // 2
    zh = d % 2
    over = 2 * y + 1 - zh
    far = (2, 1, 3)

    def at(zz, xx, cc):
        return (zz * 4 + xx) * 2 + cc

    own_rows = pl.ds(pl.multiple_of(d * SHARE, SHARE), SHARE)

    bar = pltpu.get_barrier_semaphore()
    for step in range(1, 16):
        pl.semaphore_signal(bar, inc=1, device_id=((s + step) % 16, d), device_id_type=MESH)
    for step in range(1, 8):
        pl.semaphore_signal(bar, inc=1, device_id=(s, (d + step) % 8), device_id_type=MESH)

    loads = [
        pltpu.make_async_copy(enc_hbm, enc, wsem.at[0]),
        pltpu.make_async_copy(wso_hbm, wso, wsem.at[1]),
        pltpu.make_async_copy(hidden_hbm.at[own_rows], hid, wsem.at[2]),
        pltpu.make_async_copy(wck_hbm, wck, wsem.at[3]),
        pltpu.make_async_copy(wcv_hbm, wcv, wsem.at[4]),
        pltpu.make_async_copy(wcq_hbm, wcq, wsem.at[5]),
        pltpu.make_async_copy(wco_hbm, wco, wsem.at[6]),
    ]
    for load in loads:
        load.start()
    for h in range(4):
        cols = slice(h * HD, (h + 1) * HD)
        kvs[h, 0] = k_ref[:, cols]
        kvs[h, 1] = v_ref[:, cols]
        qst[h] = q_ref[:, cols]
    pl.semaphore_wait(bar, 22)

    sends = []

    def start(copy):
        copy.start()
        sends.append(copy)

    for dx in (1, 3, 2):
        other = (x + dx) % 4
        start(remote(kvs.at[other], kv.at[s], xs.at[dx], xr.at[dx], at(zl, other, c), d))
    kv[s] = kvs[x]
    low = s % 8
    high = low // 4
    j_to = (1 - high) * low + high * (7 - low)
    slot_to = (s // 8) * 2 + high
    for h in range(4):
        goal = at(j_to // 2, h, j_to % 2)

        @pl.when(goal != s)
        def _():
            remote(qst.at[h], qb.at[slot_to], qs.at[h], qr.at[slot_to], goal, d).start()

        @pl.when(goal == s)
        def _():
            pltpu.make_async_copy(qst.at[h], qb.at[slot_to], qr.at[slot_to]).start()

    def gather_start_y(piece_b, send, recv):
        for dy in far:
            peer = 2 * ((y + dy) % 4) + zh
            start(remote(piece_b(d), piece_b(d), send.at[dy], recv.at[dy], s, peer))

    def gather_start_z(piece_a, piece_b, send, recv):
        start(remote(piece_a(d), piece_a(d), send.at[0], recv.at[0], s, over))
        start(remote(piece_b(d), piece_b(d), send.at[12], recv.at[12], s, over))
        for dy in far:
            peer = 2 * ((y + dy) % 4) + zh
            start(remote(piece_a(d), piece_a(d), send.at[4 + dy], recv.at[4 + dy], s, peer))

    def gather_forward(piece_a, piece_b, send, recv):
        remote(piece_a(over), piece_a(over), send.at[0], recv.at[0], s, over).wait_recv()
        for dy in far:
            peer = 2 * ((y + dy) % 4) + zh
            start(remote(piece_a(over), piece_a(over), send.at[8 + dy], recv.at[8 + dy], s, peer))
        for dy in (1, 3, 2):
            src = 2 * ((y - dy + 4) % 4) + zh
            remote(piece_b(src), piece_b(src), send.at[dy], recv.at[dy], s, src).wait_recv()
            start(
                remote(piece_b(src), piece_b(src), send.at[12 + dy], recv.at[12 + dy], s, over)
            )

    def gather_finish(piece_a, piece_b, send, recv):
        for dy in (1, 3, 2):
            src = 2 * ((y - dy + 4) % 4) + zh
            remote(piece_a(src), piece_a(src), send.at[4 + dy], recv.at[4 + dy], s, src).wait_recv()
        for dy in (1, 3, 2):
            src = 2 * ((y - dy + 4) % 4) + 1 - zh
            remote(piece_a(src), piece_a(src), send.at[8 + dy], recv.at[8 + dy], s, src).wait_recv()
        for dy in (0, 1, 3, 2):
            src = 2 * ((y - dy + 4) % 4) + 1 - zh
            remote(piece_b(src), piece_b(src), send.at[12 + dy], recv.at[12 + dy], s, over).wait_recv()

    loads[0].wait()
    first = jnp.int32(0)
    second = jnp.int32(0)
    found = jnp.int32(0)
    for e in range(8):
        match = shard_ref[e // 2, e % 2] == d
        row = row_ref[e // 2, e % 2]
        first = jnp.where(match & (found == 0), row, first)
        second = jnp.where(match & (found == 1), row, second)
        found = found + match.astype(jnp.int32)
    arr[d] = enc[first]
    arr[8 + d] = enc[second]
    enc_a = lambda i: arr.at[i]
    enc_b = lambda i: arr.at[8 + i]
    gather_start_y(enc_b, es, er)

    def forward(src, k):
        start(remote(kv.at[src], kv.at[src], zs.at[k], zr.at[k], at(1 - zl, x, c), d))
        start(remote(kv.at[src], kv.at[src], cs.at[k], cr.at[k], at(zl, x, 1 - c), d))

    forward(s, 0)
    for dx in (1, 3, 2):
        src = at(zl, (x - dx + 4) % 4, c)
        remote(kv.at[src], kv.at[src], xs.at[dx], xr.at[dx], src, d).wait_recv()
        forward(src, dx)
    gather_start_z(enc_a, enc_b, es, er)
    for dx in (0, 1, 3, 2):
        src = at(1 - zl, (x - dx + 4) % 4, c)
        remote(kv.at[src], kv.at[src], zs.at[dx], zr.at[dx], src, d).wait_recv()
        start(remote(kv.at[src], kv.at[src], cs.at[4 + dx], cr.at[4 + dx], at(zl, x, 1 - c), d))
    for zz in range(2):
        for dx in range(4):
            src = at((zl + zz) % 2, (x - dx + 4) % 4, 1 - c)
            k = 4 * zz + dx
            remote(kv.at[src], kv.at[src], cs.at[k], cr.at[k], src, d).wait_recv()

    gather_forward(enc_a, enc_b, es, er)

    j = zl * 2 + c

    def block_of(i):
        return (i // 2) * 8 + (i % 2) * (7 - j) + (1 - i % 2) * j

    def slot(i, carry):
        b = block_of(i)
        remote(qst.at[0], qb.at[i], qs.at[0], qr.at[i], s, d).wait_recv()
        query = qb[i]
        last = (b + 2) // 2 - 1

        def lanes_max(scores):
            return jnp.maximum(
                jnp.maximum(scores[:, 0:128], scores[:, 128:256]),
                jnp.maximum(scores[:, 256:384], scores[:, 384:512]),
            )

        def first_pass(kb, top):
            keys = kv[pl.ds(2 * kb, 2), 0].reshape(512, HD)
            scores = dot_nt(query, keys)
            sc_buf[kb] = scores
            return jnp.maximum(top, lanes_max(scores))

        top = lax.fori_loop(0, last, first_pass, jnp.full((TOK, 128), NEG_BIG, F32))
        keys = kv[pl.ds(2 * last, 2), 0].reshape(512, HD)
        scores = dot_nt(query, keys)
        key_pos = last * 512 + lax.broadcasted_iota(jnp.int32, (TOK, 512), 1)
        query_pos = b * TOK + lax.broadcasted_iota(jnp.int32, (TOK, 512), 0)
        scores = jnp.where(key_pos <= query_pos, scores, NEG_BIG)
        sc_buf[last] = scores
        top = jnp.max(jnp.maximum(top, lanes_max(scores)), axis=-1, keepdims=True)
        lsum[...] = jnp.zeros_like(lsum)
        acc[...] = jnp.zeros_like(acc)

        def second_pass(kb, carry):
            weights = jnp.exp2((sc_buf[kb] - top) * EXP2_SCALE)
            values = kv[pl.ds(2 * kb, 2), 1].reshape(512, HD)
            lsum[...] += (weights[:, 0:128] + weights[:, 128:256]) + (
                weights[:, 256:384] + weights[:, 384:512]
            )
            acc[...] += dot_f32(weights.astype(BF16), values)
            return carry

        lax.fori_loop(0, last + 1, second_pass, 0)
        total = jnp.sum(lsum[...], axis=-1, keepdims=True)
        ob[i] = (acc[...] / total).astype(BF16)

        @pl.when(b != s)
        def _():
            remote(ob.at[i], ret.at[x], os_.at[i], or_.at[x], b, d).start()

        @pl.when(b == s)
        def _():
            pltpu.make_async_copy(ob.at[i], ret.at[x], or_.at[x]).start()

        return carry

    lax.fori_loop(0, 4, slot, 0)
    for h in range(4):
        remote(ob.at[0], ret.at[h], os_.at[0], or_.at[h], s, d).wait_recv()
        att[:, h * HD : (h + 1) * HD] = ret[h]

    def project(lhs, weight):
        def tile(n, carry):
            cols = pl.ds(pl.multiple_of(n * 512, 512), 512)
            right = pl.ds(pl.multiple_of(HALF + n * 512, 512), 512)
            product = dot_f32(lhs, weight[:, cols]).astype(BF16)
            for share in range(8):
                part_a[(share % 2) * 4 + share // 2, :, cols] = product[
                    share * SHARE : (share + 1) * SHARE
                ]
            product = dot_f32(lhs, weight[:, right]).astype(BF16)
            part_b[:, :, cols] = product.reshape(8, SHARE, 512)
            return carry

        lax.fori_loop(0, 4, tile, 0)

    spread = []

    def go(copy):
        copy.start()
        spread.append(copy)

    def scatter(send, recv, za, ya, yb, zb):
        for dy in (2, 1, 3, 0):
            yy = (y + dy) % 4
            go(
                remote(
                    part_a.at[(1 - zh) * 4 + yy], za.at[yy], send.at[dy], recv.at[dy], s, over
                )
            )
            if dy:
                go(
                    remote(
                        part_b.at[pl.ds(2 * yy, 2)],
                        yb.at[dy],
                        send.at[4 + dy],
                        recv.at[4 + dy],
                        s,
                        2 * yy + zh,
                    )
                )
        for dy in far:
            yy = (y + dy) % 4
            remote(za.at[yy], za.at[yy], send.at[dy], recv.at[dy], s, over).wait_recv()
            sum_a[dy] = (part_a[zh * 4 + yy].astype(F32) + za[yy].astype(F32)).astype(BF16)
            go(
                remote(
                    sum_a.at[dy], ya.at[dy], send.at[8 + dy], recv.at[8 + dy], s, 2 * yy + zh
                )
            )
        for dy in far:
            remote(yb.at[dy], yb.at[dy], send.at[4 + dy], recv.at[4 + dy], s, d).wait_recv()
        total = part_b[over].astype(F32)
        for dy in range(1, 4):
            total = total + yb[dy, 1 - zh].astype(F32)
        sum_b[...] = total.astype(BF16)
        go(remote(sum_b, zb, send.at[12], recv.at[12], s, over))

    def scatter_wait(send, recv, za, ya, zb):
        remote(za.at[0], za.at[y], send.at[0], recv.at[0], s, over).wait_recv()
        for dy in far:
            remote(ya.at[dy], ya.at[dy], send.at[8 + dy], recv.at[8 + dy], s, d).wait_recv()
        remote(zb, zb, send.at[12], recv.at[12], s, over).wait_recv()

    def total_of(half, cols, za, ya, yb, zb):
        if half == 0:
            total = part_a[zh * 4 + y, :, cols].astype(F32) + za[y, :, cols].astype(F32)
            for dy in range(1, 4):
                total = total + ya[dy, :, cols].astype(F32)
        else:
            total = part_b[d, :, cols].astype(F32) + zb[:, cols].astype(F32)
            for dy in range(1, 4):
                total = total + yb[dy, zh, :, cols].astype(F32)
        return total

    loads[1].wait()
    project(att[...], wso)
    scatter(r1s, r1r, za1, ya1, yb1, zb1)

    loads[2].wait()
    scatter_wait(r1s, r1r, za1, ya1, zb1)

    def add_up(n, square):
        cols = pl.ds(pl.multiple_of(n * 512, 512), 512)
        for half in range(2):
            wide = pl.ds(pl.multiple_of(half * HALF + n * 512, 512), 512)
            total = total_of(half, cols, za1, ya1, yb1, zb1) + hid[:, wide].astype(F32)
            res[:, wide] = total
            square = square + total * total
        return square

    square = lax.fori_loop(0, 4, add_up, jnp.zeros((SHARE, 512), F32))
    scale = lax.rsqrt(jnp.sum(square, axis=-1, keepdims=True) / D + 1e-05)

    def normalise(n, carry):
        cols = pl.ds(pl.multiple_of(n * 512, 512), 512)
        for half, held in enumerate((nf_a, nf_b)):
            wide = pl.ds(pl.multiple_of(half * HALF + n * 512, 512), 512)
            held[d, :, cols] = (
                res[:, wide] * scale * gain_ref[:, wide].astype(F32)
            ).astype(BF16)
        return carry

    lax.fori_loop(0, 4, normalise, 0)
    share_a = lambda i: nf_a.at[i]
    share_b = lambda i: nf_b.at[i]
    gather_start_y(share_b, ags, agr)
    gather_start_z(share_a, share_b, ags, agr)

    gather_finish(enc_a, enc_b, es, er)
    loads[3].wait()
    loads[4].wait()

    def cross_pair(e):
        shard = shard_ref[e // 2, e % 2]
        rank = jnp.int32(0)
        for earlier in range(e):
            rank = rank + (shard_ref[earlier // 2, earlier % 2] == shard).astype(jnp.int32)
        entry = arr[jnp.minimum(rank, 1) * 8 + shard]
        rows = slice((e % 2) * NLEN, (e % 2 + 1) * NLEN)
        kx[e // 2 + 1, rows, :] = dot_f32(entry, wck[...]).astype(BF16)
        vx[e // 2 + 1, rows, :] = dot_f32(entry, wcv[...]).astype(BF16)

    cross_pair(6)
    cross_pair(7)

    @pl.when(s < 15)
    def _():
        remote(kx.at[4], kx.at[0], ps.at[0], pr.at[0], s + 1, d).start()
        remote(vx.at[4], vx.at[0], ps.at[1], pr.at[1], s + 1, d).start()

    @pl.when(s == 0)
    def _():
        kx[0] = jnp.zeros((2 * NLEN, WIDTH), BF16)
        vx[0] = jnp.zeros((2 * NLEN, WIDTH), BF16)

    gather_forward(share_a, share_b, ags, agr)
    for e in range(6):
        cross_pair(e)
    for copy in spread:
        copy.wait_send()
    spread.clear()
    loads[5].wait()
    gather_finish(share_a, share_b, ags, agr)

    cqa[...] = jnp.zeros_like(cqa)

    def contract(n, carry):
        cols = pl.ds(pl.multiple_of(n * 512, 512), 512)
        right = pl.ds(pl.multiple_of(HALF + n * 512, 512), 512)
        cqa[...] += dot_f32(nf_a[:, :, cols].reshape(TOK, 512), wcq[cols, :]) + dot_f32(
            nf_b[:, :, cols].reshape(TOK, 512), wcq[right, :]
        )
        return carry

    lax.fori_loop(0, 4, contract, 0)
    qx[...] = pltpu.roll(cqa[...].astype(BF16).astype(F32), 1, 0).astype(BF16)

    @pl.when(s > 0)
    def _():
        remote(kx.at[4], kx.at[0], ps.at[0], pr.at[0], s, d).wait_recv()
        remote(vx.at[4], vx.at[0], ps.at[1], pr.at[1], s, d).wait_recv()

    def attend(query, keys, values):
        scores = dot_nt(query, keys)
        top = jnp.max(scores, axis=-1, keepdims=True)
        weights = jnp.exp2((scores - top) * EXP2_SCALE)
        total = jnp.sum(weights, axis=-1, keepdims=True)
        return dot_f32(weights.astype(BF16), values) / total

    def group(g, carry):
        rows = pl.ds(pl.multiple_of(g * SPAN, SPAN), SPAN)
        for h in range(4):
            cols = slice(h * HD, (h + 1) * HD)
            cqa[rows, cols] = attend(qx[rows, cols], kx[g, :, cols], vx[g, :, cols])
        return carry

    lax.fori_loop(0, 4, group, 0)
    for h in range(4):
        cols = slice(h * HD, (h + 1) * HD)
        tail = attend(qx[0:16, cols], kx[4, :, cols], vx[4, :, cols])
        first_row = lax.broadcasted_iota(jnp.int32, (16, HD), 0) == 0
        cqa[0:16, cols] = jnp.where(first_row, tail, cqa[0:16, cols])
    att[...] = pltpu.roll(cqa[...], TOK - 1, 0).astype(BF16)

    loads[6].wait()
    project(att[...], wco)
    scatter(r2s, r2r, za2, ya2, yb2, zb2)
    scatter_wait(r2s, r2r, za2, ya2, zb2)

    def finish(n, carry):
        cols = pl.ds(pl.multiple_of(n * 512, 512), 512)
        for half in range(2):
            wide = pl.ds(pl.multiple_of(half * HALF + n * 512, 512), 512)
            out_ref[:, wide] = res[:, wide] + total_of(half, cols, za2, ya2, yb2, zb2)
        return carry

    lax.fori_loop(0, 4, finish, 0)

    for copy in spread:
        copy.wait_send()
    for copy in sends:
        copy.wait_send()
    for h in range(4):
        goal = at(j_to // 2, h, j_to % 2)

        @pl.when(goal != s)
        def _():
            remote(qst.at[h], qb.at[0], qs.at[h], qr.at[0], goal, d).wait_send()

    for i in range(4):

        @pl.when(block_of(i) != s)
        def _():
            remote(ob.at[i], ret.at[0], os_.at[i], or_.at[0], s, d).wait_send()

    @pl.when(s < 15)
    def _():
        remote(kx.at[4], kx.at[0], ps.at[0], pr.at[0], s, d).wait_send()
        remote(vx.at[4], vx.at[0], ps.at[1], pr.at[1], s, d).wait_send()


def per_device(
    hidden_in,
    query_rows,
    key_rows,
    value_rows,
    w_self_out,
    norm_gain,
    w_cross_q,
    w_cross_k,
    w_cross_v,
    w_cross_out,
    enc_table,
    nb_shard,
    nb_row,
):
    vmem = pl.BlockSpec(memory_space=pltpu.VMEM)
    smem = pl.BlockSpec(memory_space=pltpu.SMEM)
    hbm = pl.BlockSpec(memory_space=pl.ANY)
    scratch = [
        pltpu.VMEM((WIDTH, D), BF16),
        pltpu.VMEM((D, WIDTH), BF16),
        pltpu.VMEM((1024, WIDTH), BF16),
        pltpu.VMEM((1024, WIDTH), BF16),
        pltpu.VMEM((WIDTH, D), BF16),
        pltpu.VMEM((8, NLEN, 1024), BF16),
        pltpu.VMEM((SHARE, D), BF16),
        pltpu.VMEM((4, 2, TOK, HD), BF16),
        pltpu.VMEM((4, TOK, HD), BF16),
        pltpu.VMEM((16, 2, TOK, HD), BF16),
        pltpu.VMEM((4, TOK, HD), BF16),
        pltpu.VMEM((4, TOK, HD), BF16),
        pltpu.VMEM((4, TOK, HD), BF16),
        pltpu.VMEM((8, TOK, 512), F32),
        pltpu.VMEM((TOK, HD), F32),
        pltpu.VMEM((TOK, HD), F32),
        pltpu.VMEM((TOK, WIDTH), BF16),
        pltpu.VMEM((16, NLEN, 1024), BF16),
        pltpu.VMEM((8, SHARE, HALF), BF16),
        pltpu.VMEM((8, SHARE, HALF), BF16),
    ]
    scratch += [
        pltpu.VMEM((4, SHARE, HALF), BF16),
        pltpu.VMEM((4, SHARE, HALF), BF16),
        pltpu.VMEM((4, 2, SHARE, HALF), BF16),
        pltpu.VMEM((SHARE, HALF), BF16),
    ] * 2
    scratch += [
        pltpu.VMEM((4, SHARE, HALF), BF16),
        pltpu.VMEM((SHARE, HALF), BF16),
        pltpu.VMEM((SHARE, D), F32),
        pltpu.VMEM((8, SHARE, HALF), BF16),
        pltpu.VMEM((8, SHARE, HALF), BF16),
        pltpu.VMEM((TOK, WIDTH), F32),
        pltpu.VMEM((TOK, WIDTH), BF16),
        pltpu.VMEM((5, 2 * NLEN, WIDTH), BF16),
        pltpu.VMEM((5, 2 * NLEN, WIDTH), BF16),
    ]
    counts = (7, 4, 4, 4, 4, 8, 8, 4, 4, 4, 4, 16, 16, 13, 13, 16, 16, 13, 13, 2, 2)
    scratch += [pltpu.SemaphoreType.DMA((count,)) for count in counts]
    return pl.pallas_call(
        block_kernel,
        out_shape=jax.ShapeDtypeStruct((SHARE, D), F32),
        in_specs=[vmem] * 4 + [smem] * 2 + [hbm] * 7,
        out_specs=vmem,
        scratch_shapes=scratch,
        compiler_params=pltpu.CompilerParams(
            collective_id=0, has_side_effects=True, vmem_limit_bytes=56 << 20
        ),
        name="retro_block",
    )(
        query_rows,
        key_rows,
        value_rows,
        norm_gain.reshape(1, D),
        nb_shard,
        nb_row,
        hidden_in,
        w_self_out,
        w_cross_q,
        w_cross_k,
        w_cross_v,
        w_cross_out,
        enc_table,
    )


def solution(mesh):
    placed = (
        P("seq", None),
        P("seq", "db"),
        P("seq", "db"),
        P("seq", "db"),
        P("db", None),
        P(),
        P(None, "db"),
        P(None, "db"),
        P(None, "db"),
        P("db", None),
        P("db", None, None),
        P("seq", None),
        P("seq", None),
    )
    return jax.shard_map(
        per_device, mesh=mesh, in_specs=placed, out_specs=P(("seq", "db"), None), check_vma=False
    )
```

```python
import math

import jax
import jax.numpy as jnp
from jax import lax
from jax.experimental import pallas as pl
from jax.experimental.pallas import tpu as pltpu
from jax.sharding import PartitionSpec as P

HD = 128
SPAN = 64
NLEN = 128
TOK = 256
WIDTH = 512
D = 4096
SHARE = 32
HALF = 2048
NEG_BIG = -1e30
MESH = pl.DeviceIdType.MESH
EXP2_SCALE = math.log2(math.e) / math.sqrt(HD)
BF16 = jnp.bfloat16
F32 = jnp.float32


def remote(src, dst, send, recv, seq, db):
    return pltpu.make_async_remote_copy(
        src_ref=src, dst_ref=dst, send_sem=send, recv_sem=recv, device_id=(seq, db), device_id_type=MESH
    )


def dot_f32(a, b):
    return jnp.dot(a, b, preferred_element_type=F32)


def dot_nt(a, b):
    return lax.dot_general(a, b, (((1,), (1,)), ((), ())), preferred_element_type=F32)


def block_kernel(
    q_ref,
    k_ref,
    v_ref,
    gain_hbm,
    shard_hbm,
    row_hbm,
    hidden_hbm,
    wso_hbm,
    wcq_hbm,
    wck_hbm,
    wcv_hbm,
    wco_hbm,
    enc_hbm,
    out_ref,
    gain,
    shard_ref,
    row_ref,
    wso,
    wcq,
    wck,
    wcv,
    wco,
    enc,
    hid,
    kvs,
    qst,
    kv,
    qb,
    ob,
    ret,
    sc_buf,
    lsum,
    acc,
    att,
    arr,
    part_a,
    part_b,
    za1,
    ya1,
    yb1,
    zb1,
    za2,
    ya2,
    yb2,
    zb2,
    sum_a,
    sum_b,
    sum_y,
    res,
    nf_a,
    nf_b,
    cqa,
    qx,
    kx,
    vx,
    wsem,
    xs,
    xr,
    zs,
    zr,
    cs,
    cr,
    qs,
    qr,
    os_,
    or_,
    es,
    er,
    r1s,
    r1r,
    ags,
    agr,
    r2s,
    r2r,
    ps,
    pr,
):
    s = lax.axis_index("seq")
    d = lax.axis_index("db")
    c = s % 2
    x = (s // 2) % 4
    zl = s // 8
    y = d // 2
    zh = d % 2
    over = 2 * y + 1 - zh
    far = (2, 1, 3)

    def at(zz, xx, cc):
        return (zz * 4 + xx) * 2 + cc

    own_rows = pl.ds(pl.multiple_of(d * SHARE, SHARE), SHARE)

    bar = pltpu.get_barrier_semaphore()
    for step in range(1, 16):
        pl.semaphore_signal(bar, inc=1, device_id=((s + step) % 16, d), device_id_type=MESH)
    for step in range(1, 8):
        pl.semaphore_signal(bar, inc=1, device_id=(s, (d + step) % 8), device_id_type=MESH)

    loads = [
        pltpu.make_async_copy(enc_hbm, enc, wsem.at[0]),
        pltpu.make_async_copy(wso_hbm, wso, wsem.at[1]),
        pltpu.make_async_copy(hidden_hbm.at[own_rows], hid, wsem.at[2]),
        pltpu.make_async_copy(wck_hbm, wck, wsem.at[3]),
        pltpu.make_async_copy(wcv_hbm, wcv, wsem.at[4]),
        pltpu.make_async_copy(wcq_hbm, wcq, wsem.at[5]),
        pltpu.make_async_copy(wco_hbm, wco, wsem.at[6]),
        pltpu.make_async_copy(shard_hbm, shard_ref, wsem.at[7]),
        pltpu.make_async_copy(row_hbm, row_ref, wsem.at[8]),
        pltpu.make_async_copy(gain_hbm, gain, wsem.at[9]),
    ]
    for k in (0, 7, 8):
        loads[k].start()
    for h in range(4):
        cols = slice(h * HD, (h + 1) * HD)
        kvs[h, 0] = k_ref[:, cols]
        kvs[h, 1] = v_ref[:, cols]
        qst[h] = q_ref[:, cols]
    pl.semaphore_wait(bar, 22)

    sends = []

    def start(copy):
        copy.start()
        sends.append(copy)

    for dx in (1, 3, 2):
        other = (x + dx) % 4
        start(remote(kvs.at[other], kv.at[s], xs.at[dx], xr.at[dx], at(zl, other, c), d))
    kv[s] = kvs[x]
    def forward(src, k):
        start(remote(kv.at[src], kv.at[src], zs.at[k], zr.at[k], at(1 - zl, x, c), d))
        start(remote(kv.at[src], kv.at[src], cs.at[k], cr.at[k], at(zl, x, 1 - c), d))

    forward(s, 0)
    low = s % 8
    high = low // 4
    j_to = (1 - high) * low + high * (7 - low)
    slot_to = (s // 8) * 2 + high
    for h in range(4):
        goal = at(j_to // 2, h, j_to % 2)

        @pl.when(goal != s)
        def _():
            remote(qst.at[h], qb.at[slot_to], qs.at[h], qr.at[slot_to], goal, d).start()

        @pl.when(goal == s)
        def _():
            pltpu.make_async_copy(qst.at[h], qb.at[slot_to], qr.at[slot_to]).start()

    def share_at(step, side):
        return 2 * ((y + step + 4) % 4) + side

    def flow_copies(flow, piece, side, sems):
        send, recv = sems
        held = piece(share_at(0, side), 0)
        return [
            remote(held, held, send.at[4 * flow + k], recv.at[4 * flow + k], s, share_at(step, zh))
            for k, step in ((0, 1), (1, -1))
        ]

    def flow_send(flow, piece, side, sems):
        for copy in flow_copies(flow, piece, side, sems):
            start(copy)

    def flow_forward(flow, piece, side, sems, then=None):
        send, recv = sems
        for k, step in ((0, 1), (1, -1)):
            came = share_at(-step, side)
            held = piece(came, 0)
            remote(held, held, send.at[4 * flow + k], recv.at[4 * flow + k], s, d).wait_recv()
            part = piece(came, 1 + k)
            k2 = 4 * flow + 2 + k
            start(remote(part, part, send.at[k2], recv.at[k2], s, share_at(step, zh)))
            if then is not None:
                then(came, k)

    def flow_last(flow, piece, side, sems):
        send, recv = sems
        for k in range(2):
            part = piece(share_at(2, side), 1 + k)
            k2 = 4 * flow + 2 + k
            remote(part, part, send.at[k2], recv.at[k2], s, d).wait_recv()

    def cross_send(piece, owner, k, sems):
        send, recv = sems
        held = piece(owner, 0)
        start(remote(held, held, send.at[k], recv.at[k], s, over))

    def cross_wait(piece, owner, k, sems):
        send, recv = sems
        held = piece(owner, 0)
        remote(held, held, send.at[k], recv.at[k], s, over).wait_recv()

    def gather_b_on(piece_b, sems):
        flow_forward(2, piece_b, zh, sems, lambda came, k: cross_send(piece_b, came, 14 + k, sems))

    def gather_a_over(piece_a, sems):
        cross_wait(piece_a, over, 12, sems)
        for copy in flow_copies(1, piece_a, 1 - zh, sems):
            copy.start()

    def gather_a_sent(piece_a, sems):
        for copy in flow_copies(1, piece_a, 1 - zh, sems):
            copy.wait_send()

    def gather_last_on(piece_a, piece_b, sems):
        flow_last(2, piece_b, zh, sems)
        cross_send(piece_b, share_at(2, zh), 16, sems)
        flow_forward(1, piece_a, 1 - zh, sems)

    def gather_finish_a(piece_a, sems):
        flow_last(0, piece_a, zh, sems)
        flow_last(1, piece_a, 1 - zh, sems)

    def gather_finish_b(piece_b, sems):
        for k, step in ((13, 0), (14, -1), (15, 1), (16, 2)):
            cross_wait(piece_b, share_at(step, 1 - zh), k, sems)

    for k in (0, 7, 8):
        loads[k].wait()
    for k in (1, 2, 3, 4, 5, 6, 9):
        loads[k].start()
    first = jnp.int32(0)
    second = jnp.int32(0)
    found = jnp.int32(0)
    for e in range(8):
        match = shard_ref[e % 2, e // 2] == d
        row = row_ref[e % 2, e // 2]
        first = jnp.where(match & (found == 0), row, first)
        second = jnp.where(match & (found == 1), row, second)
        found = found + match.astype(jnp.int32)
    arr[d, 0:NLEN] = enc[first]
    arr[d, NLEN : 2 * NLEN] = enc[second]

    def enc_a(i, part):
        return arr.at[i, pl.ds((0, 0, 96)[part], (192, 96, 96)[part])]

    def enc_b(i, part):
        return arr.at[i, pl.ds((192, 192, 224)[part], (64, 32, 32)[part])]

    enc_sems = (es, er)
    cross_send(enc_a, d, 12, enc_sems)
    flow_send(2, enc_b, zh, enc_sems)
    flow_send(0, enc_a, zh, enc_sems)

    for dx in (1, 3, 2):
        src = at(zl, (x - dx + 4) % 4, c)
        remote(kv.at[src], kv.at[src], xs.at[dx], xr.at[dx], src, d).wait_recv()
        forward(src, dx)
    cross_send(enc_b, d, 13, enc_sems)
    for dx in (0, 1, 3, 2):
        src = at(1 - zl, (x - dx + 4) % 4, c)
        remote(kv.at[src], kv.at[src], zs.at[dx], zr.at[dx], src, d).wait_recv()
        start(remote(kv.at[src], kv.at[src], cs.at[4 + dx], cr.at[4 + dx], at(zl, x, 1 - c), d))
    for zz in range(2):
        for dx in range(4):
            src = at((zl + zz) % 2, (x - dx + 4) % 4, 1 - c)
            k = 4 * zz + dx
            remote(kv.at[src], kv.at[src], cs.at[k], cr.at[k], src, d).wait_recv()

    gather_a_over(enc_a, enc_sems)
    gather_b_on(enc_b, enc_sems)
    flow_forward(0, enc_a, zh, enc_sems)

    j = zl * 2 + c

    def block_of(i):
        return (i // 2) * 8 + (i % 2) * (7 - j) + (1 - i % 2) * j

    def slot(i, carry):
        b = block_of(i)

        remote(qst.at[0], qb.at[i], qs.at[0], qr.at[i], s, d).wait_recv()
        query = qb[i]
        last = (b + 2) // 2 - 1

        def lanes_max(scores):
            return jnp.maximum(
                jnp.maximum(scores[:, 0:128], scores[:, 128:256]),
                jnp.maximum(scores[:, 256:384], scores[:, 384:512]),
            )

        def first_pass(kb, top):
            keys = kv[pl.ds(2 * kb, 2), 0].reshape(512, HD)
            scores = dot_nt(query, keys)
            sc_buf[kb] = scores
            return jnp.maximum(top, lanes_max(scores))

        top = lax.fori_loop(0, last, first_pass, jnp.full((TOK, 128), NEG_BIG, F32))
        keys = kv[pl.ds(2 * last, 2), 0].reshape(512, HD)
        scores = dot_nt(query, keys)
        key_pos = last * 512 + lax.broadcasted_iota(jnp.int32, (TOK, 512), 1)
        query_pos = b * TOK + lax.broadcasted_iota(jnp.int32, (TOK, 512), 0)
        scores = jnp.where(key_pos <= query_pos, scores, NEG_BIG)
        sc_buf[last] = scores
        top = jnp.max(jnp.maximum(top, lanes_max(scores)), axis=-1, keepdims=True)
        lsum[...] = jnp.zeros_like(lsum)
        acc[...] = jnp.zeros_like(acc)

        def second_pass(kb, carry):
            weights = jnp.exp2((sc_buf[kb] - top) * EXP2_SCALE)
            values = kv[pl.ds(2 * kb, 2), 1].reshape(512, HD)
            lsum[...] += (weights[:, 0:128] + weights[:, 128:256]) + (
                weights[:, 256:384] + weights[:, 384:512]
            )
            acc[...] += dot_f32(weights.astype(BF16), values)
            return carry

        lax.fori_loop(0, last + 1, second_pass, 0)
        total = jnp.sum(lsum[...], axis=-1, keepdims=True)
        ob[i] = (acc[...] / total).astype(BF16)

        @pl.when(b != s)
        def _():
            remote(ob.at[i], ret.at[x], os_.at[i], or_.at[x], b, d).start()

        @pl.when(b == s)
        def _():
            pltpu.make_async_copy(ob.at[i], ret.at[x], or_.at[x]).start()

        return carry

    lax.fori_loop(0, 4, slot, 0)
    gather_last_on(enc_a, enc_b, enc_sems)
    for h in range(4):
        remote(ob.at[0], ret.at[h], os_.at[0], or_.at[h], s, d).wait_recv()
        att[:, h * HD : (h + 1) * HD] = ret[h]

    def project_a(lhs, weight):
        def tile(n, carry):
            cols = pl.ds(pl.multiple_of(n * 512, 512), 512)
            product = dot_f32(lhs, weight[:, cols]).astype(BF16)
            for share in range(8):
                part_a[(share % 2) * 4 + share // 2, :, cols] = product[
                    share * SHARE : (share + 1) * SHARE
                ]
            return carry

        lax.fori_loop(0, 4, tile, 0)

    def project_b(lhs, weight):
        def tile(n, carry):
            cols = pl.ds(pl.multiple_of(n * 512, 512), 512)
            right = pl.ds(pl.multiple_of(HALF + n * 512, 512), 512)
            product = dot_f32(lhs, weight[:, right]).astype(BF16)
            part_b[:, :, cols] = product.reshape(8, SHARE, 512)
            return carry

        lax.fori_loop(0, 4, tile, 0)

    spread = []

    def go(copy):
        copy.start()
        spread.append(copy)

    def scatter(lhs, weight, send, recv, za, ya, yb, zb):
        project_a(lhs, weight)
        for dy in (2, 1, 3, 0):
            yy = (y + dy) % 4
            go(remote(part_a.at[(1 - zh) * 4 + yy], za.at[yy], send.at[dy], recv.at[dy], s, over))
        project_b(lhs, weight)
        steps = ((0, 1), (1, -1))
        for k, step in steps:
            go(
                remote(
                    part_b.at[share_at(2, k)],
                    yb.at[k],
                    send.at[4 + k],
                    recv.at[4 + k],
                    s,
                    share_at(step, zh),
                )
            )
        for k, step in steps:
            go(
                remote(
                    part_b.at[share_at(step, 1 - k)],
                    yb.at[4 + k],
                    send.at[12 + k],
                    recv.at[12 + k],
                    s,
                    share_at(step, zh),
                )
            )
        for k, step in steps:
            remote(yb.at[k], yb.at[k], send.at[4 + k], recv.at[4 + k], s, d).wait_recv()
            sum_y[k] = (part_b[share_at(step, k)].astype(F32) + yb[k].astype(F32)).astype(BF16)
            go(
                remote(
                    sum_y.at[k], yb.at[2 + k], send.at[6 + k], recv.at[6 + k], s, share_at(step, zh)
                )
            )
        for dy in far:
            yy = (y + dy) % 4
            remote(za.at[yy], za.at[yy], send.at[dy], recv.at[dy], s, over).wait_recv()
            sum_a[dy] = (part_a[zh * 4 + yy].astype(F32) + za[yy].astype(F32)).astype(BF16)
            go(
                remote(
                    sum_a.at[dy], ya.at[dy], send.at[8 + dy], recv.at[8 + dy], s, 2 * yy + zh
                )
            )
        for k in range(2):
            remote(yb.at[2 + k], yb.at[2 + k], send.at[6 + k], recv.at[6 + k], s, d).wait_recv()
            remote(yb.at[4 + k], yb.at[4 + k], send.at[12 + k], recv.at[12 + k], s, d).wait_recv()
        sum_b[...] = b_share(over, 1 - zh, slice(None), yb).astype(BF16)
        go(remote(sum_b, zb, send.at[14], recv.at[14], s, over))

    def b_share(share, k, cols, yb):
        return (
            part_b[share, :, cols].astype(F32)
            + yb[2 + k, :, cols].astype(F32)
            + yb[5 - k, :, cols].astype(F32)
        )

    def scatter_wait(send, recv, za, ya, zb):
        remote(za.at[0], za.at[y], send.at[0], recv.at[0], s, over).wait_recv()
        for dy in far:
            remote(ya.at[dy], ya.at[dy], send.at[8 + dy], recv.at[8 + dy], s, d).wait_recv()
        remote(zb, zb, send.at[14], recv.at[14], s, over).wait_recv()

    def total_of(half, cols, za, ya, yb, zb):
        if half == 0:
            total = part_a[zh * 4 + y, :, cols].astype(F32) + za[y, :, cols].astype(F32)
            for dy in range(1, 4):
                total = total + ya[dy, :, cols].astype(F32)
        else:
            total = b_share(d, zh, cols, yb) + zb[:, cols].astype(F32)
        return total

    loads[1].wait()
    scatter(att[...], wso, r1s, r1r, za1, ya1, yb1, zb1)

    loads[2].wait()
    loads[9].wait()
    scatter_wait(r1s, r1r, za1, ya1, zb1)

    def add_up(n, square):
        cols = pl.ds(pl.multiple_of(n * 512, 512), 512)
        for half in range(2):
            wide = pl.ds(pl.multiple_of(half * HALF + n * 512, 512), 512)
            total = total_of(half, cols, za1, ya1, yb1, zb1) + hid[:, wide].astype(F32)
            res[:, wide] = total
            square = square + total * total
        return square

    square = lax.fori_loop(0, 4, add_up, jnp.zeros((SHARE, 512), F32))
    scale = lax.rsqrt(jnp.sum(square, axis=-1, keepdims=True) / D + 1e-05)

    def normalise(n, carry):
        cols = pl.ds(pl.multiple_of(n * 512, 512), 512)
        for half, held in enumerate((nf_a, nf_b)):
            wide = pl.ds(pl.multiple_of(half * HALF + n * 512, 512), 512)
            held[d, :, cols] = (
                res[:, wide] * scale * gain[wide].astype(F32)
            ).astype(BF16)
        return carry

    lax.fori_loop(0, 4, normalise, 0)

    def share_a(i, part):
        return nf_a.at[i, pl.ds((0, 0, 16)[part], (32, 16, 16)[part])]

    def share_b(i, part):
        return nf_b.at[i, pl.ds((0, 0, 16)[part], (32, 16, 16)[part])]

    ag_sems = (ags, agr)
    cross_send(share_a, d, 12, ag_sems)
    flow_send(2, share_b, zh, ag_sems)
    flow_send(0, share_a, zh, ag_sems)
    cross_send(share_b, d, 13, ag_sems)

    gather_finish_a(enc_a, enc_sems)
    gather_finish_b(enc_b, enc_sems)
    loads[3].wait()
    loads[4].wait()

    def cross_pair(e):
        shard = shard_ref[e % 2, e // 2]
        rank = jnp.int32(0)
        for earlier in range(e):
            rank = rank + (shard_ref[earlier % 2, earlier // 2] == shard).astype(jnp.int32)
        entry = arr.reshape(16, NLEN, 1024)[shard * 2 + jnp.minimum(rank, 1)]
        rows = slice((e % 2) * NLEN, (e % 2 + 1) * NLEN)
        kx[e // 2 + 1, rows, :] = dot_f32(entry, wck[...]).astype(BF16)
        vx[e // 2 + 1, rows, :] = dot_f32(entry, wcv[...]).astype(BF16)

    cross_pair(6)
    cross_pair(7)

    @pl.when(s < 15)
    def _():
        remote(kx.at[4], kx.at[0], ps.at[0], pr.at[0], s + 1, d).start()
        remote(vx.at[4], vx.at[0], ps.at[1], pr.at[1], s + 1, d).start()

    @pl.when(s == 0)
    def _():
        kx[0] = jnp.zeros((2 * NLEN, WIDTH), BF16)
        vx[0] = jnp.zeros((2 * NLEN, WIDTH), BF16)

    gather_a_over(share_a, ag_sems)
    gather_b_on(share_b, ag_sems)
    flow_forward(0, share_a, zh, ag_sems)
    for e in range(4):
        cross_pair(e)
    gather_last_on(share_a, share_b, ag_sems)
    for e in range(4, 6):
        cross_pair(e)
    for copy in spread:
        copy.wait_send()
    spread.clear()
    loads[5].wait()
    gather_finish_a(share_a, ag_sems)

    cqa[...] = jnp.zeros_like(cqa)

    def contract_a(n, carry):
        cols = pl.ds(pl.multiple_of(n * 512, 512), 512)
        cqa[...] += dot_f32(nf_a[:, :, cols].reshape(TOK, 512), wcq[cols, :])
        return carry

    def contract_b(n, carry):
        cols = pl.ds(pl.multiple_of(n * 512, 512), 512)
        right = pl.ds(pl.multiple_of(HALF + n * 512, 512), 512)
        cqa[...] += dot_f32(nf_b[:, :, cols].reshape(TOK, 512), wcq[right, :])
        return carry

    lax.fori_loop(0, 4, contract_a, 0)
    gather_finish_b(share_b, ag_sems)
    lax.fori_loop(0, 4, contract_b, 0)
    qx[...] = pltpu.roll(cqa[...].astype(BF16).astype(F32), 1, 0).astype(BF16)

    @pl.when(s > 0)
    def _():
        remote(kx.at[4], kx.at[0], ps.at[0], pr.at[0], s, d).wait_recv()
        remote(vx.at[4], vx.at[0], ps.at[1], pr.at[1], s, d).wait_recv()

    def attend(query, keys, values):
        scores = dot_nt(query, keys)
        top = jnp.max(scores, axis=-1, keepdims=True)
        weights = jnp.exp2((scores - top) * EXP2_SCALE)
        total = jnp.sum(weights, axis=-1, keepdims=True)
        return dot_f32(weights.astype(BF16), values) / total

    def group(g, carry):
        rows = pl.ds(pl.multiple_of(g * SPAN, SPAN), SPAN)
        for h in range(4):
            cols = slice(h * HD, (h + 1) * HD)
            cqa[rows, cols] = attend(qx[rows, cols], kx[g, :, cols], vx[g, :, cols])
        return carry

    lax.fori_loop(0, 4, group, 0)
    for h in range(4):
        cols = slice(h * HD, (h + 1) * HD)
        tail = attend(qx[0:16, cols], kx[4, :, cols], vx[4, :, cols])
        first_row = lax.broadcasted_iota(jnp.int32, (16, HD), 0) == 0
        cqa[0:16, cols] = jnp.where(first_row, tail, cqa[0:16, cols])
    att[...] = pltpu.roll(cqa[...], TOK - 1, 0).astype(BF16)

    loads[6].wait()
    scatter(att[...], wco, r2s, r2r, za2, ya2, yb2, zb2)
    scatter_wait(r2s, r2r, za2, ya2, zb2)

    def finish(n, carry):
        cols = pl.ds(pl.multiple_of(n * 512, 512), 512)
        for half in range(2):
            wide = pl.ds(pl.multiple_of(half * HALF + n * 512, 512), 512)
            out_ref[:, wide] = res[:, wide] + total_of(half, cols, za2, ya2, yb2, zb2)
        return carry

    lax.fori_loop(0, 4, finish, 0)

    for copy in spread:
        copy.wait_send()
    for copy in sends:
        copy.wait_send()
    gather_a_sent(enc_a, enc_sems)
    gather_a_sent(share_a, ag_sems)
    for h in range(4):
        goal = at(j_to // 2, h, j_to % 2)

        @pl.when(goal != s)
        def _():
            remote(qst.at[h], qb.at[0], qs.at[h], qr.at[0], goal, d).wait_send()

    for i in range(4):

        @pl.when(block_of(i) != s)
        def _():
            remote(ob.at[i], ret.at[0], os_.at[i], or_.at[0], s, d).wait_send()

    @pl.when(s < 15)
    def _():
        remote(kx.at[4], kx.at[0], ps.at[0], pr.at[0], s, d).wait_send()
        remote(vx.at[4], vx.at[0], ps.at[1], pr.at[1], s, d).wait_send()


def per_device(
    hidden_in,
    query_rows,
    key_rows,
    value_rows,
    w_self_out,
    norm_gain,
    w_cross_q,
    w_cross_k,
    w_cross_v,
    w_cross_out,
    enc_table,
    nb_shard,
    nb_row,
):
    vmem = pl.BlockSpec(memory_space=pltpu.VMEM)
    hbm = pl.BlockSpec(memory_space=pl.ANY)
    scratch = [
        pltpu.VMEM((D,), BF16),
        pltpu.SMEM((2, 4), jnp.int32),
        pltpu.SMEM((2, 4), jnp.int32),
        pltpu.VMEM((WIDTH, D), BF16),
        pltpu.VMEM((D, WIDTH), BF16),
        pltpu.VMEM((1024, WIDTH), BF16),
        pltpu.VMEM((1024, WIDTH), BF16),
        pltpu.VMEM((WIDTH, D), BF16),
        pltpu.VMEM((8, NLEN, 1024), BF16),
        pltpu.VMEM((SHARE, D), BF16),
        pltpu.VMEM((4, 2, TOK, HD), BF16),
        pltpu.VMEM((4, TOK, HD), BF16),
        pltpu.VMEM((16, 2, TOK, HD), BF16),
        pltpu.VMEM((4, TOK, HD), BF16),
        pltpu.VMEM((4, TOK, HD), BF16),
        pltpu.VMEM((4, TOK, HD), BF16),
        pltpu.VMEM((8, TOK, 512), F32),
        pltpu.VMEM((TOK, HD), F32),
        pltpu.VMEM((TOK, HD), F32),
        pltpu.VMEM((TOK, WIDTH), BF16),
        pltpu.VMEM((8, 2 * NLEN, 1024), BF16),
        pltpu.VMEM((8, SHARE, HALF), BF16),
        pltpu.VMEM((8, SHARE, HALF), BF16),
    ]
    scratch += [
        pltpu.VMEM((4, SHARE, HALF), BF16),
        pltpu.VMEM((4, SHARE, HALF), BF16),
        pltpu.VMEM((6, SHARE, HALF), BF16),
        pltpu.VMEM((SHARE, HALF), BF16),
    ] * 2
    scratch += [
        pltpu.VMEM((4, SHARE, HALF), BF16),
        pltpu.VMEM((SHARE, HALF), BF16),
        pltpu.VMEM((2, SHARE, HALF), BF16),
        pltpu.VMEM((SHARE, D), F32),
        pltpu.VMEM((8, SHARE, HALF), BF16),
        pltpu.VMEM((8, SHARE, HALF), BF16),
        pltpu.VMEM((TOK, WIDTH), F32),
        pltpu.VMEM((TOK, WIDTH), BF16),
        pltpu.VMEM((5, 2 * NLEN, WIDTH), BF16),
        pltpu.VMEM((5, 2 * NLEN, WIDTH), BF16),
    ]
    counts = (10, 4, 4, 4, 4, 8, 8, 4, 4, 4, 4, 17, 17, 15, 15, 17, 17, 15, 15, 2, 2)
    scratch += [pltpu.SemaphoreType.DMA((count,)) for count in counts]
    return pl.pallas_call(
        block_kernel,
        out_shape=jax.ShapeDtypeStruct((SHARE, D), F32),
        in_specs=[vmem] * 3 + [hbm] * 10,
        out_specs=vmem,
        scratch_shapes=scratch,
        compiler_params=pltpu.CompilerParams(
            collective_id=0, has_side_effects=True, vmem_limit_bytes=56 << 20
        ),
        name="retro_block",
    )(
        query_rows,
        key_rows,
        value_rows,
        norm_gain,
        nb_shard.T,
        nb_row.T,
        hidden_in,
        w_self_out,
        w_cross_q,
        w_cross_k,
        w_cross_v,
        w_cross_out,
        enc_table,
    )


def solution(mesh):
    placed = (
        P("seq", None),
        P("seq", "db"),
        P("seq", "db"),
        P("seq", "db"),
        P("db", None),
        P(),
        P(None, "db"),
        P(None, "db"),
        P(None, "db"),
        P("db", None),
        P("db", None, None),
        P("seq", None),
        P("seq", None),
    )
    return jax.shard_map(
        per_device, mesh=mesh, in_specs=placed, out_specs=P(("seq", "db"), None), check_vma=False
    )
```

```python
import math

import jax
import jax.numpy as jnp
from jax import lax
from jax.experimental import pallas as pl
from jax.experimental.pallas import tpu as pltpu
from jax.sharding import PartitionSpec as P

HD = 128
SPAN = 64
NLEN = 128
TOK = 256
WIDTH = 512
D = 4096
SHARE = 32
HALF = 2048
NEG_BIG = -1e30
MESH = pl.DeviceIdType.MESH
EXP2_SCALE = math.log2(math.e) / math.sqrt(HD)
BF16 = jnp.bfloat16
F32 = jnp.float32


def remote(src, dst, send, recv, seq, db):
    return pltpu.make_async_remote_copy(
        src_ref=src, dst_ref=dst, send_sem=send, recv_sem=recv, device_id=(seq, db), device_id_type=MESH
    )


def dot_f32(a, b):
    return jnp.dot(a, b, preferred_element_type=F32)


def dot_nt(a, b):
    return lax.dot_general(a, b, (((1,), (1,)), ((), ())), preferred_element_type=F32)


def block_kernel(
    q_ref,
    k_ref,
    v_ref,
    gain_hbm,
    shard_hbm,
    row_hbm,
    hidden_hbm,
    wso_hbm,
    wcq_hbm,
    wck_hbm,
    wcv_hbm,
    wco_hbm,
    enc_hbm,
    out_ref,
    gain,
    shard_ref,
    row_ref,
    wso,
    wcq,
    wck,
    wcv,
    wco,
    enc,
    hid,
    kvs,
    qst,
    kv,
    qb,
    ob,
    ret,
    sc_buf,
    lsum,
    acc,
    att,
    arr,
    part_a,
    part_b,
    za1,
    ya1,
    yb1,
    zb1,
    za2,
    ya2,
    yb2,
    zb2,
    sum_a,
    sum_b,
    sum_y,
    res,
    nf_a,
    nf_b,
    cqa,
    qx,
    kx,
    vx,
    wsem,
    xs,
    xr,
    zs,
    zr,
    cs,
    cr,
    qs,
    qr,
    os_,
    or_,
    es,
    er,
    r1s,
    r1r,
    ags,
    agr,
    r2s,
    r2r,
    ps,
    pr,
):
    s = lax.axis_index("seq")
    d = lax.axis_index("db")
    c = s % 2
    x = (s // 2) % 4
    zl = s // 8
    y = d // 2
    zh = d % 2
    over = 2 * y + 1 - zh
    far = (2, 1, 3)

    def at(zz, xx, cc):
        return (zz * 4 + xx) * 2 + cc

    own_rows = pl.ds(pl.multiple_of(d * SHARE, SHARE), SHARE)

    bar = pltpu.get_barrier_semaphore()
    for step in range(1, 16):
        pl.semaphore_signal(bar, inc=1, device_id=((s + step) % 16, d), device_id_type=MESH)
    for step in range(1, 8):
        pl.semaphore_signal(bar, inc=1, device_id=(s, (d + step) % 8), device_id_type=MESH)

    loads = [
        pltpu.make_async_copy(enc_hbm, enc, wsem.at[0]),
        pltpu.make_async_copy(wso_hbm, wso, wsem.at[1]),
        pltpu.make_async_copy(hidden_hbm.at[own_rows], hid, wsem.at[2]),
        pltpu.make_async_copy(wck_hbm, wck, wsem.at[3]),
        pltpu.make_async_copy(wcv_hbm, wcv, wsem.at[4]),
        pltpu.make_async_copy(wcq_hbm, wcq, wsem.at[5]),
        pltpu.make_async_copy(wco_hbm, wco, wsem.at[6]),
        pltpu.make_async_copy(shard_hbm, shard_ref, wsem.at[7]),
        pltpu.make_async_copy(row_hbm, row_ref, wsem.at[8]),
        pltpu.make_async_copy(gain_hbm, gain, wsem.at[9]),
    ]
    for k in (0, 7, 8):
        loads[k].start()
    for h in range(4):
        cols = slice(h * HD, (h + 1) * HD)
        kvs[h, 0] = k_ref[:, cols]
        kvs[h, 1] = v_ref[:, cols]
        qst[h] = q_ref[:, cols]
    pl.semaphore_wait(bar, 22)

    sends = []

    def start(copy):
        copy.start()
        sends.append(copy)

    for dx in (1, 3, 2):
        other = (x + dx) % 4
        start(remote(kvs.at[other], kv.at[s], xs.at[dx], xr.at[dx], at(zl, other, c), d))
    kv[s] = kvs[x]
    def forward(src, k):
        start(remote(kv.at[src], kv.at[src], zs.at[k], zr.at[k], at(1 - zl, x, c), d))
        start(remote(kv.at[src], kv.at[src], cs.at[k], cr.at[k], at(zl, x, 1 - c), d))

    forward(s, 0)
    low = s % 8
    high = low // 4
    j_to = (1 - high) * low + high * (7 - low)
    slot_to = (s // 8) * 2 + high
    for h in range(4):
        goal = at(j_to // 2, h, j_to % 2)

        @pl.when(goal != s)
        def _():
            remote(qst.at[h], qb.at[slot_to], qs.at[h], qr.at[slot_to], goal, d).start()

        @pl.when(goal == s)
        def _():
            pltpu.make_async_copy(qst.at[h], qb.at[slot_to], qr.at[slot_to]).start()

    def share_at(step, side):
        return 2 * ((y + step + 4) % 4) + side

    def flow_copies(flow, piece, side, sems):
        send, recv = sems
        held = piece(share_at(0, side), 0)
        return [
            remote(held, held, send.at[4 * flow + k], recv.at[4 * flow + k], s, share_at(step, zh))
            for k, step in ((0, 1), (1, -1))
        ]

    def flow_send(flow, piece, side, sems):
        for copy in flow_copies(flow, piece, side, sems):
            start(copy)

    def flow_forward(flow, piece, side, sems, then=None):
        send, recv = sems
        for k, step in ((0, 1), (1, -1)):
            came = share_at(-step, side)
            held = piece(came, 0)
            remote(held, held, send.at[4 * flow + k], recv.at[4 * flow + k], s, d).wait_recv()
            part = piece(came, 1 + k)
            k2 = 4 * flow + 2 + k
            start(remote(part, part, send.at[k2], recv.at[k2], s, share_at(step, zh)))
            if then is not None:
                then(came, k)

    def flow_last(flow, piece, side, sems):
        send, recv = sems
        for k in range(2):
            part = piece(share_at(2, side), 1 + k)
            k2 = 4 * flow + 2 + k
            remote(part, part, send.at[k2], recv.at[k2], s, d).wait_recv()

    def cross_send(piece, owner, k, sems):
        send, recv = sems
        held = piece(owner, 0)
        start(remote(held, held, send.at[k], recv.at[k], s, over))

    def cross_wait(piece, owner, k, sems):
        send, recv = sems
        held = piece(owner, 0)
        remote(held, held, send.at[k], recv.at[k], s, over).wait_recv()

    def gather_b_on(piece_b, sems):
        flow_forward(2, piece_b, zh, sems, lambda came, k: cross_send(piece_b, came, 14 + k, sems))

    def gather_a_over(piece_a, sems):
        cross_wait(piece_a, over, 12, sems)
        for copy in flow_copies(1, piece_a, 1 - zh, sems):
            copy.start()

    def gather_a_sent(piece_a, sems):
        for copy in flow_copies(1, piece_a, 1 - zh, sems):
            copy.wait_send()

    def gather_last_on(piece_a, piece_b, sems):
        flow_last(2, piece_b, zh, sems)
        cross_send(piece_b, share_at(2, zh), 16, sems)
        flow_forward(1, piece_a, 1 - zh, sems)

    def gather_finish_a(piece_a, sems):
        flow_last(0, piece_a, zh, sems)
        flow_last(1, piece_a, 1 - zh, sems)

    def gather_finish_b(piece_b, sems):
        for k, step in ((13, 0), (14, -1), (15, 1), (16, 2)):
            cross_wait(piece_b, share_at(step, 1 - zh), k, sems)

    for k in (0, 7, 8):
        loads[k].wait()
    first = jnp.int32(0)
    second = jnp.int32(0)
    found = jnp.int32(0)
    for e in range(8):
        match = shard_ref[e % 2, e // 2] == d
        row = row_ref[e % 2, e // 2]
        first = jnp.where(match & (found == 0), row, first)
        second = jnp.where(match & (found == 1), row, second)
        found = found + match.astype(jnp.int32)
    arr[d, 0:NLEN] = enc[first]
    arr[d, NLEN : 2 * NLEN] = enc[second]

    def enc_a(i, part):
        return arr.at[i, pl.ds((0, 0, 96)[part], (192, 96, 96)[part])]

    def enc_b(i, part):
        return arr.at[i, pl.ds((192, 192, 224)[part], (64, 32, 32)[part])]

    enc_sems = (es, er)
    flow_send(2, enc_b, zh, enc_sems)
    flow_send(0, enc_a, zh, enc_sems)

    for dx in (1, 3, 2):
        src = at(zl, (x - dx + 4) % 4, c)
        remote(kv.at[src], kv.at[src], xs.at[dx], xr.at[dx], src, d).wait_recv()
        forward(src, dx)
    cross_send(enc_a, d, 12, enc_sems)
    cross_send(enc_b, d, 13, enc_sems)
    for dx in (0, 1, 3, 2):
        src = at(1 - zl, (x - dx + 4) % 4, c)
        remote(kv.at[src], kv.at[src], zs.at[dx], zr.at[dx], src, d).wait_recv()
        start(remote(kv.at[src], kv.at[src], cs.at[4 + dx], cr.at[4 + dx], at(zl, x, 1 - c), d))
    for zz in range(2):
        for dx in range(4):
            src = at((zl + zz) % 2, (x - dx + 4) % 4, 1 - c)
            k = 4 * zz + dx
            remote(kv.at[src], kv.at[src], cs.at[k], cr.at[k], src, d).wait_recv()

    gather_b_on(enc_b, enc_sems)
    flow_forward(0, enc_a, zh, enc_sems)

    for k in (1, 2, 3, 4, 5, 6, 9):
        loads[k].start()

    j = zl * 2 + c

    def block_of(i):
        return (i // 2) * 8 + (i % 2) * (7 - j) + (1 - i % 2) * j

    def slot(i, carry):
        b = block_of(i)

        @pl.when(i == 2)
        def _():
            gather_a_over(enc_a, enc_sems)


        remote(qst.at[0], qb.at[i], qs.at[0], qr.at[i], s, d).wait_recv()
        query = qb[i]
        last = (b + 2) // 2 - 1

        def lanes_max(scores):
            return jnp.maximum(
                jnp.maximum(scores[:, 0:128], scores[:, 128:256]),
                jnp.maximum(scores[:, 256:384], scores[:, 384:512]),
            )

        def first_pass(kb, top):
            keys = kv[pl.ds(2 * kb, 2), 0].reshape(512, HD)
            scores = dot_nt(query, keys)
            sc_buf[kb] = scores
            return jnp.maximum(top, lanes_max(scores))

        top = lax.fori_loop(0, last, first_pass, jnp.full((TOK, 128), NEG_BIG, F32))
        keys = kv[pl.ds(2 * last, 2), 0].reshape(512, HD)
        scores = dot_nt(query, keys)
        key_pos = last * 512 + lax.broadcasted_iota(jnp.int32, (TOK, 512), 1)
        query_pos = b * TOK + lax.broadcasted_iota(jnp.int32, (TOK, 512), 0)
        scores = jnp.where(key_pos <= query_pos, scores, NEG_BIG)
        sc_buf[last] = scores
        top = jnp.max(jnp.maximum(top, lanes_max(scores)), axis=-1, keepdims=True)
        lsum[...] = jnp.zeros_like(lsum)
        acc[...] = jnp.zeros_like(acc)

        def second_pass(kb, carry):
            weights = jnp.exp2((sc_buf[kb] - top) * EXP2_SCALE)
            values = kv[pl.ds(2 * kb, 2), 1].reshape(512, HD)
            lsum[...] += (weights[:, 0:128] + weights[:, 128:256]) + (
                weights[:, 256:384] + weights[:, 384:512]
            )
            acc[...] += dot_f32(weights.astype(BF16), values)
            return carry

        lax.fori_loop(0, last + 1, second_pass, 0)
        total = jnp.sum(lsum[...], axis=-1, keepdims=True)
        ob[i] = (acc[...] / total).astype(BF16)

        @pl.when(b != s)
        def _():
            remote(ob.at[i], ret.at[x], os_.at[i], or_.at[x], b, d).start()

        @pl.when(b == s)
        def _():
            pltpu.make_async_copy(ob.at[i], ret.at[x], or_.at[x]).start()

        return carry

    lax.fori_loop(0, 4, slot, 0)
    for h in range(4):
        remote(ob.at[0], ret.at[h], os_.at[0], or_.at[h], s, d).wait_recv()
        att[:, h * HD : (h + 1) * HD] = ret[h]

    def project_a(lhs, weight):
        def tile(n, carry):
            cols = pl.ds(pl.multiple_of(n * 512, 512), 512)
            product = dot_f32(lhs, weight[:, cols]).astype(BF16)
            for share in range(8):
                part_a[(share % 2) * 4 + share // 2, :, cols] = product[
                    share * SHARE : (share + 1) * SHARE
                ]
            return carry

        lax.fori_loop(0, 4, tile, 0)

    def project_b(lhs, weight):
        def tile(n, carry):
            cols = pl.ds(pl.multiple_of(n * 512, 512), 512)
            right = pl.ds(pl.multiple_of(HALF + n * 512, 512), 512)
            product = dot_f32(lhs, weight[:, right]).astype(BF16)
            part_b[:, :, cols] = product.reshape(8, SHARE, 512)
            return carry

        lax.fori_loop(0, 4, tile, 0)

    spread = []

    def go(copy):
        copy.start()
        spread.append(copy)

    def scatter(lhs, weight, send, recv, za, ya, yb, zb):
        project_a(lhs, weight)
        for dy in (2, 1, 3, 0):
            yy = (y + dy) % 4
            go(remote(part_a.at[(1 - zh) * 4 + yy], za.at[yy], send.at[dy], recv.at[dy], s, over))
        project_b(lhs, weight)
        steps = ((0, 1), (1, -1))
        for k, step in steps:
            go(
                remote(
                    part_b.at[share_at(2, k)],
                    yb.at[k],
                    send.at[4 + k],
                    recv.at[4 + k],
                    s,
                    share_at(step, zh),
                )
            )
        for k, step in steps:
            go(
                remote(
                    part_b.at[share_at(step, 1 - k)],
                    yb.at[4 + k],
                    send.at[12 + k],
                    recv.at[12 + k],
                    s,
                    share_at(step, zh),
                )
            )
        for k, step in steps:
            remote(yb.at[k], yb.at[k], send.at[4 + k], recv.at[4 + k], s, d).wait_recv()
            sum_y[k] = (part_b[share_at(step, k)].astype(F32) + yb[k].astype(F32)).astype(BF16)
            go(
                remote(
                    sum_y.at[k], yb.at[2 + k], send.at[6 + k], recv.at[6 + k], s, share_at(step, zh)
                )
            )
        for dy in far:
            yy = (y + dy) % 4
            remote(za.at[yy], za.at[yy], send.at[dy], recv.at[dy], s, over).wait_recv()
            sum_a[dy] = (part_a[zh * 4 + yy].astype(F32) + za[yy].astype(F32)).astype(BF16)
            go(
                remote(
                    sum_a.at[dy], ya.at[dy], send.at[8 + dy], recv.at[8 + dy], s, 2 * yy + zh
                )
            )
        for k in range(2):
            remote(yb.at[2 + k], yb.at[2 + k], send.at[6 + k], recv.at[6 + k], s, d).wait_recv()
            remote(yb.at[4 + k], yb.at[4 + k], send.at[12 + k], recv.at[12 + k], s, d).wait_recv()
        sum_b[...] = b_share(over, 1 - zh, slice(None), yb).astype(BF16)
        go(remote(sum_b, zb, send.at[14], recv.at[14], s, over))

    def b_share(share, k, cols, yb):
        return (
            part_b[share, :, cols].astype(F32)
            + yb[2 + k, :, cols].astype(F32)
            + yb[5 - k, :, cols].astype(F32)
        )

    def scatter_wait(send, recv, za, ya, zb):
        remote(za.at[0], za.at[y], send.at[0], recv.at[0], s, over).wait_recv()
        for dy in far:
            remote(ya.at[dy], ya.at[dy], send.at[8 + dy], recv.at[8 + dy], s, d).wait_recv()
        remote(zb, zb, send.at[14], recv.at[14], s, over).wait_recv()

    def total_of(half, cols, za, ya, yb, zb):
        if half == 0:
            total = part_a[zh * 4 + y, :, cols].astype(F32) + za[y, :, cols].astype(F32)
            for dy in range(1, 4):
                total = total + ya[dy, :, cols].astype(F32)
        else:
            total = b_share(d, zh, cols, yb) + zb[:, cols].astype(F32)
        return total

    loads[1].wait()
    scatter(att[...], wso, r1s, r1r, za1, ya1, yb1, zb1)
    gather_last_on(enc_a, enc_b, enc_sems)

    loads[2].wait()
    loads[9].wait()
    scatter_wait(r1s, r1r, za1, ya1, zb1)

    def add_up(n, square):
        cols = pl.ds(pl.multiple_of(n * 512, 512), 512)
        for half in range(2):
            wide = pl.ds(pl.multiple_of(half * HALF + n * 512, 512), 512)
            total = total_of(half, cols, za1, ya1, yb1, zb1) + hid[:, wide].astype(F32)
            res[:, wide] = total
            square = square + total * total
        return square

    square = lax.fori_loop(0, 4, add_up, jnp.zeros((SHARE, 512), F32))
    scale = lax.rsqrt(jnp.sum(square, axis=-1, keepdims=True) / D + 1e-05)

    def normalise(n, carry):
        cols = pl.ds(pl.multiple_of(n * 512, 512), 512)
        for half, held in enumerate((nf_a, nf_b)):
            wide = pl.ds(pl.multiple_of(half * HALF + n * 512, 512), 512)
            held[d, :, cols] = (
                res[:, wide] * scale * gain[wide].astype(F32)
            ).astype(BF16)
        return carry

    lax.fori_loop(0, 4, normalise, 0)

    def share_a(i, part):
        return nf_a.at[i, pl.ds((0, 0, 16)[part], (32, 16, 16)[part])]

    def share_b(i, part):
        return nf_b.at[i, pl.ds((0, 0, 16)[part], (32, 16, 16)[part])]

    ag_sems = (ags, agr)
    cross_send(share_a, d, 12, ag_sems)
    flow_send(2, share_b, zh, ag_sems)
    flow_send(0, share_a, zh, ag_sems)
    cross_send(share_b, d, 13, ag_sems)

    gather_finish_a(enc_a, enc_sems)
    gather_finish_b(enc_b, enc_sems)
    loads[3].wait()
    loads[4].wait()

    def cross_pair(e):
        shard = shard_ref[e % 2, e // 2]
        rank = jnp.int32(0)
        for earlier in range(e):
            rank = rank + (shard_ref[earlier % 2, earlier // 2] == shard).astype(jnp.int32)
        entry = arr.reshape(16, NLEN, 1024)[shard * 2 + jnp.minimum(rank, 1)]
        rows = slice((e % 2) * NLEN, (e % 2 + 1) * NLEN)
        kx[e // 2 + 1, rows, :] = dot_f32(entry, wck[...]).astype(BF16)
        vx[e // 2 + 1, rows, :] = dot_f32(entry, wcv[...]).astype(BF16)

    cross_pair(6)
    cross_pair(7)

    @pl.when(s < 15)
    def _():
        remote(kx.at[4], kx.at[0], ps.at[0], pr.at[0], s + 1, d).start()
        remote(vx.at[4], vx.at[0], ps.at[1], pr.at[1], s + 1, d).start()

    @pl.when(s == 0)
    def _():
        kx[0] = jnp.zeros((2 * NLEN, WIDTH), BF16)
        vx[0] = jnp.zeros((2 * NLEN, WIDTH), BF16)

    gather_a_over(share_a, ag_sems)
    gather_b_on(share_b, ag_sems)
    flow_forward(0, share_a, zh, ag_sems)
    for e in range(4):
        cross_pair(e)
    gather_last_on(share_a, share_b, ag_sems)
    for e in range(4, 6):
        cross_pair(e)
    for copy in spread:
        copy.wait_send()
    spread.clear()
    loads[5].wait()
    gather_finish_a(share_a, ag_sems)

    cqa[...] = jnp.zeros_like(cqa)

    def contract_a(n, carry):
        cols = pl.ds(pl.multiple_of(n * 512, 512), 512)
        cqa[...] += dot_f32(nf_a[:, :, cols].reshape(TOK, 512), wcq[cols, :])
        return carry

    def contract_b(n, carry):
        cols = pl.ds(pl.multiple_of(n * 512, 512), 512)
        right = pl.ds(pl.multiple_of(HALF + n * 512, 512), 512)
        cqa[...] += dot_f32(nf_b[:, :, cols].reshape(TOK, 512), wcq[right, :])
        return carry

    lax.fori_loop(0, 4, contract_a, 0)
    gather_finish_b(share_b, ag_sems)
    lax.fori_loop(0, 4, contract_b, 0)
    qx[...] = pltpu.roll(cqa[...].astype(BF16).astype(F32), 1, 0).astype(BF16)

    @pl.when(s > 0)
    def _():
        remote(kx.at[4], kx.at[0], ps.at[0], pr.at[0], s, d).wait_recv()
        remote(vx.at[4], vx.at[0], ps.at[1], pr.at[1], s, d).wait_recv()

    def attend(query, keys, values):
        scores = dot_nt(query, keys)
        top = jnp.max(scores, axis=-1, keepdims=True)
        weights = jnp.exp2((scores - top) * EXP2_SCALE)
        total = jnp.sum(weights, axis=-1, keepdims=True)
        return dot_f32(weights.astype(BF16), values) / total

    def group(g, carry):
        rows = pl.ds(pl.multiple_of(g * SPAN, SPAN), SPAN)
        for h in range(4):
            cols = slice(h * HD, (h + 1) * HD)
            cqa[rows, cols] = attend(qx[rows, cols], kx[g, :, cols], vx[g, :, cols])
        return carry

    lax.fori_loop(0, 4, group, 0, unroll=True)
    for h in range(4):
        cols = slice(h * HD, (h + 1) * HD)
        tail = attend(qx[0:16, cols], kx[4, :, cols], vx[4, :, cols])
        first_row = lax.broadcasted_iota(jnp.int32, (16, HD), 0) == 0
        cqa[0:16, cols] = jnp.where(first_row, tail, cqa[0:16, cols])
    att[...] = pltpu.roll(cqa[...], TOK - 1, 0).astype(BF16)

    loads[6].wait()
    scatter(att[...], wco, r2s, r2r, za2, ya2, yb2, zb2)
    scatter_wait(r2s, r2r, za2, ya2, zb2)

    def finish(n, carry):
        cols = pl.ds(pl.multiple_of(n * 512, 512), 512)
        for half in range(2):
            wide = pl.ds(pl.multiple_of(half * HALF + n * 512, 512), 512)
            out_ref[:, wide] = res[:, wide] + total_of(half, cols, za2, ya2, yb2, zb2)
        return carry

    lax.fori_loop(0, 4, finish, 0)

    for copy in spread:
        copy.wait_send()
    for copy in sends:
        copy.wait_send()
    gather_a_sent(enc_a, enc_sems)
    gather_a_sent(share_a, ag_sems)
    for h in range(4):
        goal = at(j_to // 2, h, j_to % 2)

        @pl.when(goal != s)
        def _():
            remote(qst.at[h], qb.at[0], qs.at[h], qr.at[0], goal, d).wait_send()

    for i in range(4):

        @pl.when(block_of(i) != s)
        def _():
            remote(ob.at[i], ret.at[0], os_.at[i], or_.at[0], s, d).wait_send()

    @pl.when(s < 15)
    def _():
        remote(kx.at[4], kx.at[0], ps.at[0], pr.at[0], s, d).wait_send()
        remote(vx.at[4], vx.at[0], ps.at[1], pr.at[1], s, d).wait_send()


def per_device(
    hidden_in,
    query_rows,
    key_rows,
    value_rows,
    w_self_out,
    norm_gain,
    w_cross_q,
    w_cross_k,
    w_cross_v,
    w_cross_out,
    enc_table,
    nb_shard,
    nb_row,
):
    vmem = pl.BlockSpec(memory_space=pltpu.VMEM)
    hbm = pl.BlockSpec(memory_space=pl.ANY)
    scratch = [
        pltpu.VMEM((D,), BF16),
        pltpu.SMEM((2, 4), jnp.int32),
        pltpu.SMEM((2, 4), jnp.int32),
        pltpu.VMEM((WIDTH, D), BF16),
        pltpu.VMEM((D, WIDTH), BF16),
        pltpu.VMEM((1024, WIDTH), BF16),
        pltpu.VMEM((1024, WIDTH), BF16),
        pltpu.VMEM((WIDTH, D), BF16),
        pltpu.VMEM((8, NLEN, 1024), BF16),
        pltpu.VMEM((SHARE, D), BF16),
        pltpu.VMEM((4, 2, TOK, HD), BF16),
        pltpu.VMEM((4, TOK, HD), BF16),
        pltpu.VMEM((16, 2, TOK, HD), BF16),
        pltpu.VMEM((4, TOK, HD), BF16),
        pltpu.VMEM((4, TOK, HD), BF16),
        pltpu.VMEM((4, TOK, HD), BF16),
        pltpu.VMEM((8, TOK, 512), F32),
        pltpu.VMEM((TOK, HD), F32),
        pltpu.VMEM((TOK, HD), F32),
        pltpu.VMEM((TOK, WIDTH), BF16),
        pltpu.VMEM((8, 2 * NLEN, 1024), BF16),
        pltpu.VMEM((8, SHARE, HALF), BF16),
        pltpu.VMEM((8, SHARE, HALF), BF16),
    ]
    scratch += [
        pltpu.VMEM((4, SHARE, HALF), BF16),
        pltpu.VMEM((4, SHARE, HALF), BF16),
        pltpu.VMEM((6, SHARE, HALF), BF16),
        pltpu.VMEM((SHARE, HALF), BF16),
    ] * 2
    scratch += [
        pltpu.VMEM((4, SHARE, HALF), BF16),
        pltpu.VMEM((SHARE, HALF), BF16),
        pltpu.VMEM((2, SHARE, HALF), BF16),
        pltpu.VMEM((SHARE, D), F32),
        pltpu.VMEM((8, SHARE, HALF), BF16),
        pltpu.VMEM((8, SHARE, HALF), BF16),
        pltpu.VMEM((TOK, WIDTH), F32),
        pltpu.VMEM((TOK, WIDTH), BF16),
        pltpu.VMEM((5, 2 * NLEN, WIDTH), BF16),
        pltpu.VMEM((5, 2 * NLEN, WIDTH), BF16),
    ]
    counts = (10, 4, 4, 4, 4, 8, 8, 4, 4, 4, 4, 17, 17, 15, 15, 17, 17, 15, 15, 2, 2)
    scratch += [pltpu.SemaphoreType.DMA((count,)) for count in counts]
    return pl.pallas_call(
        block_kernel,
        out_shape=jax.ShapeDtypeStruct((SHARE, D), F32),
        in_specs=[vmem] * 3 + [hbm] * 10,
        out_specs=vmem,
        scratch_shapes=scratch,
        compiler_params=pltpu.CompilerParams(
            collective_id=0, has_side_effects=True, vmem_limit_bytes=56 << 20
        ),
        name="retro_block",
    )(
        query_rows,
        key_rows,
        value_rows,
        norm_gain,
        nb_shard.T,
        nb_row.T,
        hidden_in,
        w_self_out,
        w_cross_q,
        w_cross_k,
        w_cross_v,
        w_cross_out,
        enc_table,
    )


def solution(mesh):
    placed = (
        P("seq", None),
        P("seq", "db"),
        P("seq", "db"),
        P("seq", "db"),
        P("db", None),
        P(),
        P(None, "db"),
        P(None, "db"),
        P(None, "db"),
        P("db", None),
        P("db", None, None),
        P("seq", None),
        P("seq", None),
    )
    return jax.shard_map(
        per_device, mesh=mesh, in_specs=placed, out_specs=P(("seq", "db"), None), check_vma=False
    )
```

```python
import math

import jax
import jax.numpy as jnp
from jax import lax
from jax.experimental import pallas as pl
from jax.experimental.pallas import tpu as pltpu
from jax.sharding import PartitionSpec as P

HD = 128
SPAN = 64
NLEN = 128
TOK = 256
WIDTH = 512
D = 4096
SHARE = 32
HALF = 2048
NEG_BIG = -1e30
MESH = pl.DeviceIdType.MESH
EXP2_SCALE = math.log2(math.e) / math.sqrt(HD)
BF16 = jnp.bfloat16
F32 = jnp.float32


def remote(src, dst, send, recv, seq, db):
    return pltpu.make_async_remote_copy(
        src_ref=src, dst_ref=dst, send_sem=send, recv_sem=recv, device_id=(seq, db), device_id_type=MESH
    )


def dot_f32(a, b):
    return jnp.dot(a, b, preferred_element_type=F32)


def dot_nt(a, b):
    return lax.dot_general(a, b, (((1,), (1,)), ((), ())), preferred_element_type=F32)


def block_kernel(
    q_ref,
    k_ref,
    v_ref,
    gain_hbm,
    shard_hbm,
    row_hbm,
    hidden_hbm,
    wso_hbm,
    wcq_hbm,
    wck_hbm,
    wcv_hbm,
    wco_hbm,
    enc_hbm,
    out_ref,
    gain,
    shard_ref,
    row_ref,
    wso,
    wcq,
    wck,
    wcv,
    wco,
    enc,
    hid,
    kvs,
    qst,
    kv,
    qb,
    ob,
    ret,
    sc_buf,
    lsum,
    acc,
    att,
    arr,
    part_a,
    part_b,
    za1,
    ya1,
    yb1,
    zb1,
    za2,
    ya2,
    yb2,
    zb2,
    sum_a,
    sum_b,
    sum_y,
    res,
    nf_a,
    nf_b,
    cqa,
    qx,
    kx,
    vx,
    wsem,
    xs,
    xr,
    zs,
    zr,
    cs,
    cr,
    qs,
    qr,
    os_,
    or_,
    es,
    er,
    r1s,
    r1r,
    ags,
    agr,
    r2s,
    r2r,
    ps,
    pr,
    tab,
    shard_two,
    row_two,
    lent,
    ts,
    tr,
):
    s = lax.axis_index("seq")
    d = lax.axis_index("db")
    c = s % 2
    x = (s // 2) % 4
    zl = s // 8
    y = d // 2
    zh = d % 2
    over = 2 * y + 1 - zh
    beside = (s + 8) % 16
    far = (2, 1, 3)

    def at(zz, xx, cc):
        return (zz * 4 + xx) * 2 + cc

    own_rows = pl.ds(pl.multiple_of(d * SHARE, SHARE), SHARE)

    bar = pltpu.get_barrier_semaphore()
    for step in range(1, 16):
        pl.semaphore_signal(bar, inc=1, device_id=((s + step) % 16, d), device_id_type=MESH)
    for step in range(1, 8):
        pl.semaphore_signal(bar, inc=1, device_id=(s, (d + step) % 8), device_id_type=MESH)

    loads = [
        pltpu.make_async_copy(enc_hbm, enc, wsem.at[0]),
        pltpu.make_async_copy(wso_hbm, wso, wsem.at[1]),
        pltpu.make_async_copy(hidden_hbm.at[own_rows], hid, wsem.at[2]),
        pltpu.make_async_copy(wck_hbm, wck, wsem.at[3]),
        pltpu.make_async_copy(wcv_hbm, wcv, wsem.at[4]),
        pltpu.make_async_copy(wcq_hbm, wcq, wsem.at[5]),
        pltpu.make_async_copy(wco_hbm, wco, wsem.at[6]),
        pltpu.make_async_copy(shard_hbm, shard_ref, wsem.at[7]),
        pltpu.make_async_copy(row_hbm, row_ref, wsem.at[8]),
        pltpu.make_async_copy(gain_hbm, gain, wsem.at[9]),
    ]
    for k in (0, 7, 8):
        loads[k].start()
    for h in range(4):
        cols = slice(h * HD, (h + 1) * HD)
        kvs[h, 0] = k_ref[:, cols]
        kvs[h, 1] = v_ref[:, cols]
        qst[h] = q_ref[:, cols]
    pl.semaphore_signal(bar, inc=1, device_id=(beside, over), device_id_type=MESH)
    pl.semaphore_wait(bar, 23)

    sends = []

    def start(copy):
        copy.start()
        sends.append(copy)

    for dx in (1, 3, 2):
        other = (x + dx) % 4
        start(remote(kvs.at[other], kv.at[s], xs.at[dx], xr.at[dx], at(zl, other, c), d))
    kv[s] = kvs[x]
    def forward(src, k):
        start(remote(kv.at[src], kv.at[src], zs.at[k], zr.at[k], at(1 - zl, x, c), d))
        start(remote(kv.at[src], kv.at[src], cs.at[k], cr.at[k], at(zl, x, 1 - c), d))

    forward(s, 0)
    start(remote(shard_hbm, tab.at[0], ts.at[0], tr.at[0], beside, d))
    start(remote(row_hbm, tab.at[1], ts.at[1], tr.at[1], beside, d))

    low = s % 8
    high = low // 4
    j_to = (1 - high) * low + high * (7 - low)
    slot_to = (s // 8) * 2 + high
    for h in range(4):
        goal = at(j_to // 2, h, j_to % 2)

        @pl.when(goal != s)
        def _():
            remote(qst.at[h], qb.at[slot_to], qs.at[h], qr.at[slot_to], goal, d).start()

        @pl.when(goal == s)
        def _():
            pltpu.make_async_copy(qst.at[h], qb.at[slot_to], qr.at[slot_to]).start()

    def share_at(step, side):
        return 2 * ((y + step + 4) % 4) + side

    def flow_copies(flow, piece, side, sems):
        send, recv = sems
        held = piece(share_at(0, side), 0)
        return [
            remote(held, held, send.at[4 * flow + k], recv.at[4 * flow + k], s, share_at(step, zh))
            for k, step in ((0, 1), (1, -1))
        ]

    def flow_send(flow, piece, side, sems):
        for copy in flow_copies(flow, piece, side, sems):
            start(copy)

    def flow_forward(flow, piece, side, sems, then=None):
        send, recv = sems
        for k, step in ((0, 1), (1, -1)):
            came = share_at(-step, side)
            held = piece(came, 0)
            remote(held, held, send.at[4 * flow + k], recv.at[4 * flow + k], s, d).wait_recv()
            part = piece(came, 1 + k)
            k2 = 4 * flow + 2 + k
            start(remote(part, part, send.at[k2], recv.at[k2], s, share_at(step, zh)))
            if then is not None:
                then(came, k)

    def flow_last(flow, piece, side, sems):
        send, recv = sems
        for k in range(2):
            part = piece(share_at(2, side), 1 + k)
            k2 = 4 * flow + 2 + k
            remote(part, part, send.at[k2], recv.at[k2], s, d).wait_recv()

    def cross_send(piece, owner, k, sems):
        send, recv = sems
        held = piece(owner, 0)
        start(remote(held, held, send.at[k], recv.at[k], s, over))

    def cross_wait(piece, owner, k, sems):
        send, recv = sems
        held = piece(owner, 0)
        remote(held, held, send.at[k], recv.at[k], s, over).wait_recv()

    def gather_b_on(piece_b, sems):
        flow_forward(2, piece_b, zh, sems, lambda came, k: cross_send(piece_b, came, 14 + k, sems))

    def gather_a_over(piece_a, sems):
        cross_wait(piece_a, over, 12, sems)
        for copy in flow_copies(1, piece_a, 1 - zh, sems):
            copy.start()

    def gather_a_sent(piece_a, sems):
        for copy in flow_copies(1, piece_a, 1 - zh, sems):
            copy.wait_send()

    def gather_last_on(piece_a, piece_b, sems):
        flow_last(2, piece_b, zh, sems)
        cross_send(piece_b, share_at(2, zh), 16, sems)
        flow_forward(1, piece_a, 1 - zh, sems)

    def gather_finish_a(piece_a, sems):
        flow_last(0, piece_a, zh, sems)
        flow_last(1, piece_a, 1 - zh, sems)

    def gather_finish_b(piece_b, sems):
        for k, step in ((13, 0), (14, -1), (15, 1), (16, 2)):
            cross_wait(piece_b, share_at(step, 1 - zh), k, sems)

    for k in (0, 7, 8):
        loads[k].wait()

    def asked(shards, rows):
        first = jnp.int32(0)
        second = jnp.int32(0)
        found = jnp.int32(0)
        for e in range(8):
            match = shards[e % 2, e // 2] == d
            row = rows[e % 2, e // 2]
            first = jnp.where(match & (found == 0), row, first)
            second = jnp.where(match & (found == 1), row, second)
            found = found + match.astype(jnp.int32)
        return first, second

    first, second = asked(shard_ref, row_ref)
    arr[d, 0:NLEN] = enc[first]
    arr[d, NLEN : 2 * NLEN] = enc[second]

    def enc_a(i, part):
        return arr.at[i, pl.ds((0, 0, 96)[part], (192, 96, 96)[part])]

    def enc_b(i, part):
        return arr.at[i, pl.ds((192, 192, 224)[part], (64, 32, 32)[part])]

    enc_sems = (es, er)
    flow_send(2, enc_b, zh, enc_sems)
    flow_send(0, enc_a, zh, enc_sems)
    for k, table in ((0, shard_two), (1, row_two)):
        remote(tab.at[k], tab.at[k], ts.at[k], tr.at[k], beside, d).wait_recv()
        pltpu.make_async_copy(tab.at[k], table, wsem.at[10 + k]).start()
    for k, table in ((0, shard_two), (1, row_two)):
        pltpu.make_async_copy(tab.at[k], table, wsem.at[10 + k]).wait()
    first, second = asked(shard_two, row_two)
    lent[0:NLEN] = enc[first]
    lent[NLEN:192] = enc[second, 0:64]
    start(remote(lent, enc_a(d, 0), es.at[12], er.at[12], beside, over))

    for dx in (1, 3, 2):
        src = at(zl, (x - dx + 4) % 4, c)
        remote(kv.at[src], kv.at[src], xs.at[dx], xr.at[dx], src, d).wait_recv()
        forward(src, dx)
    cross_send(enc_b, d, 13, enc_sems)
    for dx in (0, 1, 3, 2):
        src = at(1 - zl, (x - dx + 4) % 4, c)
        remote(kv.at[src], kv.at[src], zs.at[dx], zr.at[dx], src, d).wait_recv()
        start(remote(kv.at[src], kv.at[src], cs.at[4 + dx], cr.at[4 + dx], at(zl, x, 1 - c), d))
    for zz in range(2):
        for dx in range(4):
            src = at((zl + zz) % 2, (x - dx + 4) % 4, 1 - c)
            k = 4 * zz + dx
            remote(kv.at[src], kv.at[src], cs.at[k], cr.at[k], src, d).wait_recv()

    gather_a_over(enc_a, enc_sems)
    gather_b_on(enc_b, enc_sems)
    flow_forward(0, enc_a, zh, enc_sems)

    for k in (1, 2, 3, 4, 5, 6, 9):
        loads[k].start()

    j = zl * 2 + c

    def block_of(i):
        return (i // 2) * 8 + (i % 2) * (7 - j) + (1 - i % 2) * j

    def slot(i, carry):
        b = block_of(i)


        remote(qst.at[0], qb.at[i], qs.at[0], qr.at[i], s, d).wait_recv()
        query = qb[i]
        last = (b + 2) // 2 - 1

        def lanes_max(scores):
            return jnp.maximum(
                jnp.maximum(scores[:, 0:128], scores[:, 128:256]),
                jnp.maximum(scores[:, 256:384], scores[:, 384:512]),
            )

        def first_pass(kb, top):
            keys = kv[pl.ds(2 * kb, 2), 0].reshape(512, HD)
            scores = dot_nt(query, keys)
            sc_buf[kb] = scores
            return jnp.maximum(top, lanes_max(scores))

        top = lax.fori_loop(0, last, first_pass, jnp.full((TOK, 128), NEG_BIG, F32))
        keys = kv[pl.ds(2 * last, 2), 0].reshape(512, HD)
        scores = dot_nt(query, keys)
        key_pos = last * 512 + lax.broadcasted_iota(jnp.int32, (TOK, 512), 1)
        query_pos = b * TOK + lax.broadcasted_iota(jnp.int32, (TOK, 512), 0)
        scores = jnp.where(key_pos <= query_pos, scores, NEG_BIG)
        sc_buf[last] = scores
        top = jnp.max(jnp.maximum(top, lanes_max(scores)), axis=-1, keepdims=True)
        lsum[...] = jnp.zeros_like(lsum)
        acc[...] = jnp.zeros_like(acc)

        def second_pass(kb, carry):
            weights = jnp.exp2((sc_buf[kb] - top) * EXP2_SCALE)
            values = kv[pl.ds(2 * kb, 2), 1].reshape(512, HD)
            lsum[...] += (weights[:, 0:128] + weights[:, 128:256]) + (
                weights[:, 256:384] + weights[:, 384:512]
            )
            acc[...] += dot_f32(weights.astype(BF16), values)
            return carry

        lax.fori_loop(0, last + 1, second_pass, 0)
        total = jnp.sum(lsum[...], axis=-1, keepdims=True)
        ob[i] = (acc[...] / total).astype(BF16)

        @pl.when(b != s)
        def _():
            remote(ob.at[i], ret.at[x], os_.at[i], or_.at[x], b, d).start()

        @pl.when(b == s)
        def _():
            pltpu.make_async_copy(ob.at[i], ret.at[x], or_.at[x]).start()

        return carry

    lax.fori_loop(0, 4, slot, 0)
    for h in range(4):
        remote(ob.at[0], ret.at[h], os_.at[0], or_.at[h], s, d).wait_recv()
        att[:, h * HD : (h + 1) * HD] = ret[h]

    def project_a(lhs, weight):
        def tile(n, carry):
            cols = pl.ds(pl.multiple_of(n * 512, 512), 512)
            product = dot_f32(lhs, weight[:, cols]).astype(BF16)
            for share in range(8):
                part_a[(share % 2) * 4 + share // 2, :, cols] = product[
                    share * SHARE : (share + 1) * SHARE
                ]
            return carry

        lax.fori_loop(0, 4, tile, 0)

    def project_b(lhs, weight):
        def tile(n, carry):
            cols = pl.ds(pl.multiple_of(n * 512, 512), 512)
            right = pl.ds(pl.multiple_of(HALF + n * 512, 512), 512)
            product = dot_f32(lhs, weight[:, right]).astype(BF16)
            part_b[:, :, cols] = product.reshape(8, SHARE, 512)
            return carry

        lax.fori_loop(0, 4, tile, 0)

    spread = []

    def go(copy):
        copy.start()
        spread.append(copy)

    def scatter(lhs, weight, send, recv, za, ya, yb, zb):
        project_a(lhs, weight)
        for dy in (2, 1, 3, 0):
            yy = (y + dy) % 4
            go(remote(part_a.at[(1 - zh) * 4 + yy], za.at[yy], send.at[dy], recv.at[dy], s, over))
        project_b(lhs, weight)
        steps = ((0, 1), (1, -1))
        for k, step in steps:
            go(
                remote(
                    part_b.at[share_at(2, k)],
                    yb.at[k],
                    send.at[4 + k],
                    recv.at[4 + k],
                    s,
                    share_at(step, zh),
                )
            )
        for k, step in steps:
            go(
                remote(
                    part_b.at[share_at(step, 1 - k)],
                    yb.at[4 + k],
                    send.at[12 + k],
                    recv.at[12 + k],
                    s,
                    share_at(step, zh),
                )
            )
        for k, step in steps:
            remote(yb.at[k], yb.at[k], send.at[4 + k], recv.at[4 + k], s, d).wait_recv()
            sum_y[k] = (part_b[share_at(step, k)].astype(F32) + yb[k].astype(F32)).astype(BF16)
            go(
                remote(
                    sum_y.at[k], yb.at[2 + k], send.at[6 + k], recv.at[6 + k], s, share_at(step, zh)
                )
            )
        for dy in far:
            yy = (y + dy) % 4
            remote(za.at[yy], za.at[yy], send.at[dy], recv.at[dy], s, over).wait_recv()
            sum_a[dy] = (part_a[zh * 4 + yy].astype(F32) + za[yy].astype(F32)).astype(BF16)
            go(
                remote(
                    sum_a.at[dy], ya.at[dy], send.at[8 + dy], recv.at[8 + dy], s, 2 * yy + zh
                )
            )
        for k in range(2):
            remote(yb.at[2 + k], yb.at[2 + k], send.at[6 + k], recv.at[6 + k], s, d).wait_recv()
            remote(yb.at[4 + k], yb.at[4 + k], send.at[12 + k], recv.at[12 + k], s, d).wait_recv()
        sum_b[...] = b_share(over, 1 - zh, slice(None), yb).astype(BF16)
        go(remote(sum_b, zb, send.at[14], recv.at[14], s, over))

    def b_share(share, k, cols, yb):
        return (
            part_b[share, :, cols].astype(F32)
            + yb[2 + k, :, cols].astype(F32)
            + yb[5 - k, :, cols].astype(F32)
        )

    def scatter_wait(send, recv, za, ya, zb):
        remote(za.at[0], za.at[y], send.at[0], recv.at[0], s, over).wait_recv()
        for dy in far:
            remote(ya.at[dy], ya.at[dy], send.at[8 + dy], recv.at[8 + dy], s, d).wait_recv()
        remote(zb, zb, send.at[14], recv.at[14], s, over).wait_recv()

    def total_of(half, cols, za, ya, yb, zb):
        if half == 0:
            total = part_a[zh * 4 + y, :, cols].astype(F32) + za[y, :, cols].astype(F32)
            for dy in range(1, 4):
                total = total + ya[dy, :, cols].astype(F32)
        else:
            total = b_share(d, zh, cols, yb) + zb[:, cols].astype(F32)
        return total

    loads[1].wait()
    scatter(att[...], wso, r1s, r1r, za1, ya1, yb1, zb1)
    gather_last_on(enc_a, enc_b, enc_sems)

    loads[2].wait()
    loads[9].wait()
    scatter_wait(r1s, r1r, za1, ya1, zb1)

    def add_up(n, square):
        cols = pl.ds(pl.multiple_of(n * 512, 512), 512)
        for half in range(2):
            wide = pl.ds(pl.multiple_of(half * HALF + n * 512, 512), 512)
            total = total_of(half, cols, za1, ya1, yb1, zb1) + hid[:, wide].astype(F32)
            res[:, wide] = total
            square = square + total * total
        return square

    square = lax.fori_loop(0, 4, add_up, jnp.zeros((SHARE, 512), F32))
    scale = lax.rsqrt(jnp.sum(square, axis=-1, keepdims=True) / D + 1e-05)

    def normalise(n, carry):
        cols = pl.ds(pl.multiple_of(n * 512, 512), 512)
        for half, held in enumerate((nf_a, nf_b)):
            wide = pl.ds(pl.multiple_of(half * HALF + n * 512, 512), 512)
            held[d, :, cols] = (
                res[:, wide] * scale * gain[wide].astype(F32)
            ).astype(BF16)
        return carry

    lax.fori_loop(0, 4, normalise, 0)

    def share_a(i, part):
        return nf_a.at[i, pl.ds((0, 0, 16)[part], (32, 16, 16)[part])]

    def share_b(i, part):
        return nf_b.at[i, pl.ds((0, 0, 16)[part], (32, 16, 16)[part])]

    ag_sems = (ags, agr)
    cross_send(share_a, d, 12, ag_sems)
    flow_send(2, share_b, zh, ag_sems)
    flow_send(0, share_a, zh, ag_sems)
    cross_send(share_b, d, 13, ag_sems)

    gather_finish_a(enc_a, enc_sems)
    gather_finish_b(enc_b, enc_sems)
    loads[3].wait()
    loads[4].wait()

    def cross_pair(e):
        shard = shard_ref[e % 2, e // 2]
        rank = jnp.int32(0)
        for earlier in range(e):
            rank = rank + (shard_ref[earlier % 2, earlier // 2] == shard).astype(jnp.int32)
        entry = arr.reshape(16, NLEN, 1024)[shard * 2 + jnp.minimum(rank, 1)]
        rows = slice((e % 2) * NLEN, (e % 2 + 1) * NLEN)
        kx[e // 2 + 1, rows, :] = dot_f32(entry, wck[...]).astype(BF16)
        vx[e // 2 + 1, rows, :] = dot_f32(entry, wcv[...]).astype(BF16)

    cross_pair(6)
    cross_pair(7)

    @pl.when(s < 15)
    def _():
        remote(kx.at[4], kx.at[0], ps.at[0], pr.at[0], s + 1, d).start()
        remote(vx.at[4], vx.at[0], ps.at[1], pr.at[1], s + 1, d).start()

    @pl.when(s == 0)
    def _():
        kx[0] = jnp.zeros((2 * NLEN, WIDTH), BF16)
        vx[0] = jnp.zeros((2 * NLEN, WIDTH), BF16)

    gather_a_over(share_a, ag_sems)
    gather_b_on(share_b, ag_sems)
    flow_forward(0, share_a, zh, ag_sems)
    for e in range(4):
        cross_pair(e)
    gather_last_on(share_a, share_b, ag_sems)
    for e in range(4, 6):
        cross_pair(e)
    for copy in spread:
        copy.wait_send()
    spread.clear()
    loads[5].wait()
    gather_finish_a(share_a, ag_sems)

    cqa[...] = jnp.zeros_like(cqa)

    def contract_a(n, carry):
        cols = pl.ds(pl.multiple_of(n * 512, 512), 512)
        cqa[...] += dot_f32(nf_a[:, :, cols].reshape(TOK, 512), wcq[cols, :])
        return carry

    def contract_b(n, carry):
        cols = pl.ds(pl.multiple_of(n * 512, 512), 512)
        right = pl.ds(pl.multiple_of(HALF + n * 512, 512), 512)
        cqa[...] += dot_f32(nf_b[:, :, cols].reshape(TOK, 512), wcq[right, :])
        return carry

    lax.fori_loop(0, 4, contract_a, 0)
    gather_finish_b(share_b, ag_sems)
    lax.fori_loop(0, 4, contract_b, 0)
    qx[...] = pltpu.roll(cqa[...].astype(BF16).astype(F32), 1, 0).astype(BF16)

    @pl.when(s > 0)
    def _():
        remote(kx.at[4], kx.at[0], ps.at[0], pr.at[0], s, d).wait_recv()
        remote(vx.at[4], vx.at[0], ps.at[1], pr.at[1], s, d).wait_recv()

    def attend(query, keys, values):
        scores = dot_nt(query, keys)
        top = jnp.max(scores, axis=-1, keepdims=True)
        weights = jnp.exp2((scores - top) * EXP2_SCALE)
        total = jnp.sum(weights, axis=-1, keepdims=True)
        return dot_f32(weights.astype(BF16), values) / total

    def group(g, carry):
        rows = pl.ds(pl.multiple_of(g * SPAN, SPAN), SPAN)
        for h in range(4):
            cols = slice(h * HD, (h + 1) * HD)
            cqa[rows, cols] = attend(qx[rows, cols], kx[g, :, cols], vx[g, :, cols])
        return carry

    lax.fori_loop(0, 4, group, 0, unroll=True)
    for h in range(4):
        cols = slice(h * HD, (h + 1) * HD)
        tail = attend(qx[0:16, cols], kx[4, :, cols], vx[4, :, cols])
        first_row = lax.broadcasted_iota(jnp.int32, (16, HD), 0) == 0
        cqa[0:16, cols] = jnp.where(first_row, tail, cqa[0:16, cols])
    att[...] = pltpu.roll(cqa[...], TOK - 1, 0).astype(BF16)

    loads[6].wait()
    scatter(att[...], wco, r2s, r2r, za2, ya2, yb2, zb2)
    scatter_wait(r2s, r2r, za2, ya2, zb2)

    def finish(n, carry):
        cols = pl.ds(pl.multiple_of(n * 512, 512), 512)
        for half in range(2):
            wide = pl.ds(pl.multiple_of(half * HALF + n * 512, 512), 512)
            out_ref[:, wide] = res[:, wide] + total_of(half, cols, za2, ya2, yb2, zb2)
        return carry

    lax.fori_loop(0, 4, finish, 0)

    for copy in spread:
        copy.wait_send()
    for copy in sends:
        copy.wait_send()
    gather_a_sent(enc_a, enc_sems)
    gather_a_sent(share_a, ag_sems)
    for h in range(4):
        goal = at(j_to // 2, h, j_to % 2)

        @pl.when(goal != s)
        def _():
            remote(qst.at[h], qb.at[0], qs.at[h], qr.at[0], goal, d).wait_send()

    for i in range(4):

        @pl.when(block_of(i) != s)
        def _():
            remote(ob.at[i], ret.at[0], os_.at[i], or_.at[0], s, d).wait_send()

    @pl.when(s < 15)
    def _():
        remote(kx.at[4], kx.at[0], ps.at[0], pr.at[0], s, d).wait_send()
        remote(vx.at[4], vx.at[0], ps.at[1], pr.at[1], s, d).wait_send()


def per_device(
    hidden_in,
    query_rows,
    key_rows,
    value_rows,
    w_self_out,
    norm_gain,
    w_cross_q,
    w_cross_k,
    w_cross_v,
    w_cross_out,
    enc_table,
    nb_shard,
    nb_row,
):
    vmem = pl.BlockSpec(memory_space=pltpu.VMEM)
    hbm = pl.BlockSpec(memory_space=pl.ANY)
    scratch = [
        pltpu.VMEM((D,), BF16),
        pltpu.SMEM((2, 4), jnp.int32),
        pltpu.SMEM((2, 4), jnp.int32),
        pltpu.VMEM((WIDTH, D), BF16),
        pltpu.VMEM((D, WIDTH), BF16),
        pltpu.VMEM((1024, WIDTH), BF16),
        pltpu.VMEM((1024, WIDTH), BF16),
        pltpu.VMEM((WIDTH, D), BF16),
        pltpu.VMEM((8, NLEN, 1024), BF16),
        pltpu.VMEM((SHARE, D), BF16),
        pltpu.VMEM((4, 2, TOK, HD), BF16),
        pltpu.VMEM((4, TOK, HD), BF16),
        pltpu.VMEM((16, 2, TOK, HD), BF16),
        pltpu.VMEM((4, TOK, HD), BF16),
        pltpu.VMEM((4, TOK, HD), BF16),
        pltpu.VMEM((4, TOK, HD), BF16),
        pltpu.VMEM((8, TOK, 512), F32),
        pltpu.VMEM((TOK, HD), F32),
        pltpu.VMEM((TOK, HD), F32),
        pltpu.VMEM((TOK, WIDTH), BF16),
        pltpu.VMEM((8, 2 * NLEN, 1024), BF16),
        pltpu.VMEM((8, SHARE, HALF), BF16),
        pltpu.VMEM((8, SHARE, HALF), BF16),
    ]
    scratch += [
        pltpu.VMEM((4, SHARE, HALF), BF16),
        pltpu.VMEM((4, SHARE, HALF), BF16),
        pltpu.VMEM((6, SHARE, HALF), BF16),
        pltpu.VMEM((SHARE, HALF), BF16),
    ] * 2
    scratch += [
        pltpu.VMEM((4, SHARE, HALF), BF16),
        pltpu.VMEM((SHARE, HALF), BF16),
        pltpu.VMEM((2, SHARE, HALF), BF16),
        pltpu.VMEM((SHARE, D), F32),
        pltpu.VMEM((8, SHARE, HALF), BF16),
        pltpu.VMEM((8, SHARE, HALF), BF16),
        pltpu.VMEM((TOK, WIDTH), F32),
        pltpu.VMEM((TOK, WIDTH), BF16),
        pltpu.VMEM((5, 2 * NLEN, WIDTH), BF16),
        pltpu.VMEM((5, 2 * NLEN, WIDTH), BF16),
    ]
    counts = (12, 4, 4, 4, 4, 8, 8, 4, 4, 4, 4, 17, 17, 15, 15, 17, 17, 15, 15, 2, 2)
    scratch += [pltpu.SemaphoreType.DMA((count,)) for count in counts]
    scratch += [
        pltpu.VMEM((2, 2, 4), jnp.int32),
        pltpu.SMEM((2, 4), jnp.int32),
        pltpu.SMEM((2, 4), jnp.int32),
        pltpu.VMEM((192, 1024), BF16),
        pltpu.SemaphoreType.DMA((2,)),
        pltpu.SemaphoreType.DMA((2,)),
    ]
    return pl.pallas_call(
        block_kernel,
        out_shape=jax.ShapeDtypeStruct((SHARE, D), F32),
        in_specs=[vmem] * 3 + [hbm] * 10,
        out_specs=vmem,
        scratch_shapes=scratch,
        compiler_params=pltpu.CompilerParams(
            collective_id=0, has_side_effects=True, vmem_limit_bytes=56 << 20
        ),
        name="retro_block",
    )(
        query_rows,
        key_rows,
        value_rows,
        norm_gain,
        nb_shard.T,
        nb_row.T,
        hidden_in,
        w_self_out,
        w_cross_q,
        w_cross_k,
        w_cross_v,
        w_cross_out,
        enc_table,
    )


def solution(mesh):
    placed = (
        P("seq", None),
        P("seq", "db"),
        P("seq", "db"),
        P("seq", "db"),
        P("db", None),
        P(),
        P(None, "db"),
        P(None, "db"),
        P(None, "db"),
        P("db", None),
        P("db", None, None),
        P("seq", None),
        P("seq", None),
    )
    return jax.shard_map(
        per_device, mesh=mesh, in_specs=placed, out_specs=P(("seq", "db"), None), check_vma=False
    )
```

```python
import math

import jax
import jax.numpy as jnp
from jax import lax
from jax.experimental import pallas as pl
from jax.experimental.pallas import tpu as pltpu
from jax.sharding import PartitionSpec as P

HD = 128
SPAN = 64
NLEN = 128
TOK = 256
WIDTH = 512
D = 4096
SHARE = 32
HALF = 2048
NEG_BIG = -1e30
MESH = pl.DeviceIdType.MESH
EXP2_SCALE = math.log2(math.e) / math.sqrt(HD)
BF16 = jnp.bfloat16
F32 = jnp.float32


def remote(src, dst, send, recv, seq, db):
    return pltpu.make_async_remote_copy(
        src_ref=src, dst_ref=dst, send_sem=send, recv_sem=recv, device_id=(seq, db), device_id_type=MESH
    )


def dot_f32(a, b):
    return jnp.dot(a, b, preferred_element_type=F32)


def dot_nt(a, b):
    return lax.dot_general(a, b, (((1,), (1,)), ((), ())), preferred_element_type=F32)


def block_kernel(
    q_ref,
    k_ref,
    v_ref,
    gain_hbm,
    shard_hbm,
    row_hbm,
    hidden_hbm,
    wso_hbm,
    wcq_hbm,
    wck_hbm,
    wcv_hbm,
    wco_hbm,
    enc_hbm,
    out_ref,
    gain,
    shard_ref,
    row_ref,
    wso,
    wcq,
    wck,
    wcv,
    wco,
    enc,
    hid,
    kvs,
    qst,
    kv,
    qb,
    ob,
    ret,
    sc_buf,
    lsum,
    acc,
    att,
    arr,
    part_a,
    part_b,
    za1,
    ya1,
    yb1,
    zb1,
    za2,
    ya2,
    yb2,
    zb2,
    sum_a,
    sum_b,
    sum_y,
    res,
    nf_a,
    nf_b,
    cqa,
    qx,
    kx,
    vx,
    wsem,
    xs,
    xr,
    zs,
    zr,
    cs,
    cr,
    qs,
    qr,
    os_,
    or_,
    es,
    er,
    r1s,
    r1r,
    ags,
    agr,
    r2s,
    r2r,
    ps,
    pr,
    tab,
    shard_two,
    row_two,
    lent,
    ts,
    tr,
):
    s = lax.axis_index("seq")
    d = lax.axis_index("db")
    c = s % 2
    x = (s // 2) % 4
    zl = s // 8
    y = d // 2
    zh = d % 2
    over = 2 * y + 1 - zh
    beside = (s + 8) % 16
    far = (2, 1, 3)

    def at(zz, xx, cc):
        return (zz * 4 + xx) * 2 + cc

    own_rows = pl.ds(pl.multiple_of(d * SHARE, SHARE), SHARE)

    bar = pltpu.get_barrier_semaphore()
    for step in range(1, 16):
        pl.semaphore_signal(bar, inc=1, device_id=((s + step) % 16, d), device_id_type=MESH)
    for step in range(1, 8):
        pl.semaphore_signal(bar, inc=1, device_id=(s, (d + step) % 8), device_id_type=MESH)

    loads = [
        pltpu.make_async_copy(enc_hbm, enc, wsem.at[0]),
        pltpu.make_async_copy(wso_hbm, wso, wsem.at[1]),
        pltpu.make_async_copy(hidden_hbm.at[own_rows], hid, wsem.at[2]),
        pltpu.make_async_copy(wck_hbm, wck, wsem.at[3]),
        pltpu.make_async_copy(wcv_hbm, wcv, wsem.at[4]),
        pltpu.make_async_copy(wcq_hbm, wcq, wsem.at[5]),
        pltpu.make_async_copy(wco_hbm, wco, wsem.at[6]),
        pltpu.make_async_copy(shard_hbm, shard_ref, wsem.at[7]),
        pltpu.make_async_copy(row_hbm, row_ref, wsem.at[8]),
        pltpu.make_async_copy(gain_hbm, gain, wsem.at[9]),
    ]
    for k in (0, 7, 8):
        loads[k].start()
    for h in range(4):
        cols = slice(h * HD, (h + 1) * HD)
        kvs[h, 0] = k_ref[:, cols]
        kvs[h, 1] = v_ref[:, cols]
        qst[h] = q_ref[:, cols]
    pl.semaphore_signal(bar, inc=1, device_id=(beside, over), device_id_type=MESH)
    pl.semaphore_wait(bar, 23)

    sends = []

    def start(copy):
        copy.start()
        sends.append(copy)

    for dx in (1, 3, 2):
        other = (x + dx) % 4
        start(remote(kvs.at[other], kv.at[s], xs.at[dx], xr.at[dx], at(zl, other, c), d))
    kv[s] = kvs[x]
    def forward(src, k):
        start(remote(kv.at[src], kv.at[src], zs.at[k], zr.at[k], at(1 - zl, x, c), d))
        start(remote(kv.at[src], kv.at[src], cs.at[k], cr.at[k], at(zl, x, 1 - c), d))

    forward(s, 0)
    start(remote(shard_hbm, tab.at[0], ts.at[0], tr.at[0], beside, d))
    start(remote(row_hbm, tab.at[1], ts.at[1], tr.at[1], beside, d))

    low = s % 8
    high = low // 4
    j_to = (1 - high) * low + high * (7 - low)
    slot_to = (s // 8) * 2 + high
    for h in range(4):
        goal = at(j_to // 2, h, j_to % 2)

        @pl.when(goal != s)
        def _():
            remote(qst.at[h], qb.at[slot_to], qs.at[h], qr.at[slot_to], goal, d).start()

        @pl.when(goal == s)
        def _():
            pltpu.make_async_copy(qst.at[h], qb.at[slot_to], qr.at[slot_to]).start()

    def share_at(step, side):
        return 2 * ((y + step + 4) % 4) + side

    def flow_copies(flow, piece, side, sems):
        send, recv = sems
        held = piece(share_at(0, side), 0)
        return [
            remote(held, held, send.at[4 * flow + k], recv.at[4 * flow + k], s, share_at(step, zh))
            for k, step in ((0, 1), (1, -1))
        ]

    def flow_send(flow, piece, side, sems):
        for copy in flow_copies(flow, piece, side, sems):
            start(copy)

    def flow_forward(flow, piece, side, sems, then=None):
        send, recv = sems
        for k, step in ((0, 1), (1, -1)):
            came = share_at(-step, side)
            held = piece(came, 0)
            remote(held, held, send.at[4 * flow + k], recv.at[4 * flow + k], s, d).wait_recv()
            part = piece(came, 1 + k)
            k2 = 4 * flow + 2 + k
            start(remote(part, part, send.at[k2], recv.at[k2], s, share_at(step, zh)))
            if then is not None:
                then(came, k)

    def flow_last(flow, piece, side, sems):
        send, recv = sems
        for k in range(2):
            part = piece(share_at(2, side), 1 + k)
            k2 = 4 * flow + 2 + k
            remote(part, part, send.at[k2], recv.at[k2], s, d).wait_recv()

    def cross_send(piece, owner, k, sems):
        send, recv = sems
        held = piece(owner, 0)
        start(remote(held, held, send.at[k], recv.at[k], s, over))

    def cross_wait(piece, owner, k, sems):
        send, recv = sems
        held = piece(owner, 0)
        remote(held, held, send.at[k], recv.at[k], s, over).wait_recv()

    def gather_b_on(piece_b, sems):
        flow_forward(2, piece_b, zh, sems, lambda came, k: cross_send(piece_b, came, 14 + k, sems))

    def gather_a_over(piece_a, sems):
        cross_wait(piece_a, over, 12, sems)
        for copy in flow_copies(1, piece_a, 1 - zh, sems):
            copy.start()

    def gather_a_sent(piece_a, sems):
        for copy in flow_copies(1, piece_a, 1 - zh, sems):
            copy.wait_send()

    def gather_last_on(piece_a, piece_b, sems):
        flow_last(2, piece_b, zh, sems)
        cross_send(piece_b, share_at(2, zh), 16, sems)
        flow_forward(1, piece_a, 1 - zh, sems)

    def gather_finish_a(piece_a, sems):
        flow_last(0, piece_a, zh, sems)
        flow_last(1, piece_a, 1 - zh, sems)

    def gather_finish_b(piece_b, sems):
        for k, step in ((13, 0), (14, -1), (15, 1), (16, 2)):
            cross_wait(piece_b, share_at(step, 1 - zh), k, sems)

    for k in (0, 7, 8):
        loads[k].wait()

    def asked(shards, rows):
        first = jnp.int32(0)
        second = jnp.int32(0)
        found = jnp.int32(0)
        for e in range(8):
            match = shards[e % 2, e // 2] == d
            row = rows[e % 2, e // 2]
            first = jnp.where(match & (found == 0), row, first)
            second = jnp.where(match & (found == 1), row, second)
            found = found + match.astype(jnp.int32)
        return first, second

    first, second = asked(shard_ref, row_ref)
    arr[d, 0:NLEN] = enc[first]
    arr[d, NLEN : 2 * NLEN] = enc[second]

    def enc_a(i, part):
        return arr.at[i, pl.ds((0, 0, 96)[part], (192, 96, 96)[part])]

    def enc_b(i, part):
        return arr.at[i, pl.ds((192, 192, 224)[part], (64, 32, 32)[part])]

    enc_sems = (es, er)
    flow_send(2, enc_b, zh, enc_sems)
    flow_send(0, enc_a, zh, enc_sems)
    for k, table in ((0, shard_two), (1, row_two)):
        remote(tab.at[k], tab.at[k], ts.at[k], tr.at[k], beside, d).wait_recv()
        pltpu.make_async_copy(tab.at[k], table, wsem.at[10 + k]).start()
    for k, table in ((0, shard_two), (1, row_two)):
        pltpu.make_async_copy(tab.at[k], table, wsem.at[10 + k]).wait()
    first, second = asked(shard_two, row_two)
    lent[0:NLEN] = enc[first]
    lent[NLEN:192] = enc[second, 0:64]
    start(remote(lent, enc_a(d, 0), es.at[12], er.at[12], beside, over))

    for dx in (1, 3, 2):
        src = at(zl, (x - dx + 4) % 4, c)
        remote(kv.at[src], kv.at[src], xs.at[dx], xr.at[dx], src, d).wait_recv()
        forward(src, dx)
    cross_send(enc_b, d, 13, enc_sems)
    for dx in (0, 1, 3, 2):
        src = at(1 - zl, (x - dx + 4) % 4, c)
        remote(kv.at[src], kv.at[src], zs.at[dx], zr.at[dx], src, d).wait_recv()
        start(remote(kv.at[src], kv.at[src], cs.at[4 + dx], cr.at[4 + dx], at(zl, x, 1 - c), d))
    for zz in range(2):
        for dx in range(4):
            src = at((zl + zz) % 2, (x - dx + 4) % 4, 1 - c)
            k = 4 * zz + dx
            remote(kv.at[src], kv.at[src], cs.at[k], cr.at[k], src, d).wait_recv()

    gather_a_over(enc_a, enc_sems)
    gather_b_on(enc_b, enc_sems)
    flow_forward(0, enc_a, zh, enc_sems)

    for k in (1, 2, 3, 4, 5, 6, 9):
        loads[k].start()

    j = zl * 2 + c

    def block_of(i):
        return (i // 2) * 8 + (i % 2) * (7 - j) + (1 - i % 2) * j

    def slot(i, carry):
        b = block_of(i)


        remote(qst.at[0], qb.at[i], qs.at[0], qr.at[i], s, d).wait_recv()
        query = qb[i]
        last = (b + 2) // 2 - 1

        def lanes_max(scores):
            return jnp.maximum(
                jnp.maximum(scores[:, 0:128], scores[:, 128:256]),
                jnp.maximum(scores[:, 256:384], scores[:, 384:512]),
            )

        def first_pass(kb, top):
            keys = kv[pl.ds(2 * kb, 2), 0].reshape(512, HD)
            scores = dot_nt(query, keys)
            sc_buf[kb] = scores
            return jnp.maximum(top, lanes_max(scores))

        top = lax.fori_loop(0, last, first_pass, jnp.full((TOK, 128), NEG_BIG, F32))
        keys = kv[pl.ds(2 * last, 2), 0].reshape(512, HD)
        scores = dot_nt(query, keys)
        key_pos = last * 512 + lax.broadcasted_iota(jnp.int32, (TOK, 512), 1)
        query_pos = b * TOK + lax.broadcasted_iota(jnp.int32, (TOK, 512), 0)
        scores = jnp.where(key_pos <= query_pos, scores, NEG_BIG)
        sc_buf[last] = scores
        top = jnp.max(jnp.maximum(top, lanes_max(scores)), axis=-1, keepdims=True)
        lsum[...] = jnp.zeros_like(lsum)
        acc[...] = jnp.zeros_like(acc)

        def second_pass(kb, carry):
            weights = jnp.exp2((sc_buf[kb] - top) * EXP2_SCALE)
            values = kv[pl.ds(2 * kb, 2), 1].reshape(512, HD)
            lsum[...] += (weights[:, 0:128] + weights[:, 128:256]) + (
                weights[:, 256:384] + weights[:, 384:512]
            )
            acc[...] += dot_f32(weights.astype(BF16), values)
            return carry

        lax.fori_loop(0, last + 1, second_pass, 0)
        total = jnp.sum(lsum[...], axis=-1, keepdims=True)
        ob[i] = (acc[...] / total).astype(BF16)

        @pl.when(b != s)
        def _():
            remote(ob.at[i], ret.at[x], os_.at[i], or_.at[x], b, d).start()

        @pl.when(b == s)
        def _():
            pltpu.make_async_copy(ob.at[i], ret.at[x], or_.at[x]).start()

        return carry

    lax.fori_loop(0, 4, slot, 0)
    for h in range(4):
        remote(ob.at[0], ret.at[h], os_.at[0], or_.at[h], s, d).wait_recv()
        att[:, h * HD : (h + 1) * HD] = ret[h]

    def project_a(lhs, weight):
        def tile(n, carry):
            cols = pl.ds(pl.multiple_of(n * 512, 512), 512)
            product = dot_f32(lhs, weight[:, cols]).astype(BF16)
            for share in range(8):
                part_a[(share % 2) * 4 + share // 2, :, cols] = product[
                    share * SHARE : (share + 1) * SHARE
                ]
            return carry

        lax.fori_loop(0, 4, tile, 0)

    def project_b(lhs, weight):
        def tile(n, carry):
            cols = pl.ds(pl.multiple_of(n * 512, 512), 512)
            right = pl.ds(pl.multiple_of(HALF + n * 512, 512), 512)
            product = dot_f32(lhs, weight[:, right]).astype(BF16)
            part_b[:, :, cols] = product.reshape(8, SHARE, 512)
            return carry

        lax.fori_loop(0, 4, tile, 0)

    spread = []

    def go(copy):
        copy.start()
        spread.append(copy)

    def scatter(lhs, weight, send, recv, za, ya, yb, zb):
        project_b(lhs, weight)
        steps = ((0, 1), (1, -1))
        for k, step in steps:
            go(
                remote(
                    part_b.at[share_at(2, k)],
                    yb.at[k],
                    send.at[4 + k],
                    recv.at[4 + k],
                    s,
                    share_at(step, zh),
                )
            )
        for k, step in steps:
            go(
                remote(
                    part_b.at[share_at(step, 1 - k)],
                    yb.at[4 + k],
                    send.at[12 + k],
                    recv.at[12 + k],
                    s,
                    share_at(step, zh),
                )
            )
        project_a(lhs, weight)
        for dy in (2, 1, 3, 0):
            yy = (y + dy) % 4
            go(remote(part_a.at[(1 - zh) * 4 + yy], za.at[yy], send.at[dy], recv.at[dy], s, over))
        for k, step in steps:
            remote(yb.at[k], yb.at[k], send.at[4 + k], recv.at[4 + k], s, d).wait_recv()
            sum_y[k] = (part_b[share_at(step, k)].astype(F32) + yb[k].astype(F32)).astype(BF16)
            go(
                remote(
                    sum_y.at[k], yb.at[2 + k], send.at[6 + k], recv.at[6 + k], s, share_at(step, zh)
                )
            )
        for dy in far:
            yy = (y + dy) % 4
            remote(za.at[yy], za.at[yy], send.at[dy], recv.at[dy], s, over).wait_recv()
            sum_a[dy] = (part_a[zh * 4 + yy].astype(F32) + za[yy].astype(F32)).astype(BF16)
            go(
                remote(
                    sum_a.at[dy], ya.at[dy], send.at[8 + dy], recv.at[8 + dy], s, 2 * yy + zh
                )
            )
        for k in range(2):
            remote(yb.at[2 + k], yb.at[2 + k], send.at[6 + k], recv.at[6 + k], s, d).wait_recv()
            remote(yb.at[4 + k], yb.at[4 + k], send.at[12 + k], recv.at[12 + k], s, d).wait_recv()
        sum_b[...] = b_share(over, 1 - zh, slice(None), yb).astype(BF16)
        go(remote(sum_b, zb, send.at[14], recv.at[14], s, over))

    def b_share(share, k, cols, yb):
        return (
            part_b[share, :, cols].astype(F32)
            + yb[2 + k, :, cols].astype(F32)
            + yb[5 - k, :, cols].astype(F32)
        )

    def scatter_wait_a(send, recv, za, ya):
        remote(za.at[0], za.at[y], send.at[0], recv.at[0], s, over).wait_recv()
        for dy in far:
            remote(ya.at[dy], ya.at[dy], send.at[8 + dy], recv.at[8 + dy], s, d).wait_recv()

    def scatter_wait_b(send, recv, zb):
        remote(zb, zb, send.at[14], recv.at[14], s, over).wait_recv()

    def total_of(half, cols, za, ya, yb, zb):
        if half == 0:
            total = part_a[zh * 4 + y, :, cols].astype(F32) + za[y, :, cols].astype(F32)
            for dy in range(1, 4):
                total = total + ya[dy, :, cols].astype(F32)
        else:
            total = b_share(d, zh, cols, yb) + zb[:, cols].astype(F32)
        return total

    loads[1].wait()
    scatter(att[...], wso, r1s, r1r, za1, ya1, yb1, zb1)
    gather_last_on(enc_a, enc_b, enc_sems)

    loads[2].wait()
    loads[9].wait()

    def add_up(half):
        def block(n, square):
            cols = pl.ds(pl.multiple_of(n * 512, 512), 512)
            wide = pl.ds(pl.multiple_of(half * HALF + n * 512, 512), 512)
            total = total_of(half, cols, za1, ya1, yb1, zb1) + hid[:, wide].astype(F32)
            res[:, wide] = total
            return square + total * total

        return block

    square = jnp.zeros((SHARE, 512), F32)
    scatter_wait_b(r1s, r1r, zb1)
    square = lax.fori_loop(0, 4, add_up(1), square)
    scatter_wait_a(r1s, r1r, za1, ya1)
    square = lax.fori_loop(0, 4, add_up(0), square)
    scale = lax.rsqrt(jnp.sum(square, axis=-1, keepdims=True) / D + 1e-05)

    def normalise(half, held):
        def block(n, carry):
            cols = pl.ds(pl.multiple_of(n * 512, 512), 512)
            wide = pl.ds(pl.multiple_of(half * HALF + n * 512, 512), 512)
            held[d, :, cols] = (res[:, wide] * scale * gain[wide].astype(F32)).astype(BF16)
            return carry

        lax.fori_loop(0, 4, block, 0)

    def share_a(i, part):
        return nf_a.at[i, pl.ds((0, 0, 16)[part], (32, 16, 16)[part])]

    def share_b(i, part):
        return nf_b.at[i, pl.ds((0, 0, 16)[part], (32, 16, 16)[part])]

    ag_sems = (ags, agr)
    normalise(1, nf_b)
    flow_send(2, share_b, zh, ag_sems)
    normalise(0, nf_a)
    cross_send(share_a, d, 12, ag_sems)
    flow_send(0, share_a, zh, ag_sems)
    cross_send(share_b, d, 13, ag_sems)

    gather_finish_a(enc_a, enc_sems)
    gather_finish_b(enc_b, enc_sems)
    loads[3].wait()
    loads[4].wait()

    def cross_pair(e):
        shard = shard_ref[e % 2, e // 2]
        rank = jnp.int32(0)
        for earlier in range(e):
            rank = rank + (shard_ref[earlier % 2, earlier // 2] == shard).astype(jnp.int32)
        entry = arr.reshape(16, NLEN, 1024)[shard * 2 + jnp.minimum(rank, 1)]
        rows = slice((e % 2) * NLEN, (e % 2 + 1) * NLEN)
        kx[e // 2 + 1, rows, :] = dot_f32(entry, wck[...]).astype(BF16)
        vx[e // 2 + 1, rows, :] = dot_f32(entry, wcv[...]).astype(BF16)

    cross_pair(6)
    cross_pair(7)

    @pl.when(s < 15)
    def _():
        remote(kx.at[4], kx.at[0], ps.at[0], pr.at[0], s + 1, d).start()
        remote(vx.at[4], vx.at[0], ps.at[1], pr.at[1], s + 1, d).start()

    @pl.when(s == 0)
    def _():
        kx[0] = jnp.zeros((2 * NLEN, WIDTH), BF16)
        vx[0] = jnp.zeros((2 * NLEN, WIDTH), BF16)

    gather_a_over(share_a, ag_sems)
    gather_b_on(share_b, ag_sems)
    flow_forward(0, share_a, zh, ag_sems)
    for e in range(4):
        cross_pair(e)
    gather_last_on(share_a, share_b, ag_sems)
    for e in range(4, 6):
        cross_pair(e)
    for copy in spread:
        copy.wait_send()
    spread.clear()
    loads[5].wait()
    gather_finish_a(share_a, ag_sems)

    cqa[...] = jnp.zeros_like(cqa)

    def contract_a(n, carry):
        cols = pl.ds(pl.multiple_of(n * 512, 512), 512)
        cqa[...] += dot_f32(nf_a[:, :, cols].reshape(TOK, 512), wcq[cols, :])
        return carry

    def contract_b(n, carry):
        cols = pl.ds(pl.multiple_of(n * 512, 512), 512)
        right = pl.ds(pl.multiple_of(HALF + n * 512, 512), 512)
        cqa[...] += dot_f32(nf_b[:, :, cols].reshape(TOK, 512), wcq[right, :])
        return carry

    lax.fori_loop(0, 4, contract_a, 0)
    gather_finish_b(share_b, ag_sems)
    lax.fori_loop(0, 4, contract_b, 0)
    qx[...] = pltpu.roll(cqa[...].astype(BF16).astype(F32), 1, 0).astype(BF16)

    def attend(query, keys, values):
        scores = dot_nt(query, keys)
        top = jnp.max(scores, axis=-1, keepdims=True)
        weights = jnp.exp2((scores - top) * EXP2_SCALE)
        total = jnp.sum(weights, axis=-1, keepdims=True)
        return dot_f32(weights.astype(BF16), values) / total

    def group(g, carry):
        rows = pl.ds(pl.multiple_of(g * SPAN, SPAN), SPAN)
        for h in range(4):
            cols = slice(h * HD, (h + 1) * HD)
            cqa[rows, cols] = attend(qx[rows, cols], kx[g, :, cols], vx[g, :, cols])
        return carry

    lax.fori_loop(1, 4, group, 0, unroll=True)
    @pl.when(s > 0)
    def _():
        remote(kx.at[4], kx.at[0], ps.at[0], pr.at[0], s, d).wait_recv()
        remote(vx.at[4], vx.at[0], ps.at[1], pr.at[1], s, d).wait_recv()

    group(0, 0)
    for h in range(4):
        cols = slice(h * HD, (h + 1) * HD)
        tail = attend(qx[0:16, cols], kx[4, :, cols], vx[4, :, cols])
        first_row = lax.broadcasted_iota(jnp.int32, (16, HD), 0) == 0
        cqa[0:16, cols] = jnp.where(first_row, tail, cqa[0:16, cols])
    att[...] = pltpu.roll(cqa[...], TOK - 1, 0).astype(BF16)

    loads[6].wait()
    scatter(att[...], wco, r2s, r2r, za2, ya2, yb2, zb2)

    def finish(half):
        def block(n, carry):
            cols = pl.ds(pl.multiple_of(n * 512, 512), 512)
            wide = pl.ds(pl.multiple_of(half * HALF + n * 512, 512), 512)
            out_ref[:, wide] = res[:, wide] + total_of(half, cols, za2, ya2, yb2, zb2)
            return carry

        lax.fori_loop(0, 4, block, 0)

    scatter_wait_b(r2s, r2r, zb2)
    finish(1)
    scatter_wait_a(r2s, r2r, za2, ya2)
    finish(0)

    for copy in spread:
        copy.wait_send()
    for copy in sends:
        copy.wait_send()
    gather_a_sent(enc_a, enc_sems)
    gather_a_sent(share_a, ag_sems)
    for h in range(4):
        goal = at(j_to // 2, h, j_to % 2)

        @pl.when(goal != s)
        def _():
            remote(qst.at[h], qb.at[0], qs.at[h], qr.at[0], goal, d).wait_send()

    for i in range(4):

        @pl.when(block_of(i) != s)
        def _():
            remote(ob.at[i], ret.at[0], os_.at[i], or_.at[0], s, d).wait_send()

    @pl.when(s < 15)
    def _():
        remote(kx.at[4], kx.at[0], ps.at[0], pr.at[0], s, d).wait_send()
        remote(vx.at[4], vx.at[0], ps.at[1], pr.at[1], s, d).wait_send()


def per_device(
    hidden_in,
    query_rows,
    key_rows,
    value_rows,
    w_self_out,
    norm_gain,
    w_cross_q,
    w_cross_k,
    w_cross_v,
    w_cross_out,
    enc_table,
    nb_shard,
    nb_row,
):
    vmem = pl.BlockSpec(memory_space=pltpu.VMEM)
    hbm = pl.BlockSpec(memory_space=pl.ANY)
    scratch = [
        pltpu.VMEM((D,), BF16),
        pltpu.SMEM((2, 4), jnp.int32),
        pltpu.SMEM((2, 4), jnp.int32),
        pltpu.VMEM((WIDTH, D), BF16),
        pltpu.VMEM((D, WIDTH), BF16),
        pltpu.VMEM((1024, WIDTH), BF16),
        pltpu.VMEM((1024, WIDTH), BF16),
        pltpu.VMEM((WIDTH, D), BF16),
        pltpu.VMEM((8, NLEN, 1024), BF16),
        pltpu.VMEM((SHARE, D), BF16),
        pltpu.VMEM((4, 2, TOK, HD), BF16),
        pltpu.VMEM((4, TOK, HD), BF16),
        pltpu.VMEM((16, 2, TOK, HD), BF16),
        pltpu.VMEM((4, TOK, HD), BF16),
        pltpu.VMEM((4, TOK, HD), BF16),
        pltpu.VMEM((4, TOK, HD), BF16),
        pltpu.VMEM((8, TOK, 512), F32),
        pltpu.VMEM((TOK, HD), F32),
        pltpu.VMEM((TOK, HD), F32),
        pltpu.VMEM((TOK, WIDTH), BF16),
        pltpu.VMEM((8, 2 * NLEN, 1024), BF16),
        pltpu.VMEM((8, SHARE, HALF), BF16),
        pltpu.VMEM((8, SHARE, HALF), BF16),
    ]
    scratch += [
        pltpu.VMEM((4, SHARE, HALF), BF16),
        pltpu.VMEM((4, SHARE, HALF), BF16),
        pltpu.VMEM((6, SHARE, HALF), BF16),
        pltpu.VMEM((SHARE, HALF), BF16),
    ] * 2
    scratch += [
        pltpu.VMEM((4, SHARE, HALF), BF16),
        pltpu.VMEM((SHARE, HALF), BF16),
        pltpu.VMEM((2, SHARE, HALF), BF16),
        pltpu.VMEM((SHARE, D), F32),
        pltpu.VMEM((8, SHARE, HALF), BF16),
        pltpu.VMEM((8, SHARE, HALF), BF16),
        pltpu.VMEM((TOK, WIDTH), F32),
        pltpu.VMEM((TOK, WIDTH), BF16),
        pltpu.VMEM((5, 2 * NLEN, WIDTH), BF16),
        pltpu.VMEM((5, 2 * NLEN, WIDTH), BF16),
    ]
    counts = (12, 4, 4, 4, 4, 8, 8, 4, 4, 4, 4, 17, 17, 15, 15, 17, 17, 15, 15, 2, 2)
    scratch += [pltpu.SemaphoreType.DMA((count,)) for count in counts]
    scratch += [
        pltpu.VMEM((2, 2, 4), jnp.int32),
        pltpu.SMEM((2, 4), jnp.int32),
        pltpu.SMEM((2, 4), jnp.int32),
        pltpu.VMEM((192, 1024), BF16),
        pltpu.SemaphoreType.DMA((2,)),
        pltpu.SemaphoreType.DMA((2,)),
    ]
    return pl.pallas_call(
        block_kernel,
        out_shape=jax.ShapeDtypeStruct((SHARE, D), F32),
        in_specs=[vmem] * 3 + [hbm] * 10,
        out_specs=vmem,
        scratch_shapes=scratch,
        compiler_params=pltpu.CompilerParams(
            collective_id=0, has_side_effects=True, vmem_limit_bytes=56 << 20
        ),
        name="retro_block",
    )(
        query_rows,
        key_rows,
        value_rows,
        norm_gain,
        nb_shard.T,
        nb_row.T,
        hidden_in,
        w_self_out,
        w_cross_q,
        w_cross_k,
        w_cross_v,
        w_cross_out,
        enc_table,
    )


def solution(mesh):
    placed = (
        P("seq", None),
        P("seq", "db"),
        P("seq", "db"),
        P("seq", "db"),
        P("db", None),
        P(),
        P(None, "db"),
        P(None, "db"),
        P(None, "db"),
        P("db", None),
        P("db", None, None),
        P("seq", None),
        P("seq", None),
    )
    return jax.shard_map(
        per_device, mesh=mesh, in_specs=placed, out_specs=P(("seq", "db"), None), check_vma=False
    )
```

```python
import math

import jax
import jax.numpy as jnp
from jax import lax
from jax.experimental import pallas as pl
from jax.experimental.pallas import tpu as pltpu
from jax.sharding import PartitionSpec as P

HD = 128
SPAN = 64
NLEN = 128
TOK = 256
WIDTH = 512
D = 4096
SHARE = 32
HALF = 2048
NEG_BIG = -1e30
MESH = pl.DeviceIdType.MESH
EXP2_SCALE = math.log2(math.e) / math.sqrt(HD)
BF16 = jnp.bfloat16
F32 = jnp.float32


def remote(src, dst, send, recv, seq, db):
    return pltpu.make_async_remote_copy(
        src_ref=src, dst_ref=dst, send_sem=send, recv_sem=recv, device_id=(seq, db), device_id_type=MESH
    )


def dot_f32(a, b):
    return jnp.dot(a, b, preferred_element_type=F32)


def dot_nt(a, b):
    return lax.dot_general(a, b, (((1,), (1,)), ((), ())), preferred_element_type=F32)


def block_kernel(
    q_ref,
    k_ref,
    v_ref,
    gain_hbm,
    shard_hbm,
    row_hbm,
    hidden_hbm,
    wso_hbm,
    wcq_hbm,
    wck_hbm,
    wcv_hbm,
    wco_hbm,
    enc_hbm,
    out_ref,
    gain,
    shard_ref,
    row_ref,
    wso,
    wcq,
    wck,
    wcv,
    wco,
    enc,
    hid,
    kvs,
    qst,
    kv,
    qb,
    ob,
    ret,
    sc_buf,
    lsum,
    acc,
    att,
    arr,
    part_a,
    part_b,
    za1,
    ya1,
    yb1,
    zb1,
    za2,
    ya2,
    yb2,
    zb2,
    sum_a,
    sum_b,
    sum_y,
    res,
    nf_a,
    nf_b,
    cqa,
    qx,
    kx,
    vx,
    wsem,
    xs,
    xr,
    zs,
    zr,
    cs,
    cr,
    qs,
    qr,
    os_,
    or_,
    es,
    er,
    r1s,
    r1r,
    ags,
    agr,
    r2s,
    r2r,
    ps,
    pr,
    tab,
    shard_two,
    row_two,
    lent,
    ts,
    tr,
):
    s = lax.axis_index("seq")
    d = lax.axis_index("db")
    c = s % 2
    x = (s // 2) % 4
    zl = s // 8
    y = d // 2
    zh = d % 2
    over = 2 * y + 1 - zh
    beside = (s + 8) % 16
    far = (2, 1, 3)

    def at(zz, xx, cc):
        return (zz * 4 + xx) * 2 + cc

    own_rows = pl.ds(pl.multiple_of(d * SHARE, SHARE), SHARE)

    bar = pltpu.get_barrier_semaphore()
    for step in range(1, 16):
        pl.semaphore_signal(bar, inc=1, device_id=((s + step) % 16, d), device_id_type=MESH)
    for step in range(1, 8):
        pl.semaphore_signal(bar, inc=1, device_id=(s, (d + step) % 8), device_id_type=MESH)

    loads = [
        pltpu.make_async_copy(enc_hbm, enc, wsem.at[0]),
        pltpu.make_async_copy(wso_hbm, wso, wsem.at[1]),
        pltpu.make_async_copy(hidden_hbm.at[own_rows], hid, wsem.at[2]),
        pltpu.make_async_copy(wck_hbm, wck, wsem.at[3]),
        pltpu.make_async_copy(wcv_hbm, wcv, wsem.at[4]),
        pltpu.make_async_copy(wcq_hbm, wcq, wsem.at[5]),
        pltpu.make_async_copy(wco_hbm, wco, wsem.at[6]),
        pltpu.make_async_copy(shard_hbm, shard_ref, wsem.at[7]),
        pltpu.make_async_copy(row_hbm, row_ref, wsem.at[8]),
        pltpu.make_async_copy(gain_hbm, gain, wsem.at[9]),
    ]
    for k in (0, 7, 8):
        loads[k].start()
    for h in range(4):
        cols = slice(h * HD, (h + 1) * HD)
        kvs[h, 0] = k_ref[:, cols]
        kvs[h, 1] = v_ref[:, cols]
        qst[h] = q_ref[:, cols]
    pl.semaphore_signal(bar, inc=1, device_id=(beside, over), device_id_type=MESH)
    pl.semaphore_wait(bar, 23)

    sends = []

    def start(copy):
        copy.start()
        sends.append(copy)

    for dx in (1, 3, 2):
        other = (x + dx) % 4
        start(remote(kvs.at[other], kv.at[s], xs.at[dx], xr.at[dx], at(zl, other, c), d))
    kv[s] = kvs[x]
    def forward(src, k):
        start(remote(kv.at[src], kv.at[src], zs.at[k], zr.at[k], at(1 - zl, x, c), d))
        start(remote(kv.at[src], kv.at[src], cs.at[k], cr.at[k], at(zl, x, 1 - c), d))

    forward(s, 0)
    start(remote(shard_hbm, tab.at[0], ts.at[0], tr.at[0], beside, d))
    start(remote(row_hbm, tab.at[1], ts.at[1], tr.at[1], beside, d))

    low = s % 8
    high = low // 4
    j_to = (1 - high) * low + high * (7 - low)
    slot_to = (s // 8) * 2 + high
    for h in range(4):
        goal = at(j_to // 2, h, j_to % 2)

        @pl.when(goal != s)
        def _():
            remote(qst.at[h], qb.at[slot_to], qs.at[h], qr.at[slot_to], goal, d).start()

        @pl.when(goal == s)
        def _():
            pltpu.make_async_copy(qst.at[h], qb.at[slot_to], qr.at[slot_to]).start()

    def share_at(step, side):
        return 2 * ((y + step + 4) % 4) + side

    def flow_copies(flow, piece, side, sems):
        send, recv = sems
        held = piece(share_at(0, side), 0)
        return [
            remote(held, held, send.at[4 * flow + k], recv.at[4 * flow + k], s, share_at(step, zh))
            for k, step in ((0, 1), (1, -1))
        ]

    def flow_send(flow, piece, side, sems):
        for copy in flow_copies(flow, piece, side, sems):
            start(copy)

    def flow_forward(flow, piece, side, sems, then=None):
        send, recv = sems
        for k, step in ((0, 1), (1, -1)):
            came = share_at(-step, side)
            held = piece(came, 0)
            remote(held, held, send.at[4 * flow + k], recv.at[4 * flow + k], s, d).wait_recv()
            part = piece(came, 1 + k)
            k2 = 4 * flow + 2 + k
            start(remote(part, part, send.at[k2], recv.at[k2], s, share_at(step, zh)))
            if then is not None:
                then(came, k)

    def flow_last(flow, piece, side, sems):
        send, recv = sems
        for k in range(2):
            part = piece(share_at(2, side), 1 + k)
            k2 = 4 * flow + 2 + k
            remote(part, part, send.at[k2], recv.at[k2], s, d).wait_recv()

    def cross_send(piece, owner, k, sems):
        send, recv = sems
        held = piece(owner, 0)
        start(remote(held, held, send.at[k], recv.at[k], s, over))

    def cross_wait(piece, owner, k, sems):
        send, recv = sems
        held = piece(owner, 0)
        remote(held, held, send.at[k], recv.at[k], s, over).wait_recv()

    def gather_b_on(piece_b, sems):
        flow_forward(2, piece_b, zh, sems, lambda came, k: cross_send(piece_b, came, 14 + k, sems))

    def gather_a_over(piece_a, sems):
        cross_wait(piece_a, over, 12, sems)
        for copy in flow_copies(1, piece_a, 1 - zh, sems):
            copy.start()

    def gather_a_sent(piece_a, sems):
        for copy in flow_copies(1, piece_a, 1 - zh, sems):
            copy.wait_send()

    def gather_last_on(piece_a, piece_b, sems):
        flow_last(2, piece_b, zh, sems)
        cross_send(piece_b, share_at(2, zh), 16, sems)
        flow_forward(1, piece_a, 1 - zh, sems)

    def gather_finish_a(piece_a, sems):
        flow_last(0, piece_a, zh, sems)
        flow_last(1, piece_a, 1 - zh, sems)

    def gather_finish_b(piece_b, sems):
        for k, step in ((13, 0), (14, -1), (15, 1), (16, 2)):
            cross_wait(piece_b, share_at(step, 1 - zh), k, sems)

    for k in (0, 7, 8):
        loads[k].wait()

    def asked(shards, rows):
        first = jnp.int32(0)
        second = jnp.int32(0)
        found = jnp.int32(0)
        for e in range(8):
            match = shards[e % 2, e // 2] == d
            row = rows[e % 2, e // 2]
            first = jnp.where(match & (found == 0), row, first)
            second = jnp.where(match & (found == 1), row, second)
            found = found + match.astype(jnp.int32)
        return first, second

    first, second = asked(shard_ref, row_ref)
    arr[d, 0:NLEN] = enc[first]
    arr[d, NLEN : 2 * NLEN] = enc[second]

    def enc_a(i, part):
        return arr.at[i, pl.ds((0, 0, 96)[part], (192, 96, 96)[part])]

    def enc_b(i, part):
        return arr.at[i, pl.ds((192, 192, 224)[part], (64, 32, 32)[part])]

    enc_sems = (es, er)
    flow_send(2, enc_b, zh, enc_sems)
    flow_send(0, enc_a, zh, enc_sems)
    for k, table in ((0, shard_two), (1, row_two)):
        remote(tab.at[k], tab.at[k], ts.at[k], tr.at[k], beside, d).wait_recv()
        pltpu.make_async_copy(tab.at[k], table, wsem.at[10 + k]).start()
    for k, table in ((0, shard_two), (1, row_two)):
        pltpu.make_async_copy(tab.at[k], table, wsem.at[10 + k]).wait()
    first, second = asked(shard_two, row_two)
    lent[0:NLEN] = enc[first]
    lent[NLEN:192] = enc[second, 0:64]
    start(remote(lent, enc_a(d, 0), es.at[12], er.at[12], beside, over))

    for dx in (1, 3, 2):
        src = at(zl, (x - dx + 4) % 4, c)
        remote(kv.at[src], kv.at[src], xs.at[dx], xr.at[dx], src, d).wait_recv()
        forward(src, dx)
    cross_send(enc_b, d, 13, enc_sems)
    for dx in (0, 1, 3, 2):
        src = at(1 - zl, (x - dx + 4) % 4, c)
        remote(kv.at[src], kv.at[src], zs.at[dx], zr.at[dx], src, d).wait_recv()
        start(remote(kv.at[src], kv.at[src], cs.at[4 + dx], cr.at[4 + dx], at(zl, x, 1 - c), d))
    for zz in range(2):
        for dx in range(4):
            src = at((zl + zz) % 2, (x - dx + 4) % 4, 1 - c)
            k = 4 * zz + dx
            remote(kv.at[src], kv.at[src], cs.at[k], cr.at[k], src, d).wait_recv()

    gather_b_on(enc_b, enc_sems)
    flow_forward(0, enc_a, zh, enc_sems)
    gather_a_over(enc_a, enc_sems)

    for k in (1, 2, 3, 4, 5, 6, 9):
        loads[k].start()

    j = zl * 2 + c

    def block_of(i):
        return (i // 2) * 8 + (i % 2) * (7 - j) + (1 - i % 2) * j

    def slot(i, carry):
        b = block_of(i)


        remote(qst.at[0], qb.at[i], qs.at[0], qr.at[i], s, d).wait_recv()
        query = qb[i]
        last = (b + 2) // 2 - 1

        def lanes_max(scores):
            return jnp.maximum(
                jnp.maximum(scores[:, 0:128], scores[:, 128:256]),
                jnp.maximum(scores[:, 256:384], scores[:, 384:512]),
            )

        def first_pass(kb, top):
            keys = kv[pl.ds(2 * kb, 2), 0].reshape(512, HD)
            scores = dot_nt(query, keys)
            sc_buf[kb] = scores
            return jnp.maximum(top, lanes_max(scores))

        top = lax.fori_loop(0, last, first_pass, jnp.full((TOK, 128), NEG_BIG, F32))
        keys = kv[pl.ds(2 * last, 2), 0].reshape(512, HD)
        scores = dot_nt(query, keys)
        key_pos = last * 512 + lax.broadcasted_iota(jnp.int32, (TOK, 512), 1)
        query_pos = b * TOK + lax.broadcasted_iota(jnp.int32, (TOK, 512), 0)
        scores = jnp.where(key_pos <= query_pos, scores, NEG_BIG)
        sc_buf[last] = scores
        top = jnp.max(jnp.maximum(top, lanes_max(scores)), axis=-1, keepdims=True)
        lsum[...] = jnp.zeros_like(lsum)
        acc[...] = jnp.zeros_like(acc)

        def second_pass(kb, carry):
            weights = jnp.exp2((sc_buf[kb] - top) * EXP2_SCALE)
            values = kv[pl.ds(2 * kb, 2), 1].reshape(512, HD)
            lsum[...] += (weights[:, 0:128] + weights[:, 128:256]) + (
                weights[:, 256:384] + weights[:, 384:512]
            )
            acc[...] += dot_f32(weights.astype(BF16), values)
            return carry

        lax.fori_loop(0, last + 1, second_pass, 0)
        total = jnp.sum(lsum[...], axis=-1, keepdims=True)
        ob[i] = (acc[...] / total).astype(BF16)

        @pl.when(b != s)
        def _():
            remote(ob.at[i], ret.at[x], os_.at[i], or_.at[x], b, d).start()

        @pl.when(b == s)
        def _():
            pltpu.make_async_copy(ob.at[i], ret.at[x], or_.at[x]).start()

        return carry

    lax.fori_loop(0, 4, slot, 0)
    for h in range(4):
        remote(ob.at[0], ret.at[h], os_.at[0], or_.at[h], s, d).wait_recv()
        att[:, h * HD : (h + 1) * HD] = ret[h]

    def project_a(lhs, weight):
        def tile(n, carry):
            cols = pl.ds(pl.multiple_of(n * 512, 512), 512)
            product = dot_f32(lhs, weight[:, cols]).astype(BF16)
            for share in range(8):
                part_a[(share % 2) * 4 + share // 2, :, cols] = product[
                    share * SHARE : (share + 1) * SHARE
                ]
            return carry

        lax.fori_loop(0, 4, tile, 0, unroll=True)

    def project_b(lhs, weight):
        def tile(n, carry):
            cols = pl.ds(pl.multiple_of(n * 512, 512), 512)
            right = pl.ds(pl.multiple_of(HALF + n * 512, 512), 512)
            product = dot_f32(lhs, weight[:, right]).astype(BF16)
            part_b[:, :, cols] = product.reshape(8, SHARE, 512)
            return carry

        lax.fori_loop(0, 4, tile, 0, unroll=True)

    spread = []

    def go(copy):
        copy.start()
        spread.append(copy)

    def scatter(lhs, weight, send, recv, za, ya, yb, zb):
        project_b(lhs, weight)
        steps = ((0, 1), (1, -1))
        for k, step in steps:
            go(
                remote(
                    part_b.at[share_at(2, k)],
                    yb.at[k],
                    send.at[4 + k],
                    recv.at[4 + k],
                    s,
                    share_at(step, zh),
                )
            )
        for k, step in steps:
            go(
                remote(
                    part_b.at[share_at(step, 1 - k)],
                    yb.at[4 + k],
                    send.at[12 + k],
                    recv.at[12 + k],
                    s,
                    share_at(step, zh),
                )
            )
        project_a(lhs, weight)
        for dy in (2, 1, 3, 0):
            yy = (y + dy) % 4
            go(remote(part_a.at[(1 - zh) * 4 + yy], za.at[yy], send.at[dy], recv.at[dy], s, over))
        for k, step in steps:
            remote(yb.at[k], yb.at[k], send.at[4 + k], recv.at[4 + k], s, d).wait_recv()
            sum_y[k] = (part_b[share_at(step, k)].astype(F32) + yb[k].astype(F32)).astype(BF16)
            go(
                remote(
                    sum_y.at[k], yb.at[2 + k], send.at[6 + k], recv.at[6 + k], s, share_at(step, zh)
                )
            )
        for dy in far:
            yy = (y + dy) % 4
            remote(za.at[yy], za.at[yy], send.at[dy], recv.at[dy], s, over).wait_recv()
            sum_a[dy] = (part_a[zh * 4 + yy].astype(F32) + za[yy].astype(F32)).astype(BF16)
            go(
                remote(
                    sum_a.at[dy], ya.at[dy], send.at[8 + dy], recv.at[8 + dy], s, 2 * yy + zh
                )
            )
        for k in range(2):
            remote(yb.at[2 + k], yb.at[2 + k], send.at[6 + k], recv.at[6 + k], s, d).wait_recv()
            remote(yb.at[4 + k], yb.at[4 + k], send.at[12 + k], recv.at[12 + k], s, d).wait_recv()
        sum_b[...] = b_share(over, 1 - zh, slice(None), yb).astype(BF16)
        go(remote(sum_b, zb, send.at[14], recv.at[14], s, over))

    def b_share(share, k, cols, yb):
        return (
            part_b[share, :, cols].astype(F32)
            + yb[2 + k, :, cols].astype(F32)
            + yb[5 - k, :, cols].astype(F32)
        )

    def scatter_wait_a(send, recv, za, ya):
        remote(za.at[0], za.at[y], send.at[0], recv.at[0], s, over).wait_recv()
        for dy in far:
            remote(ya.at[dy], ya.at[dy], send.at[8 + dy], recv.at[8 + dy], s, d).wait_recv()

    def scatter_wait_b(send, recv, zb):
        remote(zb, zb, send.at[14], recv.at[14], s, over).wait_recv()

    def total_of(half, cols, za, ya, yb, zb):
        if half == 0:
            total = part_a[zh * 4 + y, :, cols].astype(F32) + za[y, :, cols].astype(F32)
            for dy in range(1, 4):
                total = total + ya[dy, :, cols].astype(F32)
        else:
            total = b_share(d, zh, cols, yb) + zb[:, cols].astype(F32)
        return total

    loads[1].wait()
    scatter(att[...], wso, r1s, r1r, za1, ya1, yb1, zb1)
    gather_last_on(enc_a, enc_b, enc_sems)

    loads[2].wait()
    loads[9].wait()

    def add_up(half):
        def block(n, square):
            cols = pl.ds(pl.multiple_of(n * 512, 512), 512)
            wide = pl.ds(pl.multiple_of(half * HALF + n * 512, 512), 512)
            total = total_of(half, cols, za1, ya1, yb1, zb1) + hid[:, wide].astype(F32)
            res[:, wide] = total
            return square + total * total

        return block

    square = jnp.zeros((SHARE, 512), F32)
    scatter_wait_b(r1s, r1r, zb1)
    square = lax.fori_loop(0, 4, add_up(1), square, unroll=True)
    scatter_wait_a(r1s, r1r, za1, ya1)
    square = lax.fori_loop(0, 4, add_up(0), square, unroll=True)
    scale = lax.rsqrt(jnp.sum(square, axis=-1, keepdims=True) / D + 1e-05)

    def normalise(half, held):
        def block(n, carry):
            cols = pl.ds(pl.multiple_of(n * 512, 512), 512)
            wide = pl.ds(pl.multiple_of(half * HALF + n * 512, 512), 512)
            held[d, :, cols] = (res[:, wide] * scale * gain[wide].astype(F32)).astype(BF16)
            return carry

        lax.fori_loop(0, 4, block, 0, unroll=True)

    def share_a(i, part):
        return nf_a.at[i, pl.ds((0, 0, 16)[part], (32, 16, 16)[part])]

    def share_b(i, part):
        return nf_b.at[i, pl.ds((0, 0, 16)[part], (32, 16, 16)[part])]

    ag_sems = (ags, agr)
    normalise(1, nf_b)
    flow_send(2, share_b, zh, ag_sems)
    normalise(0, nf_a)
    cross_send(share_a, d, 12, ag_sems)
    flow_send(0, share_a, zh, ag_sems)
    cross_send(share_b, d, 13, ag_sems)

    gather_finish_a(enc_a, enc_sems)
    gather_finish_b(enc_b, enc_sems)
    loads[3].wait()
    loads[4].wait()

    def cross_pair(e):
        shard = shard_ref[e % 2, e // 2]
        rank = jnp.int32(0)
        for earlier in range(e):
            rank = rank + (shard_ref[earlier % 2, earlier // 2] == shard).astype(jnp.int32)
        entry = arr.reshape(16, NLEN, 1024)[shard * 2 + jnp.minimum(rank, 1)]
        rows = slice((e % 2) * NLEN, (e % 2 + 1) * NLEN)
        kx[e // 2 + 1, rows, :] = dot_f32(entry, wck[...]).astype(BF16)
        vx[e // 2 + 1, rows, :] = dot_f32(entry, wcv[...]).astype(BF16)

    cross_pair(6)
    cross_pair(7)

    @pl.when(s < 15)
    def _():
        remote(kx.at[4], kx.at[0], ps.at[0], pr.at[0], s + 1, d).start()
        remote(vx.at[4], vx.at[0], ps.at[1], pr.at[1], s + 1, d).start()

    @pl.when(s == 0)
    def _():
        kx[0] = jnp.zeros((2 * NLEN, WIDTH), BF16)
        vx[0] = jnp.zeros((2 * NLEN, WIDTH), BF16)

    gather_a_over(share_a, ag_sems)
    gather_b_on(share_b, ag_sems)
    flow_forward(0, share_a, zh, ag_sems)
    for e in range(4):
        cross_pair(e)
    gather_last_on(share_a, share_b, ag_sems)
    for e in range(4, 6):
        cross_pair(e)
    for copy in spread:
        copy.wait_send()
    spread.clear()
    loads[5].wait()
    gather_finish_a(share_a, ag_sems)

    cqa[...] = jnp.zeros_like(cqa)

    def contract_a(n, carry):
        cols = pl.ds(pl.multiple_of(n * 512, 512), 512)
        cqa[...] += dot_f32(nf_a[:, :, cols].reshape(TOK, 512), wcq[cols, :])
        return carry

    def contract_b(n, carry):
        cols = pl.ds(pl.multiple_of(n * 512, 512), 512)
        right = pl.ds(pl.multiple_of(HALF + n * 512, 512), 512)
        cqa[...] += dot_f32(nf_b[:, :, cols].reshape(TOK, 512), wcq[right, :])
        return carry

    lax.fori_loop(0, 4, contract_a, 0, unroll=True)
    gather_finish_b(share_b, ag_sems)
    lax.fori_loop(0, 4, contract_b, 0, unroll=True)
    qx[...] = pltpu.roll(cqa[...].astype(BF16).astype(F32), 1, 0).astype(BF16)

    def attend(query, keys, values):
        scores = dot_nt(query, keys)
        top = jnp.max(scores, axis=-1, keepdims=True)
        weights = jnp.exp2((scores - top) * EXP2_SCALE)
        total = jnp.sum(weights, axis=-1, keepdims=True)
        return dot_f32(weights.astype(BF16), values) / total

    def group(g, carry):
        rows = pl.ds(pl.multiple_of(g * SPAN, SPAN), SPAN)
        for h in range(4):
            cols = slice(h * HD, (h + 1) * HD)
            cqa[rows, cols] = attend(qx[rows, cols], kx[g, :, cols], vx[g, :, cols])
        return carry

    lax.fori_loop(1, 4, group, 0, unroll=True)
    @pl.when(s > 0)
    def _():
        remote(kx.at[4], kx.at[0], ps.at[0], pr.at[0], s, d).wait_recv()
        remote(vx.at[4], vx.at[0], ps.at[1], pr.at[1], s, d).wait_recv()

    group(0, 0)
    for h in range(4):
        cols = slice(h * HD, (h + 1) * HD)
        tail = attend(qx[0:16, cols], kx[4, :, cols], vx[4, :, cols])
        first_row = lax.broadcasted_iota(jnp.int32, (16, HD), 0) == 0
        cqa[0:16, cols] = jnp.where(first_row, tail, cqa[0:16, cols])
    att[...] = pltpu.roll(cqa[...], TOK - 1, 0).astype(BF16)

    loads[6].wait()
    scatter(att[...], wco, r2s, r2r, za2, ya2, yb2, zb2)

    def finish(half):
        def block(n, carry):
            cols = pl.ds(pl.multiple_of(n * 512, 512), 512)
            wide = pl.ds(pl.multiple_of(half * HALF + n * 512, 512), 512)
            out_ref[:, wide] = res[:, wide] + total_of(half, cols, za2, ya2, yb2, zb2)
            return carry

        lax.fori_loop(0, 4, block, 0, unroll=True)

    scatter_wait_b(r2s, r2r, zb2)
    finish(1)
    scatter_wait_a(r2s, r2r, za2, ya2)
    finish(0)

    for copy in spread:
        copy.wait_send()
    for copy in sends:
        copy.wait_send()
    gather_a_sent(enc_a, enc_sems)
    gather_a_sent(share_a, ag_sems)
    for h in range(4):
        goal = at(j_to // 2, h, j_to % 2)

        @pl.when(goal != s)
        def _():
            remote(qst.at[h], qb.at[0], qs.at[h], qr.at[0], goal, d).wait_send()

    for i in range(4):

        @pl.when(block_of(i) != s)
        def _():
            remote(ob.at[i], ret.at[0], os_.at[i], or_.at[0], s, d).wait_send()

    @pl.when(s < 15)
    def _():
        remote(kx.at[4], kx.at[0], ps.at[0], pr.at[0], s, d).wait_send()
        remote(vx.at[4], vx.at[0], ps.at[1], pr.at[1], s, d).wait_send()


def per_device(
    hidden_in,
    query_rows,
    key_rows,
    value_rows,
    w_self_out,
    norm_gain,
    w_cross_q,
    w_cross_k,
    w_cross_v,
    w_cross_out,
    enc_table,
    nb_shard,
    nb_row,
):
    vmem = pl.BlockSpec(memory_space=pltpu.VMEM)
    hbm = pl.BlockSpec(memory_space=pl.ANY)
    scratch = [
        pltpu.VMEM((D,), BF16),
        pltpu.SMEM((2, 4), jnp.int32),
        pltpu.SMEM((2, 4), jnp.int32),
        pltpu.VMEM((WIDTH, D), BF16),
        pltpu.VMEM((D, WIDTH), BF16),
        pltpu.VMEM((1024, WIDTH), BF16),
        pltpu.VMEM((1024, WIDTH), BF16),
        pltpu.VMEM((WIDTH, D), BF16),
        pltpu.VMEM((8, NLEN, 1024), BF16),
        pltpu.VMEM((SHARE, D), BF16),
        pltpu.VMEM((4, 2, TOK, HD), BF16),
        pltpu.VMEM((4, TOK, HD), BF16),
        pltpu.VMEM((16, 2, TOK, HD), BF16),
        pltpu.VMEM((4, TOK, HD), BF16),
        pltpu.VMEM((4, TOK, HD), BF16),
        pltpu.VMEM((4, TOK, HD), BF16),
        pltpu.VMEM((8, TOK, 512), F32),
        pltpu.VMEM((TOK, HD), F32),
        pltpu.VMEM((TOK, HD), F32),
        pltpu.VMEM((TOK, WIDTH), BF16),
        pltpu.VMEM((8, 2 * NLEN, 1024), BF16),
        pltpu.VMEM((8, SHARE, HALF), BF16),
        pltpu.VMEM((8, SHARE, HALF), BF16),
    ]
    scratch += [
        pltpu.VMEM((4, SHARE, HALF), BF16),
        pltpu.VMEM((4, SHARE, HALF), BF16),
        pltpu.VMEM((6, SHARE, HALF), BF16),
        pltpu.VMEM((SHARE, HALF), BF16),
    ] * 2
    scratch += [
        pltpu.VMEM((4, SHARE, HALF), BF16),
        pltpu.VMEM((SHARE, HALF), BF16),
        pltpu.VMEM((2, SHARE, HALF), BF16),
        pltpu.VMEM((SHARE, D), F32),
        pltpu.VMEM((8, SHARE, HALF), BF16),
        pltpu.VMEM((8, SHARE, HALF), BF16),
        pltpu.VMEM((TOK, WIDTH), F32),
        pltpu.VMEM((TOK, WIDTH), BF16),
        pltpu.VMEM((5, 2 * NLEN, WIDTH), BF16),
        pltpu.VMEM((5, 2 * NLEN, WIDTH), BF16),
    ]
    counts = (12, 4, 4, 4, 4, 8, 8, 4, 4, 4, 4, 17, 17, 15, 15, 17, 17, 15, 15, 2, 2)
    scratch += [pltpu.SemaphoreType.DMA((count,)) for count in counts]
    scratch += [
        pltpu.VMEM((2, 2, 4), jnp.int32),
        pltpu.SMEM((2, 4), jnp.int32),
        pltpu.SMEM((2, 4), jnp.int32),
        pltpu.VMEM((192, 1024), BF16),
        pltpu.SemaphoreType.DMA((2,)),
        pltpu.SemaphoreType.DMA((2,)),
    ]
    return pl.pallas_call(
        block_kernel,
        out_shape=jax.ShapeDtypeStruct((SHARE, D), F32),
        in_specs=[vmem] * 3 + [hbm] * 10,
        out_specs=vmem,
        scratch_shapes=scratch,
        compiler_params=pltpu.CompilerParams(
            collective_id=0, has_side_effects=True, vmem_limit_bytes=56 << 20
        ),
        name="retro_block",
    )(
        query_rows,
        key_rows,
        value_rows,
        norm_gain,
        nb_shard.T,
        nb_row.T,
        hidden_in,
        w_self_out,
        w_cross_q,
        w_cross_k,
        w_cross_v,
        w_cross_out,
        enc_table,
    )


def solution(mesh):
    placed = (
        P("seq", None),
        P("seq", "db"),
        P("seq", "db"),
        P("seq", "db"),
        P("db", None),
        P(),
        P(None, "db"),
        P(None, "db"),
        P(None, "db"),
        P("db", None),
        P("db", None, None),
        P("seq", None),
        P("seq", None),
    )
    return jax.shard_map(
        per_device, mesh=mesh, in_specs=placed, out_specs=P(("seq", "db"), None), check_vma=False
    )
```

```python
import math

import jax
import jax.numpy as jnp
from jax import lax
from jax.experimental import pallas as pl
from jax.experimental.pallas import tpu as pltpu
from jax.sharding import PartitionSpec as P

HD = 128
SPAN = 64
NLEN = 128
TOK = 256
WIDTH = 512
D = 4096
SHARE = 32
HALF = 2048
NEG_BIG = -1e30
MESH = pl.DeviceIdType.MESH
EXP2_SCALE = math.log2(math.e) / math.sqrt(HD)
BF16 = jnp.bfloat16
F32 = jnp.float32


def remote(src, dst, send, recv, seq, db):
    return pltpu.make_async_remote_copy(
        src_ref=src, dst_ref=dst, send_sem=send, recv_sem=recv, device_id=(seq, db), device_id_type=MESH
    )


def dot_f32(a, b):
    return jnp.dot(a, b, preferred_element_type=F32)


def dot_nt(a, b):
    return lax.dot_general(a, b, (((1,), (1,)), ((), ())), preferred_element_type=F32)


def block_kernel(
    q_ref,
    k_ref,
    v_ref,
    gain_hbm,
    shard_hbm,
    row_hbm,
    hidden_hbm,
    wso_hbm,
    wcq_hbm,
    wck_hbm,
    wcv_hbm,
    wco_hbm,
    enc_hbm,
    out_ref,
    gain,
    shard_ref,
    row_ref,
    wso,
    wcq,
    wck,
    wcv,
    wco,
    enc,
    hid,
    kvs,
    qst,
    kv,
    qb,
    ob,
    ret,
    sc_buf,
    lsum,
    acc,
    att,
    arr,
    part_a,
    part_b,
    za1,
    ya1,
    yb1,
    zb1,
    za2,
    ya2,
    yb2,
    zb2,
    sum_a,
    sum_b,
    sum_y,
    res,
    nf_a,
    nf_b,
    cqa,
    qx,
    kx,
    vx,
    wsem,
    xs,
    xr,
    zs,
    zr,
    cs,
    cr,
    qs,
    qr,
    os_,
    or_,
    es,
    er,
    r1s,
    r1r,
    ags,
    agr,
    r2s,
    r2r,
    ps,
    pr,
    tab,
    shard_two,
    row_two,
    lent,
    ts,
    tr,
):
    s = lax.axis_index("seq")
    d = lax.axis_index("db")
    c = s % 2
    x = (s // 2) % 4
    zl = s // 8
    y = d // 2
    zh = d % 2
    over = 2 * y + 1 - zh
    beside = (s + 8) % 16
    far = (2, 1, 3)

    def at(zz, xx, cc):
        return (zz * 4 + xx) * 2 + cc

    own_rows = pl.ds(pl.multiple_of(d * SHARE, SHARE), SHARE)

    bar = pltpu.get_barrier_semaphore()
    for step in range(1, 16):
        pl.semaphore_signal(bar, inc=1, device_id=((s + step) % 16, d), device_id_type=MESH)
    for step in range(1, 8):
        pl.semaphore_signal(bar, inc=1, device_id=(s, (d + step) % 8), device_id_type=MESH)

    loads = [
        pltpu.make_async_copy(enc_hbm, enc, wsem.at[0]),
        pltpu.make_async_copy(wso_hbm, wso, wsem.at[1]),
        pltpu.make_async_copy(hidden_hbm.at[own_rows], hid, wsem.at[2]),
        pltpu.make_async_copy(wck_hbm, wck, wsem.at[3]),
        pltpu.make_async_copy(wcv_hbm, wcv, wsem.at[4]),
        pltpu.make_async_copy(wcq_hbm, wcq, wsem.at[5]),
        pltpu.make_async_copy(wco_hbm, wco, wsem.at[6]),
        pltpu.make_async_copy(shard_hbm, shard_ref, wsem.at[7]),
        pltpu.make_async_copy(row_hbm, row_ref, wsem.at[8]),
        pltpu.make_async_copy(gain_hbm, gain, wsem.at[9]),
    ]
    for k in (0, 7, 8):
        loads[k].start()
    for h in range(4):
        cols = slice(h * HD, (h + 1) * HD)
        kvs[h, 0] = k_ref[:, cols]
        kvs[h, 1] = v_ref[:, cols]
        qst[h] = q_ref[:, cols]
    pl.semaphore_signal(bar, inc=1, device_id=(beside, over), device_id_type=MESH)
    pl.semaphore_wait(bar, 23)

    sends = []

    def start(copy):
        copy.start()
        sends.append(copy)

    for dx in (1, 3, 2):
        other = (x + dx) % 4
        start(remote(kvs.at[other], kv.at[s], xs.at[dx], xr.at[dx], at(zl, other, c), d))
    kv[s] = kvs[x]
    def forward(src, k):
        start(remote(kv.at[src], kv.at[src], zs.at[k], zr.at[k], at(1 - zl, x, c), d))
        start(remote(kv.at[src], kv.at[src], cs.at[k], cr.at[k], at(zl, x, 1 - c), d))

    forward(s, 0)
    start(remote(shard_hbm, tab.at[0], ts.at[0], tr.at[0], beside, d))
    start(remote(row_hbm, tab.at[1], ts.at[1], tr.at[1], beside, d))

    low = s % 8
    high = low // 4
    j_to = (1 - high) * low + high * (7 - low)
    slot_to = (s // 8) * 2 + high
    for h in range(4):
        goal = at(j_to // 2, h, j_to % 2)

        @pl.when(goal != s)
        def _():
            remote(qst.at[h], qb.at[slot_to], qs.at[h], qr.at[slot_to], goal, d).start()

        @pl.when(goal == s)
        def _():
            pltpu.make_async_copy(qst.at[h], qb.at[slot_to], qr.at[slot_to]).start()

    def share_at(step, side):
        return 2 * ((y + step + 4) % 4) + side

    def flow_copies(flow, piece, side, sems):
        send, recv = sems
        held = piece(share_at(0, side), 0)
        return [
            remote(held, held, send.at[4 * flow + k], recv.at[4 * flow + k], s, share_at(step, zh))
            for k, step in ((0, 1), (1, -1))
        ]

    def flow_send(flow, piece, side, sems):
        for copy in flow_copies(flow, piece, side, sems):
            start(copy)

    def flow_forward(flow, piece, side, sems, then=None):
        send, recv = sems
        for k, step in ((0, 1), (1, -1)):
            came = share_at(-step, side)
            held = piece(came, 0)
            remote(held, held, send.at[4 * flow + k], recv.at[4 * flow + k], s, d).wait_recv()
            part = piece(came, 1 + k)
            k2 = 4 * flow + 2 + k
            start(remote(part, part, send.at[k2], recv.at[k2], s, share_at(step, zh)))
            if then is not None:
                then(came, k)

    def flow_last(flow, piece, side, sems):
        send, recv = sems
        for k in range(2):
            part = piece(share_at(2, side), 1 + k)
            k2 = 4 * flow + 2 + k
            remote(part, part, send.at[k2], recv.at[k2], s, d).wait_recv()

    def cross_send(piece, owner, k, sems):
        send, recv = sems
        held = piece(owner, 0)
        start(remote(held, held, send.at[k], recv.at[k], s, over))

    def cross_wait(piece, owner, k, sems):
        send, recv = sems
        held = piece(owner, 0)
        remote(held, held, send.at[k], recv.at[k], s, over).wait_recv()

    def gather_b_on(piece_b, sems):
        flow_forward(2, piece_b, zh, sems, lambda came, k: cross_send(piece_b, came, 14 + k, sems))

    def gather_a_over(piece_a, sems):
        cross_wait(piece_a, over, 12, sems)
        for copy in flow_copies(1, piece_a, 1 - zh, sems):
            copy.start()

    def gather_a_sent(piece_a, sems):
        for copy in flow_copies(1, piece_a, 1 - zh, sems):
            copy.wait_send()

    def gather_last_on(piece_a, piece_b, sems):
        flow_last(2, piece_b, zh, sems)
        cross_send(piece_b, share_at(2, zh), 16, sems)
        flow_forward(1, piece_a, 1 - zh, sems)

    def gather_finish_a(piece_a, sems):
        flow_last(0, piece_a, zh, sems)
        flow_last(1, piece_a, 1 - zh, sems)

    def gather_finish_b(piece_b, sems):
        for k, step in ((13, 0), (14, -1), (15, 1), (16, 2)):
            cross_wait(piece_b, share_at(step, 1 - zh), k, sems)

    for k in (0, 7, 8):
        loads[k].wait()

    def asked(shards, rows):
        first = jnp.int32(0)
        second = jnp.int32(0)
        found = jnp.int32(0)
        for e in range(8):
            match = shards[e % 2, e // 2] == d
            row = rows[e % 2, e // 2]
            first = jnp.where(match & (found == 0), row, first)
            second = jnp.where(match & (found == 1), row, second)
            found = found + match.astype(jnp.int32)
        return first, second

    first, second = asked(shard_ref, row_ref)
    arr[d, 0:NLEN] = enc[first]
    arr[d, NLEN : 2 * NLEN] = enc[second]

    def enc_a(i, part):
        return arr.at[i, pl.ds((0, 0, 96)[part], (192, 96, 96)[part])]

    def enc_b(i, part):
        return arr.at[i, pl.ds((192, 192, 224)[part], (64, 32, 32)[part])]

    enc_sems = (es, er)
    flow_send(2, enc_b, zh, enc_sems)
    flow_send(0, enc_a, zh, enc_sems)
    for k, table in ((0, shard_two), (1, row_two)):
        remote(tab.at[k], tab.at[k], ts.at[k], tr.at[k], beside, d).wait_recv()
        pltpu.make_async_copy(tab.at[k], table, wsem.at[10 + k]).start()
    for k, table in ((0, shard_two), (1, row_two)):
        pltpu.make_async_copy(tab.at[k], table, wsem.at[10 + k]).wait()
    first, second = asked(shard_two, row_two)
    lent[0:NLEN] = enc[first]
    lent[NLEN:192] = enc[second, 0:64]
    start(remote(lent, enc_a(d, 0), es.at[12], er.at[12], beside, over))

    for dx in (1, 3, 2):
        src = at(zl, (x - dx + 4) % 4, c)
        remote(kv.at[src], kv.at[src], xs.at[dx], xr.at[dx], src, d).wait_recv()
        forward(src, dx)
    cross_send(enc_b, d, 13, enc_sems)
    for dx in (0, 1, 3, 2):
        src = at(1 - zl, (x - dx + 4) % 4, c)
        remote(kv.at[src], kv.at[src], zs.at[dx], zr.at[dx], src, d).wait_recv()
        start(remote(kv.at[src], kv.at[src], cs.at[4 + dx], cr.at[4 + dx], at(zl, x, 1 - c), d))
    for zz in range(2):
        for dx in range(4):
            src = at((zl + zz) % 2, (x - dx + 4) % 4, 1 - c)
            k = 4 * zz + dx
            remote(kv.at[src], kv.at[src], cs.at[k], cr.at[k], src, d).wait_recv()

    gather_b_on(enc_b, enc_sems)
    flow_forward(0, enc_a, zh, enc_sems)
    gather_a_over(enc_a, enc_sems)

    for k in (1, 2, 3, 4, 5, 6, 9):
        loads[k].start()

    j = zl * 2 + c

    def block_of(i):
        return (i // 2) * 8 + (i % 2) * (7 - j) + (1 - i % 2) * j

    def slot(i, carry):
        b = block_of(i)


        remote(qst.at[0], qb.at[i], qs.at[0], qr.at[i], s, d).wait_recv()
        query = qb[i]
        last = (b + 2) // 2 - 1

        def lanes_max(scores):
            return jnp.maximum(
                jnp.maximum(scores[:, 0:128], scores[:, 128:256]),
                jnp.maximum(scores[:, 256:384], scores[:, 384:512]),
            )

        def first_pass(kb, top):
            keys = kv[pl.ds(2 * kb, 2), 0].reshape(512, HD)
            scores = dot_nt(query, keys)
            sc_buf[kb] = scores
            return jnp.maximum(top, lanes_max(scores))

        top = lax.fori_loop(0, last, first_pass, jnp.full((TOK, 128), NEG_BIG, F32))
        keys = kv[pl.ds(2 * last, 2), 0].reshape(512, HD)
        scores = dot_nt(query, keys)
        key_pos = last * 512 + lax.broadcasted_iota(jnp.int32, (TOK, 512), 1)
        query_pos = b * TOK + lax.broadcasted_iota(jnp.int32, (TOK, 512), 0)
        scores = jnp.where(key_pos <= query_pos, scores, NEG_BIG)
        sc_buf[last] = scores
        top = jnp.max(jnp.maximum(top, lanes_max(scores)), axis=-1, keepdims=True)
        lsum[...] = jnp.zeros_like(lsum)
        acc[...] = jnp.zeros_like(acc)

        def second_pass(kb, carry):
            weights = jnp.exp2((sc_buf[kb] - top) * EXP2_SCALE)
            values = kv[pl.ds(2 * kb, 2), 1].reshape(512, HD)
            lsum[...] += (weights[:, 0:128] + weights[:, 128:256]) + (
                weights[:, 256:384] + weights[:, 384:512]
            )
            acc[...] += dot_f32(weights.astype(BF16), values)
            return carry

        lax.fori_loop(0, last + 1, second_pass, 0)
        total = jnp.sum(lsum[...], axis=-1, keepdims=True)
        ob[i] = (acc[...] / total).astype(BF16)

        @pl.when(b != s)
        def _():
            remote(ob.at[i], ret.at[x], os_.at[i], or_.at[x], b, d).start()

        @pl.when(b == s)
        def _():
            pltpu.make_async_copy(ob.at[i], ret.at[x], or_.at[x]).start()

        return carry

    lax.fori_loop(0, 4, slot, 0)
    for h in range(4):
        remote(ob.at[0], ret.at[h], os_.at[0], or_.at[h], s, d).wait_recv()
        att[:, h * HD : (h + 1) * HD] = ret[h]

    def project_a(lhs, weight):
        def tile(n, carry):
            cols = pl.ds(pl.multiple_of(n * 512, 512), 512)
            product = dot_f32(lhs, weight[:, cols]).astype(BF16)
            for share in range(8):
                part_a[(share % 2) * 4 + share // 2, :, cols] = product[
                    share * SHARE : (share + 1) * SHARE
                ]
            return carry

        lax.fori_loop(0, 4, tile, 0, unroll=True)

    def project_b(lhs, weight):
        def tile(n, carry):
            cols = pl.ds(pl.multiple_of(n * 512, 512), 512)
            right = pl.ds(pl.multiple_of(HALF + n * 512, 512), 512)
            product = dot_f32(lhs, weight[:, right]).astype(BF16)
            part_b[:, :, cols] = product.reshape(8, SHARE, 512)
            return carry

        lax.fori_loop(0, 4, tile, 0, unroll=True)

    spread = []

    def go(copy):
        copy.start()
        spread.append(copy)

    def scatter(lhs, weight, send, recv, za, ya, yb, zb):
        project_b(lhs, weight)
        steps = ((0, 1), (1, -1))
        for k, step in steps:
            go(
                remote(
                    part_b.at[share_at(2, k)],
                    yb.at[k],
                    send.at[4 + k],
                    recv.at[4 + k],
                    s,
                    share_at(step, zh),
                )
            )
        for k, step in steps:
            go(
                remote(
                    part_b.at[share_at(step, 1 - k)],
                    yb.at[4 + k],
                    send.at[12 + k],
                    recv.at[12 + k],
                    s,
                    share_at(step, zh),
                )
            )
        project_a(lhs, weight)
        for dy in (2, 1, 3, 0):
            yy = (y + dy) % 4
            go(remote(part_a.at[(1 - zh) * 4 + yy], za.at[yy], send.at[dy], recv.at[dy], s, over))
        for k, step in steps:
            remote(yb.at[k], yb.at[k], send.at[4 + k], recv.at[4 + k], s, d).wait_recv()
            sum_y[k] = (part_b[share_at(step, k)].astype(F32) + yb[k].astype(F32)).astype(BF16)
            go(
                remote(
                    sum_y.at[k], yb.at[2 + k], send.at[6 + k], recv.at[6 + k], s, share_at(step, zh)
                )
            )
        for dy in far:
            yy = (y + dy) % 4
            remote(za.at[yy], za.at[yy], send.at[dy], recv.at[dy], s, over).wait_recv()
            sum_a[dy] = (part_a[zh * 4 + yy].astype(F32) + za[yy].astype(F32)).astype(BF16)
            go(
                remote(
                    sum_a.at[dy], ya.at[dy], send.at[8 + dy], recv.at[8 + dy], s, 2 * yy + zh
                )
            )
        for k in range(2):
            remote(yb.at[2 + k], yb.at[2 + k], send.at[6 + k], recv.at[6 + k], s, d).wait_recv()
            remote(yb.at[4 + k], yb.at[4 + k], send.at[12 + k], recv.at[12 + k], s, d).wait_recv()
        sum_b[...] = b_share(over, 1 - zh, slice(None), yb).astype(BF16)
        go(remote(sum_b, zb, send.at[14], recv.at[14], s, over))

    def b_share(share, k, cols, yb):
        return (
            part_b[share, :, cols].astype(F32)
            + yb[2 + k, :, cols].astype(F32)
            + yb[5 - k, :, cols].astype(F32)
        )

    def scatter_wait_a(send, recv, za, ya):
        remote(za.at[0], za.at[y], send.at[0], recv.at[0], s, over).wait_recv()
        for dy in far:
            remote(ya.at[dy], ya.at[dy], send.at[8 + dy], recv.at[8 + dy], s, d).wait_recv()

    def scatter_wait_b(send, recv, zb):
        remote(zb, zb, send.at[14], recv.at[14], s, over).wait_recv()

    def total_of(half, cols, za, ya, yb, zb):
        if half == 0:
            total = part_a[zh * 4 + y, :, cols].astype(F32) + za[y, :, cols].astype(F32)
            for dy in range(1, 4):
                total = total + ya[dy, :, cols].astype(F32)
        else:
            total = b_share(d, zh, cols, yb) + zb[:, cols].astype(F32)
        return total

    loads[1].wait()
    scatter(att[...], wso, r1s, r1r, za1, ya1, yb1, zb1)
    gather_last_on(enc_a, enc_b, enc_sems)

    loads[2].wait()
    loads[9].wait()

    def add_up(half):
        def block(n, square):
            cols = pl.ds(pl.multiple_of(n * 512, 512), 512)
            wide = pl.ds(pl.multiple_of(half * HALF + n * 512, 512), 512)
            total = total_of(half, cols, za1, ya1, yb1, zb1) + hid[:, wide].astype(F32)
            res[:, wide] = total
            return square + total * total

        return block

    square = jnp.zeros((SHARE, 512), F32)
    scatter_wait_b(r1s, r1r, zb1)
    square = lax.fori_loop(0, 4, add_up(1), square, unroll=True)
    scatter_wait_a(r1s, r1r, za1, ya1)
    square = lax.fori_loop(0, 4, add_up(0), square, unroll=True)
    scale = lax.rsqrt(jnp.sum(square, axis=-1, keepdims=True) / D + 1e-05)

    def normalise(half, held):
        def block(n, carry):
            cols = pl.ds(pl.multiple_of(n * 512, 512), 512)
            wide = pl.ds(pl.multiple_of(half * HALF + n * 512, 512), 512)
            held[d, :, cols] = (res[:, wide] * scale * gain[wide].astype(F32)).astype(BF16)
            return carry

        lax.fori_loop(0, 4, block, 0, unroll=True)

    def share_a(i, part):
        return nf_a.at[i, pl.ds((0, 0, 16)[part], (32, 16, 16)[part])]

    def share_b(i, part):
        return nf_b.at[i, pl.ds((0, 0, 16)[part], (32, 16, 16)[part])]

    ag_sems = (ags, agr)
    normalise(1, nf_b)
    flow_send(2, share_b, zh, ag_sems)
    normalise(0, nf_a)
    cross_send(share_a, d, 12, ag_sems)
    flow_send(0, share_a, zh, ag_sems)
    cross_send(share_b, d, 13, ag_sems)

    gather_finish_a(enc_a, enc_sems)
    gather_finish_b(enc_b, enc_sems)
    loads[3].wait()
    loads[4].wait()

    def entry_of(e):
        shard = shard_ref[e % 2, e // 2]
        rank = jnp.int32(0)
        for earlier in range(e):
            rank = rank + (shard_ref[earlier % 2, earlier // 2] == shard).astype(jnp.int32)
        return arr.reshape(16, NLEN, 1024)[shard * 2 + jnp.minimum(rank, 1)]

    def cross_span(u):
        entries = jnp.concatenate((entry_of(2 * u), entry_of(2 * u + 1)))
        kx[u + 1] = dot_f32(entries, wck[...]).astype(BF16)
        vx[u + 1] = dot_f32(entries, wcv[...]).astype(BF16)

    cross_span(3)

    @pl.when(s < 15)
    def _():
        remote(kx.at[4], kx.at[0], ps.at[0], pr.at[0], s + 1, d).start()
        remote(vx.at[4], vx.at[0], ps.at[1], pr.at[1], s + 1, d).start()

    @pl.when(s == 0)
    def _():
        kx[0] = jnp.zeros((2 * NLEN, WIDTH), BF16)
        vx[0] = jnp.zeros((2 * NLEN, WIDTH), BF16)

    gather_a_over(share_a, ag_sems)
    gather_b_on(share_b, ag_sems)
    flow_forward(0, share_a, zh, ag_sems)
    cross_span(0)
    cross_span(1)
    gather_last_on(share_a, share_b, ag_sems)
    cross_span(2)
    for copy in spread:
        copy.wait_send()
    spread.clear()
    loads[5].wait()
    gather_finish_a(share_a, ag_sems)

    cqa[...] = jnp.zeros_like(cqa)

    def contract_a(n, carry):
        cols = pl.ds(pl.multiple_of(n * 512, 512), 512)
        cqa[...] += dot_f32(nf_a[:, :, cols].reshape(TOK, 512), wcq[cols, :])
        return carry

    def contract_b(n, carry):
        cols = pl.ds(pl.multiple_of(n * 512, 512), 512)
        right = pl.ds(pl.multiple_of(HALF + n * 512, 512), 512)
        cqa[...] += dot_f32(nf_b[:, :, cols].reshape(TOK, 512), wcq[right, :])
        return carry

    lax.fori_loop(0, 4, contract_a, 0, unroll=True)
    gather_finish_b(share_b, ag_sems)
    lax.fori_loop(0, 4, contract_b, 0, unroll=True)
    qx[...] = pltpu.roll(cqa[...].astype(BF16).astype(F32), 1, 0).astype(BF16)

    def attend(query, keys, values):
        scores = dot_nt(query, keys)
        top = jnp.max(scores, axis=-1, keepdims=True)
        weights = jnp.exp2((scores - top) * EXP2_SCALE)
        total = jnp.sum(weights, axis=-1, keepdims=True)
        return dot_f32(weights.astype(BF16), values) / total

    def group(g, carry):
        rows = pl.ds(pl.multiple_of(g * SPAN, SPAN), SPAN)
        for h in range(4):
            cols = slice(h * HD, (h + 1) * HD)
            cqa[rows, cols] = attend(qx[rows, cols], kx[g, :, cols], vx[g, :, cols])
        return carry

    lax.fori_loop(1, 4, group, 0, unroll=True)
    @pl.when(s > 0)
    def _():
        remote(kx.at[4], kx.at[0], ps.at[0], pr.at[0], s, d).wait_recv()
        remote(vx.at[4], vx.at[0], ps.at[1], pr.at[1], s, d).wait_recv()

    group(0, 0)
    for h in range(4):
        cols = slice(h * HD, (h + 1) * HD)
        tail = attend(qx[0:16, cols], kx[4, :, cols], vx[4, :, cols])
        first_row = lax.broadcasted_iota(jnp.int32, (16, HD), 0) == 0
        cqa[0:16, cols] = jnp.where(first_row, tail, cqa[0:16, cols])
    att[...] = pltpu.roll(cqa[...], TOK - 1, 0).astype(BF16)

    loads[6].wait()
    scatter(att[...], wco, r2s, r2r, za2, ya2, yb2, zb2)

    def finish(half):
        def block(n, carry):
            cols = pl.ds(pl.multiple_of(n * 512, 512), 512)
            wide = pl.ds(pl.multiple_of(half * HALF + n * 512, 512), 512)
            out_ref[:, wide] = res[:, wide] + total_of(half, cols, za2, ya2, yb2, zb2)
            return carry

        lax.fori_loop(0, 4, block, 0, unroll=True)

    scatter_wait_b(r2s, r2r, zb2)
    finish(1)
    scatter_wait_a(r2s, r2r, za2, ya2)
    finish(0)

    for copy in spread:
        copy.wait_send()
    for copy in sends:
        copy.wait_send()
    gather_a_sent(enc_a, enc_sems)
    gather_a_sent(share_a, ag_sems)
    for h in range(4):
        goal = at(j_to // 2, h, j_to % 2)

        @pl.when(goal != s)
        def _():
            remote(qst.at[h], qb.at[0], qs.at[h], qr.at[0], goal, d).wait_send()

    for i in range(4):

        @pl.when(block_of(i) != s)
        def _():
            remote(ob.at[i], ret.at[0], os_.at[i], or_.at[0], s, d).wait_send()

    @pl.when(s < 15)
    def _():
        remote(kx.at[4], kx.at[0], ps.at[0], pr.at[0], s, d).wait_send()
        remote(vx.at[4], vx.at[0], ps.at[1], pr.at[1], s, d).wait_send()


def per_device(
    hidden_in,
    query_rows,
    key_rows,
    value_rows,
    w_self_out,
    norm_gain,
    w_cross_q,
    w_cross_k,
    w_cross_v,
    w_cross_out,
    enc_table,
    nb_shard,
    nb_row,
):
    vmem = pl.BlockSpec(memory_space=pltpu.VMEM)
    hbm = pl.BlockSpec(memory_space=pl.ANY)
    scratch = [
        pltpu.VMEM((D,), BF16),
        pltpu.SMEM((2, 4), jnp.int32),
        pltpu.SMEM((2, 4), jnp.int32),
        pltpu.VMEM((WIDTH, D), BF16),
        pltpu.VMEM((D, WIDTH), BF16),
        pltpu.VMEM((1024, WIDTH), BF16),
        pltpu.VMEM((1024, WIDTH), BF16),
        pltpu.VMEM((WIDTH, D), BF16),
        pltpu.VMEM((8, NLEN, 1024), BF16),
        pltpu.VMEM((SHARE, D), BF16),
        pltpu.VMEM((4, 2, TOK, HD), BF16),
        pltpu.VMEM((4, TOK, HD), BF16),
        pltpu.VMEM((16, 2, TOK, HD), BF16),
        pltpu.VMEM((4, TOK, HD), BF16),
        pltpu.VMEM((4, TOK, HD), BF16),
        pltpu.VMEM((4, TOK, HD), BF16),
        pltpu.VMEM((8, TOK, 512), F32),
        pltpu.VMEM((TOK, HD), F32),
        pltpu.VMEM((TOK, HD), F32),
        pltpu.VMEM((TOK, WIDTH), BF16),
        pltpu.VMEM((8, 2 * NLEN, 1024), BF16),
        pltpu.VMEM((8, SHARE, HALF), BF16),
        pltpu.VMEM((8, SHARE, HALF), BF16),
    ]
    scratch += [
        pltpu.VMEM((4, SHARE, HALF), BF16),
        pltpu.VMEM((4, SHARE, HALF), BF16),
        pltpu.VMEM((6, SHARE, HALF), BF16),
        pltpu.VMEM((SHARE, HALF), BF16),
    ] * 2
    scratch += [
        pltpu.VMEM((4, SHARE, HALF), BF16),
        pltpu.VMEM((SHARE, HALF), BF16),
        pltpu.VMEM((2, SHARE, HALF), BF16),
        pltpu.VMEM((SHARE, D), F32),
        pltpu.VMEM((8, SHARE, HALF), BF16),
        pltpu.VMEM((8, SHARE, HALF), BF16),
        pltpu.VMEM((TOK, WIDTH), F32),
        pltpu.VMEM((TOK, WIDTH), BF16),
        pltpu.VMEM((5, 2 * NLEN, WIDTH), BF16),
        pltpu.VMEM((5, 2 * NLEN, WIDTH), BF16),
    ]
    counts = (12, 4, 4, 4, 4, 8, 8, 4, 4, 4, 4, 17, 17, 15, 15, 17, 17, 15, 15, 2, 2)
    scratch += [pltpu.SemaphoreType.DMA((count,)) for count in counts]
    scratch += [
        pltpu.VMEM((2, 2, 4), jnp.int32),
        pltpu.SMEM((2, 4), jnp.int32),
        pltpu.SMEM((2, 4), jnp.int32),
        pltpu.VMEM((192, 1024), BF16),
        pltpu.SemaphoreType.DMA((2,)),
        pltpu.SemaphoreType.DMA((2,)),
    ]
    return pl.pallas_call(
        block_kernel,
        out_shape=jax.ShapeDtypeStruct((SHARE, D), F32),
        in_specs=[vmem] * 3 + [hbm] * 10,
        out_specs=vmem,
        scratch_shapes=scratch,
        compiler_params=pltpu.CompilerParams(
            collective_id=0, has_side_effects=True, vmem_limit_bytes=56 << 20
        ),
        name="retro_block",
    )(
        query_rows,
        key_rows,
        value_rows,
        norm_gain,
        nb_shard.T,
        nb_row.T,
        hidden_in,
        w_self_out,
        w_cross_q,
        w_cross_k,
        w_cross_v,
        w_cross_out,
        enc_table,
    )


def solution(mesh):
    placed = (
        P("seq", None),
        P("seq", "db"),
        P("seq", "db"),
        P("seq", "db"),
        P("db", None),
        P(),
        P(None, "db"),
        P(None, "db"),
        P(None, "db"),
        P("db", None),
        P("db", None, None),
        P("seq", None),
        P("seq", None),
    )
    return jax.shard_map(
        per_device, mesh=mesh, in_specs=placed, out_specs=P(("seq", "db"), None), check_vma=False
    )
```
